32 devices in a mesh: seq: 16 (over z, x, core), batch: 2 (over y).
Axes of the slice: x: 2, y: 2, z: 4, core: 2. Of those that a mesh axis runs over, the one named last changes fastest.
Arguments:
- tokens: bfloat16 [2, 4096, 768], P('batch', 'seq'), may hold values from -6 to 6
- cotangent: bfloat16 [2, 4096, 768], P('batch', 'seq'), may hold values from -6 to 6
- bank: bfloat16 [2, 8192, 768], P('batch', 'seq'), may hold values from -6 to 6
- prefix: int32 [2], P('batch'), may hold values from 409 to 2048
- blocks: int32 [2, 8], P('batch'), may hold values from 0 to 63
- self_qkv: bfloat16 [768, 2304], P(('seq', 'batch')), may hold values from -0.21875 to 0.21875
- self_out: bfloat16 [768, 768], P(('seq', 'batch')), may hold values from -3.5 to 3.5
- cross_q: bfloat16 [768, 768], P(('seq', 'batch')), may hold values from -0.21875 to 0.21875
- cross_kv: bfloat16 [768, 1536], P(('seq', 'batch')), may hold values from -0.21875 to 0.21875
- cross_out: bfloat16 [768, 768], P(('seq', 'batch')), may hold values from -1.75 to 1.75
- ffn_in: bfloat16 [768, 3072], P(('seq', 'batch')), may hold values from -0.21875 to 0.21875
- ffn_out: bfloat16 [3072, 768], P(('seq', 'batch')), may hold values from -0.109375 to 0.109375
- gains: bfloat16 [3, 768], P(None, ('seq', 'batch')), may hold values from 0.5 to 1.5
- biases: bfloat16 [14, 768], P(None, ('seq', 'batch')), may hold values from -1.75 to 1.75
Outputs:
- output: bfloat16 [2, 4096, 768], P('batch', 'seq')
- tokens_grad: float32 [2, 4096, 768], P('batch', 'seq')
- bank_grad: float32 [2, 8192, 768], P('batch', 'seq')
- self_qkv_grad: float32 [768, 2304], P(('seq', 'batch'))
- self_out_grad: float32 [768, 768], P(('seq', 'batch'))
- cross_q_grad: float32 [768, 768], P(('seq', 'batch'))
- cross_kv_grad: float32 [768, 1536], P(('seq', 'batch'))
- cross_out_grad: float32 [768, 768], P(('seq', 'batch'))
- ffn_in_grad: float32 [768, 3072], P(('seq', 'batch'))
- ffn_out_grad: float32 [3072, 768], P(('seq', 'batch'))
- gains_grad: float32 [3, 768], P(None, ('seq', 'batch'))
- biases_grad: float32 [14, 768], P(None, ('seq', 'batch'))
The draws below stay inside these ranges and needn't reach their ends.
All inputs are finite; a program needn't handle non-finite values.
Results may differ from the reference program's by a relative error of at most 0.025.
Values may be sent and summed in bfloat16 or wider, within the bound.
No kernel may reach another device: no remote copies, remote signals or barrier semaphores. Data moves between devices by JAX's collectives and lax.ppermute only.
A program may use at most 256 MiB of HBM per device.

```python
import jax
import jax.numpy as jnp
from jax import lax

D = 768
HEADS = 12
FF = 3072
HEAD_DIM = 64
BANK_BLOCK = 128
RETR_BLOCKS = 8
RETRIEVED = 1024
LENGTH = 4096
BANK = 8192
SEQS = 2


def plant(array, stream_key, least, high):
    longest = array.shape.index(max(array.shape))
    spots = []
    for shift in (0, 1):
        where = [jax.random.randint(jax.random.fold_in(stream_key, axis), (), 0, length) for axis, length in enumerate(array.shape)]
        where[longest] = (where[longest] + shift) % array.shape[longest]
        spots.append(tuple(where))
    return array.at[spots[0]].set(least).at[spots[1]].set(high)


def block_levels(rng, extent, cuts, low, largest):
    level, own = 1.0, jax.random.fold_in(rng, 6)
    for dim, shards_of in cuts:
        draws = jnp.exp(jax.random.uniform(jax.random.fold_in(own, dim), (shards_of,), jnp.float32, low / len(cuts), largest / len(cuts)))
        level = level * jnp.repeat(draws, extent[dim] // shards_of).reshape([-1 if axis == dim else 1 for axis in range(len(extent))])
    return level


def normal_values(own_key, dims, spread, most, cuts=(), kind=jnp.bfloat16):
    drawn = jax.random.normal(own_key, dims, jnp.float32) * spread
    if len(cuts) > 0:
        drawn = block_levels(own_key, dims, cuts, -0.22, 0.18) * drawn
    return jnp.clip(drawn, min=-most, max=most).astype(kind)


def setup_inputs(seed: int = 0) -> dict:
    arg_keys = jax.random.split(jax.random.key(seed), 15)
    return {
        "tokens": normal_values(arg_keys[0], (SEQS, LENGTH, D), 1.0, 6.0, ((0, 2), (1, 16))),
        "cotangent": normal_values(arg_keys[1], (SEQS, LENGTH, D), 1.0, 6.0, ((0, 2), (1, 16))),
        "bank": normal_values(arg_keys[2], (SEQS, BANK, D), 1.0, 6.0, ((0, 2), (1, 16))),
        "prefix": jax.random.randint(arg_keys[3], (SEQS,), LENGTH // 10, LENGTH // 2 + 1).astype(jnp.int32),
        "blocks": plant(jax.random.randint(arg_keys[4], (SEQS, RETR_BLOCKS), 0, BANK // BANK_BLOCK), jax.random.fold_in(arg_keys[4], 1), 0, (BANK // BANK_BLOCK) - 1).astype(jnp.int32),
        "self_qkv": normal_values(arg_keys[5], (D, 3 * D), D ** -0.5, 0.21875, ((0, 32),)),
        "self_out": normal_values(arg_keys[6], (D, D), (max(1, 16 * D // LENGTH)) ** -0.5, 3.5, ((0, 32),)),
        "cross_q": normal_values(arg_keys[7], (D, D), D ** -0.5, 0.21875, ((0, 32),)),
        "cross_kv": normal_values(arg_keys[8], (D, 2 * D), D ** -0.5, 0.21875, ((0, 32),)),
        "cross_out": normal_values(arg_keys[9], (D, D), (max(1, 16 * D // RETRIEVED)) ** -0.5, 1.75, ((0, 32),)),
        "ffn_in": normal_values(arg_keys[10], (D, FF), D ** -0.5, 0.21875, ((0, 32),)),
        "ffn_out": normal_values(arg_keys[11], (FF, D), FF ** -0.5, 0.109375, ((0, 32),)),
        "gains": jnp.clip(1.0 + 0.1 * jax.random.normal(arg_keys[12], (3, D), jnp.float32), 0.5, 1.5).astype(jnp.bfloat16),
        "biases": normal_values(arg_keys[13], (14, D), 0.3, 1.75, ((1, 32),)),
    }


EPSILON = 1e-05
NEGATIVE = -1e+30
PRECISE = lax.Precision.HIGHEST

@jax.custom_vjp
def low(v):
    return lax.optimization_barrier(v.astype(jnp.bfloat16)).astype(jnp.float32)

@jax.custom_vjp
def low_back(v):
    return v

def low_keep(v):
    return (low(v), None)

def low_pass(kept, grad):
    return (grad,)

def back_keep(v):
    return (v, None)

def back_low(kept, grad):
    return (low(grad),)
low.defvjp(low_keep, low_pass)
low_back.defvjp(back_keep, back_low)

def layer_norm(values, gain, shift):
    centered = values - lax.optimization_barrier(jnp.mean(values, axis=-1, keepdims=True))
    variance = lax.optimization_barrier(jnp.mean(centered * centered, axis=-1, keepdims=True))
    return centered * lax.rsqrt(variance + EPSILON) * gain + shift

def gelu_exact(values):
    return jax.nn.gelu(values, approximate=False)

def product(left, right):
    return jnp.dot(left, right, precision=PRECISE)

def attention_rows(query, keys, values, prefix_len, masked):
    length = query.shape[0]
    block = min(512, length)
    count = length // block
    key_pos = jnp.arange(keys.shape[0], dtype=jnp.int32)
    query_blocks = query.reshape(count, block, HEADS, HEAD_DIM)
    firsts = jnp.arange(count, dtype=jnp.int32) * block

    def one_block(pieces):
        query_block, first_row = pieces
        scores = jnp.einsum('qhd,khd->hqk', query_block, keys, precision=PRECISE) * HEAD_DIM ** (-0.5)
        if masked:
            query_pos = first_row + jnp.arange(block, dtype=jnp.int32)
            allowed = (key_pos[None, :] <= query_pos[:, None]) | (key_pos[None, :] < prefix_len)
            scores = jnp.where(allowed[None], scores, NEGATIVE)
        scores = low_back(scores)
        shifted = scores - lax.optimization_barrier(jnp.max(scores, axis=-1, keepdims=True))
        weights = jnp.exp(shifted)
        probs = low(weights / lax.optimization_barrier(jnp.sum(weights, axis=-1, keepdims=True)))
        return jnp.einsum('hqk,khd->qhd', probs, values, precision=PRECISE)
    result = lax.map(jax.checkpoint(one_block), (query_blocks, firsts))
    return result.reshape(length, HEADS * HEAD_DIM)

def layer_forward(tokens, bank, params, prefix_len, block_ids):
    self_qkv, self_out, cross_q, cross_kv, cross_out, ffn_in, ffn_out, gains, biases = params
    length = tokens.shape[0]
    width = tokens.shape[1]
    zero_row = jnp.zeros((width,), tokens.dtype)
    qkv = low(low_back(product(tokens, self_qkv) + jnp.concatenate([biases[3], zero_row, biases[4]])))
    heads = qkv.reshape(length, 3, HEADS, HEAD_DIM)
    attention = low(low_back(attention_rows(heads[:, 0], heads[:, 1], heads[:, 2], prefix_len, True)))
    branch = low_back(product(attention, self_out) + biases[5])
    hidden_one = layer_norm(tokens + branch, gains[0], biases[0])
    cross_query = low(low_back(product(low(hidden_one), cross_q) + biases[6]))
    rows = bank.reshape(-1, BANK_BLOCK, width)[block_ids].reshape(-1, width)
    cross_pair = low(low_back(product(rows, cross_kv) + jnp.concatenate([zero_row, biases[7]])))
    cross_heads = cross_pair.reshape(-1, 2, HEADS, HEAD_DIM)
    cross_att = low(low_back(attention_rows(cross_query.reshape(length, HEADS, HEAD_DIM), cross_heads[:, 0], cross_heads[:, 1], prefix_len, False)))
    cross_branch = low_back(product(cross_att, cross_out) + biases[8])
    hidden_two = layer_norm(hidden_one + cross_branch, gains[1], biases[1])
    inner = low_back(product(low(hidden_two), ffn_in) + biases[10:14].reshape(-1))
    outer = low_back(product(low(gelu_exact(inner)), ffn_out) + biases[9])
    return layer_norm(hidden_two + outer, gains[2], biases[2])

def reference(tokens, cotangent, bank, prefix, blocks, self_qkv, self_out, cross_q, cross_kv, cross_out, ffn_in, ffn_out, gains, biases):
    weights = tuple((matrix.astype(jnp.float32) for matrix in (self_qkv, self_out, cross_q, cross_kv, cross_out, ffn_in, ffn_out, gains, biases)))

    def one_sequence(totals, pieces):
        seq_tokens, seq_cot, seq_bank, prefix_len, block_ids = pieces

        def apply(layer_in, bank_in, params):
            return layer_forward(layer_in, bank_in, params, prefix_len, block_ids)
        result, pullback = jax.vjp(apply, seq_tokens.astype(jnp.float32), seq_bank.astype(jnp.float32), weights)
        grad_in, grad_bank, grad_params = pullback(seq_cot.astype(jnp.float32))
        totals = jax.tree.map(lambda left, right: left + right, totals, grad_params)
        return (totals, (result.astype(jnp.bfloat16), grad_in, grad_bank))
    start = jax.tree.map(jnp.zeros_like, weights)
    totals, stacked = lax.scan(one_sequence, start, (tokens, cotangent, bank, prefix, blocks))
    return (stacked[0], stacked[1], stacked[2], totals[0], totals[1], totals[2], totals[3], totals[4], totals[5], totals[6], totals[7], totals[8])
```

```python
import functools

import jax
import jax.numpy as jnp
from jax import lax
from jax.experimental import pallas as pl
from jax.experimental.pallas import tpu as pltpu
from jax.sharding import PartitionSpec as P

HEADS = 12
HEAD_DIM = 64
BANK_BLOCK = 128
GROUPS = 4
GROUP_HEADS = HEADS // GROUPS
GROUP_WIDTH = GROUP_HEADS * HEAD_DIM
PACK = 640
Q01, K01, V01, Q2, K2, V2, EXTRA = 0, 128, 256, 384, 448, 512, 576
EPSILON = 1e-05
NEGATIVE = -1e30
SCALE = HEAD_DIM ** (-0.5)
LANES_IN = (((1,), (1,)), ((), ()))
ROWS_IN = (((0,), (0,)), ((), ()))
VMEM_LIMIT = 60 * 1024 * 1024


def layer_norm(values, gain, shift):
    centered = values - jnp.mean(values, axis=-1, keepdims=True)
    variance = jnp.mean(centered * centered, axis=-1, keepdims=True)
    return centered * lax.rsqrt(variance + EPSILON) * gain + shift


def gelu_exact(values):
    return jax.nn.gelu(values, approximate=False)


def rounded(values):
    return values.astype(jnp.bfloat16)


def wide(values):
    return values.astype(jnp.float32)


def matmul(left, right):
    return jnp.dot(left, right, preferred_element_type=jnp.float32)


def weight_grad(left, right):
    return lax.dot_general(left, right, ROWS_IN, preferred_element_type=jnp.float32)


def back_matmul(left, right):
    return lax.dot_general(left, right, LANES_IN, preferred_element_type=jnp.float32)


def column_sums(values):
    return jnp.sum(wide(values), axis=0)


class Grid:
    def __init__(self, mesh):
        self.seq = mesh.shape["seq"]
        self.y = mesh.shape["batch"]
        self.z = GROUPS
        self.c = 2
        self.x = self.seq // (self.z * self.c)

    def coords(self, index):
        spot, y = divmod(index, self.y)
        spot, c = divmod(spot, self.c)
        z, x = divmod(spot, self.x)
        return z, x, c, y

    def index(self, z, x, c, y):
        return ((z * self.x + x) * self.c + c) * self.y + y

    def permute(self, array, target):
        pairs = []
        for index in range(self.seq * self.y):
            pairs.append((index, self.index(*target(*self.coords(index)))))
        return lax.ppermute(array, ("seq", "batch"), pairs)

    def send(self, array, axis, shift):
        size = getattr(self, axis)
        place = "zxcy".index(axis)

        def target(*spot):
            moved = list(spot)
            moved[place] = (moved[place] + shift) % size
            return tuple(moved)

        return self.permute(array, target)

    def fold(self, z, x, c, shift):
        if shift % 2 == 0:
            return z, x, c
        return z, self.x - 1 - x, self.c - 1 - c


def roll_pieces(pieces, me, axis=0):
    count = len(pieces)
    both = jnp.stack(list(pieces) + list(pieces[:-1]), axis=axis)
    return lax.dynamic_slice_in_dim(both, (count - me) % count, count, axis)


def take(array, index, axis):
    return lax.dynamic_index_in_dim(array, index, axis, keepdims=False)


def query_parts(block):
    lane = lax.broadcasted_iota(jnp.int32, (block.shape[0], 128), 1)
    first = wide(block[:, Q01 : Q01 + 128]) * SCALE
    third = pltpu.roll(wide(block[:, Q2 : Q2 + 128]) * SCALE, 64, 1)
    return (
        rounded(jnp.where(lane < 64, first, 0.0)),
        rounded(jnp.where(lane >= 64, first, 0.0)),
        rounded(jnp.where(lane >= 64, third, 0.0)),
    )


def key_tiles(ref, start, size):
    rows = pl.ds(start, size)
    pair_keys = ref[rows, K01 : K01 + 128]
    pair_values = ref[rows, V01 : V01 + 128]
    return (
        (pair_keys, pair_keys, ref[rows, Q2 : Q2 + 128]),
        (pair_values, pair_values, ref[rows, V2 : V2 + 128]),
    )


def allowed_keys(key_first, query_first, prefix_len, shape):
    key_pos = key_first + lax.broadcasted_iota(jnp.int32, shape, 0)
    query_pos = query_first + lax.broadcasted_iota(jnp.int32, shape, 1)
    return (key_pos <= query_pos) | (key_pos < prefix_len)


def each_block(table, refs, rows, query_first, prefix_len, work):
    half = refs[0].shape[0] // rows
    for part, ref in enumerate(refs):

        def step(local, carry, part=part, ref=ref):
            block = part * half + local
            key_first = table[block]
            last = key_first + rows - 1
            seen = (key_first <= query_first + rows - 1) | (key_first < prefix_len)
            whole = (last <= query_first) | (last < prefix_len)

            @pl.when(seen & whole)
            def _():
                work(ref, local * rows, block, key_first, False)

            @pl.when(seen & jnp.logical_not(whole))
            def _():
                work(ref, local * rows, block, key_first, True)

            return carry

        lax.fori_loop(0, half, step, 0)


def forward_kernel(rows, blocks, table, own, other, out, lse, query, accum, stats):
    m = pl.program_id(0)
    half = blocks // 2
    block = table[blocks + m]
    query_first = table[blocks + GROUPS + m]
    prefix_len = table[blocks + 2 * GROUPS]

    def load(ref, local):
        for head, part in enumerate(query_parts(ref[pl.ds(local * rows, rows), :])):
            query[head] = part

    @pl.when(block < half)
    def _():
        load(own, block)

    @pl.when(block >= half)
    def _():
        load(other, block - half)

    accum[...] = jnp.zeros_like(accum)
    stats[0:8, :] = jnp.full((8, rows), NEGATIVE, jnp.float32)
    stats[8:16, :] = jnp.zeros((8, rows), jnp.float32)

    def work(ref, start, block, key_first, masked):
        keys, values = key_tiles(ref, start, rows)
        if masked:
            mask = allowed_keys(key_first, query_first, prefix_len, (rows, rows))
        for head in range(GROUP_HEADS):
            scores = lax.dot_general(
                keys[head], query[head], LANES_IN, preferred_element_type=jnp.float32
            )
            if masked:
                scores = jnp.where(mask, scores, NEGATIVE)
            old = stats[head : head + 1, :]
            top = jnp.maximum(old, jnp.max(scores, axis=0, keepdims=True))
            weights = jnp.exp(scores - top)
            shrink = jnp.exp(old - top)
            stats[head : head + 1, :] = top
            stats[8 + head : 9 + head, :] = stats[8 + head : 9 + head, :] * shrink + jnp.sum(
                weights, axis=0, keepdims=True
            )
            accum[head] = accum[head] * shrink + lax.dot_general(
                values[head], rounded(weights), ROWS_IN, preferred_element_type=jnp.float32
            )

    each_block(table, (own, other), rows, query_first, prefix_len, work)
    totals = stats[8 : 8 + GROUP_HEADS, :]
    final = [accum[head] / totals[head : head + 1, :] for head in range(GROUP_HEADS)]
    line = lax.broadcasted_iota(jnp.int32, (128, rows), 0)
    out[0, :, 0:128] = jnp.where(line < 64, final[0], final[1]).T
    out[0, :, 128:256] = jnp.where(line < 64, final[2], 0.0).T
    lse[0] = jnp.zeros((8, rows), jnp.float32)
    lse[0, 0:GROUP_HEADS, :] = stats[0:GROUP_HEADS, :] + jnp.log(totals)


def backward_kernel(
    rows, blocks, table, own, other, dout, out, lse, own_grad, other_grad, query, accum, qgrad
):
    m = pl.program_id(0)
    half = blocks // 2
    block = table[blocks + m]
    query_first = table[blocks + GROUPS + m]
    prefix_len = table[blocks + 2 * GROUPS]

    @pl.when(m == 0)
    def _():
        def clear(index, carry):
            accum[pl.ds(index * rows, rows), :] = jnp.zeros((rows, PACK), jnp.float32)
            return carry

        lax.fori_loop(0, blocks, clear, 0)

    def load(ref, local):
        for head, part in enumerate(query_parts(ref[pl.ds(local * rows, rows), :])):
            query[head] = part

    @pl.when(block < half)
    def _():
        load(own, block)

    @pl.when(block >= half)
    def _():
        load(other, block - half)

    lane = lax.broadcasted_iota(jnp.int32, (rows, 128), 1)
    pair = wide(dout[0, :, 0:128])
    third = wide(dout[0, :, 128:256])
    query[3] = rounded(jnp.where(lane < 64, pair, 0.0))
    query[4] = rounded(jnp.where(lane >= 64, pair, 0.0))
    query[5] = rounded(jnp.where(lane < 64, third, 0.0))
    pair_prod = (pair * out[0, :, 0:128]).T
    third_prod = (third * out[0, :, 128:256]).T
    deltas = (
        jnp.sum(pair_prod[0:64], axis=0, keepdims=True),
        jnp.sum(pair_prod[64:128], axis=0, keepdims=True),
        jnp.sum(third_prod[0:64], axis=0, keepdims=True),
    )
    for head in range(GROUP_HEADS):
        qgrad[GROUP_HEADS, head : head + 1, :] = deltas[head]
        qgrad[head] = jnp.zeros((128, rows), jnp.float32)

    def work(ref, start, block, key_first, masked):
        keys, values = key_tiles(ref, start, rows)
        if masked:
            mask = allowed_keys(key_first, query_first, prefix_len, (rows, rows))
        key_parts, value_parts = [], []
        for head in range(GROUP_HEADS):
            scores = lax.dot_general(
                keys[head], query[head], LANES_IN, preferred_element_type=jnp.float32
            )
            if masked:
                scores = jnp.where(mask, scores, NEGATIVE)
            probs = jnp.exp(scores - lse[0, head : head + 1, :])
            grads = lax.dot_general(
                values[head], query[3 + head], LANES_IN, preferred_element_type=jnp.float32
            )
            low = rounded(probs * (grads - qgrad[GROUP_HEADS, head : head + 1, :]))
            value_parts.append(matmul(rounded(probs), query[3 + head]))
            key_parts.append(matmul(low, query[head]))
            qgrad[head] += lax.dot_general(
                keys[head], low, ROWS_IN, preferred_element_type=jnp.float32
            )
        span = pl.ds(pl.multiple_of(block * rows, rows), rows)
        accum[span, K01 : K01 + 128] += key_parts[0] + key_parts[1]
        accum[span, V01 : V01 + 128] += value_parts[0] + value_parts[1]
        accum[span, Q2 : Q2 + 128] += key_parts[2]
        accum[span, V2 : V2 + 128] += value_parts[2]

    each_block(table, (own, other), rows, query_first, prefix_len, work)
    line = lax.broadcasted_iota(jnp.int32, (128, rows), 0)
    span = pl.ds(pl.multiple_of(block * rows, rows), rows)
    accum[span, Q01 : Q01 + 128] = jnp.where(line < 64, qgrad[0], qgrad[1]).T * SCALE
    moved = pltpu.roll(jnp.where(line >= 64, qgrad[2], 0.0).T * SCALE, 64, 1)
    accum[span, Q2 : Q2 + 128] += moved

    @pl.when(m == GROUPS - 1)
    def _():
        def write(index, carry):
            source = pl.ds(index * rows, rows)
            own_grad[source, :] = rounded(accum[source, :])
            other_grad[source, :] = rounded(accum[pl.ds((half + index) * rows, rows), :])
            return carry

        lax.fori_loop(0, half, write, 0)


def whole(shape):
    return pl.BlockSpec(shape, lambda *_: (0,) * len(shape), pipeline_mode=pl.Buffered(1))


def slab(shape):
    return pl.BlockSpec((1,) + shape, lambda m, *_: (m, 0, 0))


def self_forward(table, own, other, rows):
    half, _ = own.shape
    blocks = 2 * half // rows
    pairs = GROUPS * blocks * GROUP_HEADS // 2
    return pl.pallas_call(
        functools.partial(forward_kernel, rows, blocks),
        grid_spec=pltpu.PrefetchScalarGridSpec(
            num_scalar_prefetch=1,
            grid=(GROUPS,),
            in_specs=[whole((half, PACK)), whole((half, PACK))],
            out_specs=[slab((rows, 256)), slab((8, rows))],
            scratch_shapes=[
                pltpu.VMEM((GROUP_HEADS, rows, 128), jnp.bfloat16),
                pltpu.VMEM((GROUP_HEADS, 128, rows), jnp.float32),
                pltpu.VMEM((16, rows), jnp.float32),
            ],
        ),
        out_shape=[
            jax.ShapeDtypeStruct((GROUPS, rows, 256), jnp.float32),
            jax.ShapeDtypeStruct((GROUPS, 8, rows), jnp.float32),
        ],
        compiler_params=pltpu.CompilerParams(vmem_limit_bytes=VMEM_LIMIT),
        cost_estimate=pl.CostEstimate(
            flops=pairs * rows * rows * 128 * 4,
            bytes_accessed=4 * half * PACK,
            transcendentals=pairs * rows * rows,
        ),
        name="self_forward",
    )(table, own, other)


def self_backward(table, own, other, dout, out, lse, rows):
    half, _ = own.shape
    blocks = 2 * half // rows
    pairs = GROUPS * blocks * GROUP_HEADS // 2
    return pl.pallas_call(
        functools.partial(backward_kernel, rows, blocks),
        grid_spec=pltpu.PrefetchScalarGridSpec(
            num_scalar_prefetch=1,
            grid=(GROUPS,),
            in_specs=[
                whole((half, PACK)),
                whole((half, PACK)),
                slab((rows, 256)),
                slab((rows, 256)),
                slab((8, rows)),
            ],
            out_specs=[whole((half, PACK)), whole((half, PACK))],
            scratch_shapes=[
                pltpu.VMEM((2 * GROUP_HEADS, rows, 128), jnp.bfloat16),
                pltpu.VMEM((2 * half, PACK), jnp.float32),
                pltpu.VMEM((GROUP_HEADS + 1, 128, rows), jnp.float32),
            ],
        ),
        out_shape=[jax.ShapeDtypeStruct((half, PACK), jnp.bfloat16)] * 2,
        compiler_params=pltpu.CompilerParams(vmem_limit_bytes=VMEM_LIMIT),
        cost_estimate=pl.CostEstimate(
            flops=pairs * rows * rows * 128 * 10,
            bytes_accessed=8 * half * PACK,
            transcendentals=pairs * rows * rows,
        ),
        name="self_backward",
    )(table, own, other, dout, out, lse)


def pair_heads(block, scale=1.0):
    lane = lax.broadcasted_iota(jnp.int32, block.shape, 1)
    values = wide(block) * scale
    return rounded(jnp.where(lane < 64, values, 0.0)), rounded(jnp.where(lane >= 64, values, 0.0))


def cross_forward_kernel(query, keys, values, out, lse):
    rows = query.shape[0]
    parts = pair_heads(query[...], SCALE)
    sides = []
    lse[0] = jnp.zeros((8, rows), jnp.float32)
    for head in range(2):
        scores = lax.dot_general(
            keys[...], parts[head], LANES_IN, preferred_element_type=jnp.float32
        )
        top = jnp.max(scores, axis=0, keepdims=True)
        weights = jnp.exp(scores - top)
        total = jnp.sum(weights, axis=0, keepdims=True)
        mixed = lax.dot_general(
            values[...], rounded(weights), ROWS_IN, preferred_element_type=jnp.float32
        )
        sides.append(mixed / total)
        lse[0, head : head + 1, :] = top + jnp.log(total)
    line = lax.broadcasted_iota(jnp.int32, (128, rows), 0)
    out[...] = rounded(jnp.where(line < 64, sides[0], sides[1]).T)


def cross_backward_kernel(query, keys, values, dout, lse, qgrad, kgrad, vgrad):
    rows = query.shape[0]
    parts = pair_heads(query[...], SCALE)
    grads = pair_heads(dout[...])
    sides, key_parts, value_parts = [], [], []
    for head in range(2):
        scores = lax.dot_general(
            keys[...], parts[head], LANES_IN, preferred_element_type=jnp.float32
        )
        probs = jnp.exp(scores - lse[0, head : head + 1, :])
        slopes = lax.dot_general(
            values[...], grads[head], LANES_IN, preferred_element_type=jnp.float32
        )
        delta = jnp.sum(probs * slopes, axis=0, keepdims=True)
        low = rounded(probs * (slopes - delta))
        value_parts.append(matmul(rounded(probs), grads[head]))
        key_parts.append(matmul(low, parts[head]))
        sides.append(lax.dot_general(keys[...], low, ROWS_IN, preferred_element_type=jnp.float32))
    line = lax.broadcasted_iota(jnp.int32, (128, rows), 0)
    qgrad[...] = rounded(jnp.where(line < 64, sides[0], sides[1]).T * SCALE)
    kgrad[...] = rounded(key_parts[0] + key_parts[1])
    vgrad[...] = rounded(value_parts[0] + value_parts[1])


def cross_forward(query, pair):
    rows, width = query.shape
    count = width // 128
    kept = pair.shape[0]
    return pl.pallas_call(
        cross_forward_kernel,
        grid=(count,),
        in_specs=[
            pl.BlockSpec((rows, 128), lambda i: (0, i)),
            pl.BlockSpec((kept, 128), lambda i: (0, i)),
            pl.BlockSpec((kept, 128), lambda i: (0, count + i)),
        ],
        out_specs=[
            pl.BlockSpec((rows, 128), lambda i: (0, i)),
            pl.BlockSpec((1, 8, rows), lambda i: (i, 0, 0)),
        ],
        out_shape=[
            jax.ShapeDtypeStruct((rows, width), jnp.bfloat16),
            jax.ShapeDtypeStruct((count, 8, rows), jnp.float32),
        ],
        compiler_params=pltpu.CompilerParams(vmem_limit_bytes=VMEM_LIMIT),
        cost_estimate=pl.CostEstimate(
            flops=8 * rows * kept * width, bytes_accessed=4 * kept * width, transcendentals=12 * rows * kept
        ),
        name="cross_forward",
    )(query, pair, pair)


def cross_backward(query, pair, dout, lse):
    rows, width = query.shape
    count = width // 128
    kept = pair.shape[0]
    return pl.pallas_call(
        cross_backward_kernel,
        grid=(count,),
        in_specs=[
            pl.BlockSpec((rows, 128), lambda i: (0, i)),
            pl.BlockSpec((kept, 128), lambda i: (0, i)),
            pl.BlockSpec((kept, 128), lambda i: (0, count + i)),
            pl.BlockSpec((rows, 128), lambda i: (0, i)),
            pl.BlockSpec((1, 8, rows), lambda i: (i, 0, 0)),
        ],
        out_specs=[
            pl.BlockSpec((rows, 128), lambda i: (0, i)),
            pl.BlockSpec((kept, 128), lambda i: (0, i)),
            pl.BlockSpec((kept, 128), lambda i: (0, i)),
        ],
        out_shape=[
            jax.ShapeDtypeStruct((rows, width), jnp.bfloat16),
            jax.ShapeDtypeStruct((kept, width), jnp.bfloat16),
            jax.ShapeDtypeStruct((kept, width), jnp.bfloat16),
        ],
        compiler_params=pltpu.CompilerParams(vmem_limit_bytes=VMEM_LIMIT),
        cost_estimate=pl.CostEstimate(
            flops=20 * rows * kept * width, bytes_accessed=8 * kept * width, transcendentals=12 * rows * kept
        ),
        name="cross_backward",
    )(query, pair, pair, dout, lse)


def pick_kernel(table, bank, out):
    i = pl.program_id(0)
    keep = table[pl.num_programs(0) + i]
    out[0] = jnp.where(keep > 0, bank[0], jnp.zeros_like(bank[0]))


def pick_rows(chunks, spots, found):
    count = spots.shape[0]
    size = chunks.shape[1:]
    table = jnp.concatenate([spots, found.astype(jnp.int32)])
    return pl.pallas_call(
        pick_kernel,
        grid_spec=pltpu.PrefetchScalarGridSpec(
            num_scalar_prefetch=1,
            grid=(count,),
            in_specs=[pl.BlockSpec((1,) + size, lambda i, t: (t[i], 0, 0))],
            out_specs=pl.BlockSpec((1,) + size, lambda i, t: (i, 0, 0)),
        ),
        out_shape=jax.ShapeDtypeStruct((count,) + size, chunks.dtype),
        name="pick_rows",
    )(table, chunks)


def place_kernel(count, table, grads, out):
    spot = pl.program_id(0)
    out[...] = jnp.zeros_like(out)
    for i in range(count):

        @pl.when(table[i] == spot)
        def _(i=i):
            out[0] += wide(grads[i])


def place_rows(grads, spots, chunks):
    count = spots.shape[0]
    size = grads.shape[1:]
    return pl.pallas_call(
        functools.partial(place_kernel, count),
        grid_spec=pltpu.PrefetchScalarGridSpec(
            num_scalar_prefetch=1,
            grid=(chunks,),
            in_specs=[whole((count,) + size)],
            out_specs=pl.BlockSpec((1,) + size, lambda n, t: (n, 0, 0)),
        ),
        out_shape=jax.ShapeDtypeStruct((chunks,) + size, jnp.float32),
        name="place_rows",
    )(spots, grads)


def scatter_step(grid, array, axis, me, place):
    size = getattr(grid, axis)
    total = wide(take(array, me, place))
    for shift in range(1, size):
        piece = take(array, (me + shift) % size, place)
        total = total + wide(grid.send(piece, axis, shift))
    return rounded(total)


def body(
    grid,
    tokens,
    cotangent,
    bank,
    prefix,
    blocks,
    self_qkv,
    self_out,
    cross_q,
    cross_kv,
    cross_out,
    ffn_in,
    ffn_out,
    gains,
    biases,
):
    Z, X, C, Y = grid.z, grid.x, grid.c, grid.y
    devices = grid.seq * Y
    seq_index = lax.axis_index("seq")
    my_y = lax.axis_index("batch")
    my_c = seq_index % C
    my_x = (seq_index // C) % X
    my_z = seq_index // (C * X)
    rows, width = tokens.shape[1:]
    hidden = ffn_in.shape[1]
    part = width // devices
    fan = hidden // width
    inputs = tokens[0]

    small = jnp.concatenate([gains, biases], axis=0).T
    small = jnp.pad(small, ((0, 0), (0, 128 - small.shape[1])))
    first_pack = jnp.concatenate([self_out, cross_q, cross_out, cross_kv, small], axis=1)
    outer_blocks = ffn_out.reshape(fan, part, width).transpose(1, 0, 2).reshape(part, hidden)
    second_pack = jnp.concatenate([ffn_in, outer_blocks], axis=1)
    first_all = lax.all_gather(first_pack, ("seq", "batch"), axis=0, tiled=True)
    second_all = lax.all_gather(second_pack, ("seq", "batch"), axis=0, tiled=True)

    token_parts = [inputs] + [grid.send(inputs, "z", m) for m in range(1, Z)]

    grouped = self_qkv.reshape(part, 3, GROUPS, GROUP_WIDTH)
    extra = jnp.stack([biases[3], biases[4]], axis=1)
    extra = jnp.broadcast_to(
        jnp.pad(extra, ((0, 0), (0, PACK - EXTRA - 2)))[:, None], (part, GROUPS, PACK - EXTRA)
    )
    packed = jnp.concatenate(
        [
            grouped[:, 0, :, :128],
            grouped[:, 1, :, :128],
            grouped[:, 2, :, :128],
            grouped[:, 0, :, 128:],
            grouped[:, 1, :, 128:],
            grouped[:, 2, :, 128:],
            extra,
        ],
        axis=2,
    ).transpose(1, 0, 2)
    pieces = [take(packed, my_z, 0)]
    for shift in range(1, Z):
        pieces.append(grid.send(take(packed, (my_z + shift) % Z, 0), "z", shift))
    gathered = roll_pieces([pieces[(-m) % Z] for m in range(Z)], my_z)
    for axis, me in (("y", my_y), ("x", my_x), ("c", my_c)):
        size = getattr(grid, axis)
        pieces = [gathered] + [grid.send(gathered, axis, m) for m in range(1, size)]
        gathered = roll_pieces([pieces[(-m) % size] for m in range(size)], me)
    qkv_group = gathered.transpose(3, 1, 0, 2, 4, 5).reshape(width, PACK)
    column = jnp.arange(PACK)
    bias_rows = lax.dynamic_slice_in_dim(qkv_group[:, EXTRA : EXTRA + 2], my_z * GROUP_WIDTH, GROUP_WIDTH, 0)
    query_bias, value_bias = bias_rows[:, 0], bias_rows[:, 1]
    none = jnp.zeros((128,), jnp.bfloat16)
    qkv_bias = wide(
        jnp.concatenate(
            [query_bias[:128], none, value_bias[:128], query_bias[128:], none[:64], value_bias[128:], none[:64]]
        )
    )
    real = (column < EXTRA)[None]
    qkv_weight = jnp.where(real, qkv_group, jnp.zeros_like(qkv_group))

    chunk = BANK_BLOCK * blocks.shape[1] // grid.seq
    per_block = BANK_BLOCK // chunk
    local_chunks = bank.shape[1] // chunk
    local_blocks = bank.shape[1] // BANK_BLOCK
    bank_chunks = bank[0].reshape(local_chunks, chunk, width)
    home = seq_index * local_blocks
    every = jnp.arange(grid.seq, dtype=jnp.int32)
    wanted = jnp.take(blocks[0], every // per_block) - home
    found = (wanted >= 0) & (wanted < local_blocks)
    spots = jnp.where(found, wanted * per_block + every % per_block, 0)
    picked = pick_rows(bank_chunks, spots, found).reshape(Z, X, C, chunk, width)
    shares = scatter_step(grid, picked, "c", my_c, 2)
    shares = scatter_step(grid, shares, "x", my_x, 1)
    own_rows = scatter_step(grid, shares, "z", my_z, 0)

    def spread(own):
        array = jnp.stack([own] + [grid.send(own, "z", m) for m in range(1, Z)])
        array = jnp.stack([array] + [grid.send(array, "x", m) for m in range(1, X)])
        return jnp.stack([array, grid.send(array, "c", 1)])

    all_rows = spread(own_rows).reshape(grid.seq * chunk, width)

    qkv_parts = [rounded(matmul(piece, qkv_weight) + qkv_bias) for piece in token_parts]
    own_side = jnp.concatenate(
        qkv_parts + [grid.send(piece, "x", m) for m in range(1, X) for piece in qkv_parts], axis=0
    )
    other_side = grid.send(own_side, "c", 1)

    order = jnp.arange(C * X * Z, dtype=jnp.int32)
    block_z = (my_z - order % Z) % Z
    block_x = (my_x - (order // Z) % X) % X
    block_c = (my_c + order // (Z * X)) % C
    key_firsts = ((block_z * X + block_x) * C + block_c) * rows
    turn = jnp.arange(GROUPS, dtype=jnp.int32)
    mirror_x = (2 * my_x - X + 1) % X
    query_blocks = jnp.where(turn % 2 == 0, turn, (X + mirror_x) * Z + turn)
    query_firsts = jnp.take(key_firsts, query_blocks)
    table = jnp.concatenate([key_firsts, query_blocks, query_firsts, prefix]).astype(jnp.int32)

    attention, lse = self_forward(table, own_side, other_side, rows)
    attention_mine = rounded(attention)

    def to_owner(array, m):
        def target(z, x, c, y):
            z, x, c = grid.fold((z - m) % Z, x, c, m)
            return z, x, c, y

        return grid.permute(array, target)

    def to_worker(array, m):
        def target(z, x, c, y):
            z, x, c = grid.fold((z + m) % Z, x, c, m)
            return z, x, c, y

        return grid.permute(array, target)

    pieces = [attention_mine[0]] + [to_owner(attention_mine[m], m) for m in range(1, Z)]
    attention_low = (
        roll_pieces(pieces, my_z)[:, :, :GROUP_WIDTH].transpose(1, 0, 2).reshape(rows, width)
    )

    selfout_full = first_all[:, :width]
    crossq_full = first_all[:, width : 2 * width]
    crossout_full = first_all[:, 2 * width : 3 * width]
    crosskv_full = first_all[:, 3 * width : 5 * width]
    small_full = wide(first_all[:, 5 * width :].T)
    gain = small_full[:3]
    bias = small_full[3:17]
    ffnin_full = second_all[:, :hidden]
    ffnout_full = (
        second_all[:, hidden:]
        .reshape(devices, part, fan, width)
        .transpose(0, 2, 1, 3)
        .reshape(hidden, width)
    )

    resid_one = wide(inputs) + matmul(attention_low, selfout_full) + bias[5]
    hidden_one = layer_norm(resid_one, gain[0], bias[0])
    hidden_one_low = rounded(hidden_one)
    cross_query = rounded(matmul(hidden_one_low, crossq_full) + bias[6])
    cross_pair = rounded(
        matmul(all_rows, crosskv_full) + jnp.concatenate([jnp.zeros((width,), jnp.float32), bias[7]])
    )
    cross_att, cross_lse = cross_forward(cross_query, cross_pair)
    resid_two = hidden_one + matmul(cross_att, crossout_full) + bias[8]
    hidden_two = layer_norm(resid_two, gain[1], bias[1])
    hidden_two_low = rounded(hidden_two)
    inner = matmul(hidden_two_low, ffnin_full) + bias[10:14].reshape(-1)
    activated = rounded(gelu_exact(inner))
    resid_three = hidden_two + matmul(activated, ffnout_full) + bias[9]
    output = layer_norm(resid_three, gain[2], bias[2])

    _unused, norm_three = jax.vjp(layer_norm, resid_three, gain[2], bias[2])
    dresid_three, dgain_three, dshift_three = norm_three(wide(cotangent[0]))
    douter_low = rounded(dresid_three)
    grad_ffnout = rounded(weight_grad(activated, douter_low))
    _unused, gelu_back = jax.vjp(gelu_exact, inner)
    dinner_low = rounded(gelu_back(back_matmul(douter_low, ffnout_full))[0])
    grad_ffnin = rounded(weight_grad(hidden_two_low, dinner_low))

    def reduce_shards(array):
        count = array.shape[0] // devices
        columns = array.shape[1]
        array = array.reshape(Z, X, C, Y, count, columns)
        array = scatter_step(grid, array, "c", my_c, 2)
        cut = columns // 256 * 128
        left = scatter_step(grid, array[..., :cut], "x", my_x, 1)
        right = scatter_step(grid, array[..., cut:], "y", my_y, 2)
        left = scatter_step(grid, left, "y", my_y, 1)
        right = scatter_step(grid, right, "x", my_x, 1)
        array = jnp.concatenate([left, right], axis=-1)
        total = wide(take(array, my_z, 0))
        for shift in range(1, Z):
            total = total + wide(grid.send(take(array, (my_z + shift) % Z, 0), "z", shift))
        return total

    out_ffnout = reduce_shards(grad_ffnout)
    out_ffnin = reduce_shards(grad_ffnin)

    _unused, norm_two = jax.vjp(layer_norm, resid_two, gain[1], bias[1])
    dresid_two, dgain_two, dshift_two = norm_two(dresid_three + back_matmul(dinner_low, ffnin_full))
    dcross_low = rounded(dresid_two)
    grad_crossout = rounded(weight_grad(cross_att, dcross_low))
    dcross_att = rounded(back_matmul(dcross_low, crossout_full))
    dcross_query, dcross_key, dcross_value = cross_backward(
        cross_query, cross_pair, dcross_att, cross_lse
    )
    grad_crossq = rounded(weight_grad(hidden_one_low, dcross_query))
    _unused, norm_one = jax.vjp(layer_norm, resid_one, gain[0], bias[0])
    dresid_one, dgain_one, dshift_one = norm_one(dresid_two + back_matmul(dcross_query, crossq_full))
    dbranch_low = rounded(dresid_one)
    grad_selfout = rounded(weight_grad(attention_low, dbranch_low))
    datt_low = rounded(back_matmul(dbranch_low, selfout_full))
    datt_groups = jnp.pad(
        datt_low.reshape(rows, GROUPS, GROUP_WIDTH).transpose(1, 0, 2),
        ((0, 0), (0, 0), (0, 256 - GROUP_WIDTH)),
    )
    pieces = [take(datt_groups, my_z, 0)]
    for m in range(1, Z):
        pieces.append(to_worker(take(datt_groups, (my_z + m) % Z, 0), m))
    own_grad, other_grad = self_backward(
        table, own_side, other_side, jnp.stack(pieces), attention, lse, rows
    )

    dcross_all = jnp.concatenate([dcross_key, dcross_value], axis=1)
    dcross_all = dcross_all.reshape(C, X, Z, chunk, 2 * width)

    def unspread(array):
        total = wide(array[0]) + wide(grid.send(array[1], "c", 1))
        array = rounded(total)
        total = wide(array[0])
        for m in range(1, X):
            total = total + wide(grid.send(array[m], "x", -m))
        array = rounded(total)
        total = wide(array[0])
        for m in range(1, Z):
            total = total + wide(grid.send(array[m], "z", -m))
        return rounded(total)

    dcross_pair = unspread(dcross_all)
    grad_crosskv = rounded(weight_grad(own_rows, dcross_pair))
    drows = spread(rounded(back_matmul(dcross_pair, crosskv_full))).reshape(grid.seq, chunk, width)
    source = (block_z * X + block_x) * C + block_c
    target = jnp.take(blocks[0], source // per_block) - home
    inside = (target >= 0) & (target < local_blocks)
    places = jnp.where(inside, target * per_block + source % per_block, -1)
    bank_grad = place_rows(drows, places, local_chunks).reshape(bank.shape[1], width)

    dqkv = rounded(wide(own_grad) + wide(grid.send(other_grad, "c", 1)))
    dqkv = dqkv.reshape(X, Z, rows, PACK)
    total = wide(dqkv[0])
    for m in range(1, X):
        total = total + wide(grid.send(dqkv[m], "x", -m))
    dqkv = rounded(total)
    dqkv = jnp.where(real[None], dqkv, jnp.zeros_like(dqkv))
    tokens_grad = dresid_one + back_matmul(dqkv[0], qkv_weight)
    for m in range(1, Z):
        tokens_grad = tokens_grad + wide(
            grid.send(rounded(back_matmul(dqkv[m], qkv_weight)), "z", -m)
        )
    grad_group = weight_grad(token_parts[0], dqkv[0])
    for m in range(1, Z):
        grad_group = grad_group + weight_grad(token_parts[m], dqkv[m])
    dqkv_sums = jnp.sum(wide(dqkv), axis=(0, 1))
    sums = jnp.stack(
        [
            jnp.concatenate([dqkv_sums[Q01 : Q01 + 128], dqkv_sums[Q2 : Q2 + 64]]),
            jnp.concatenate([dqkv_sums[V01 : V01 + 128], dqkv_sums[V2 : V2 + 64]]),
        ],
        axis=1,
    )
    sums = lax.dynamic_update_slice_in_dim(
        jnp.zeros((width, 2), jnp.float32), sums, my_z * GROUP_WIDTH, 0
    )
    grad_group = jnp.concatenate(
        [grad_group[:, :EXTRA], jnp.pad(sums, ((0, 0), (0, PACK - EXTRA - 2)))], axis=1
    )
    grad_group = rounded(grad_group).reshape(Z, X, C, Y, part, PACK)
    grad_group = scatter_step(grid, grad_group, "c", my_c, 2)
    grad_group = scatter_step(grid, grad_group, "x", my_x, 1)
    grad_group = scatter_step(grid, grad_group, "y", my_y, 1)
    pieces = [take(grad_group, my_z, 0)]
    for shift in range(1, Z):
        pieces.append(grid.send(take(grad_group, (my_z + shift) % Z, 0), "z", shift))
    grad_groups = wide(roll_pieces([pieces[(-m) % Z] for m in range(Z)], my_z))
    pair = grad_groups[:, :, :384].reshape(GROUPS, part, 3, 128)
    last = grad_groups[:, :, 384:576].reshape(GROUPS, part, 3, 64)
    out_qkv = (
        jnp.concatenate([pair, last], axis=-1).transpose(1, 2, 0, 3).reshape(part, 3 * width)
    )
    late_bias = jnp.sum(grad_groups[:, :, EXTRA : EXTRA + 2], axis=0)

    bias_rows = jnp.stack(
        [
            dgain_one,
            dgain_two,
            dgain_three,
            dshift_one,
            dshift_two,
            dshift_three,
            column_sums(dbranch_low),
            column_sums(dcross_query),
            column_sums(dcross_pair[:, width:]),
            column_sums(dcross_low),
            column_sums(douter_low),
        ]
    )
    bias_rows = jnp.concatenate([bias_rows, column_sums(dinner_low).reshape(fan, width)], axis=0)
    bias_columns = jnp.pad(rounded(bias_rows.T), ((0, 0), (0, 128 - bias_rows.shape[0])))
    rest = jnp.concatenate(
        [grad_selfout, grad_crossq, grad_crossout, grad_crosskv, bias_columns], axis=1
    )
    out_rest = reduce_shards(rest)
    out_small = out_rest[:, 5 * width :].T
    bias_grad = jnp.concatenate([out_small[3:6], late_bias.T, out_small[6:15]], axis=0)
    return (
        rounded(output)[None],
        tokens_grad[None],
        bank_grad[None],
        out_qkv,
        out_rest[:, :width],
        out_rest[:, width : 2 * width],
        out_rest[:, 3 * width : 5 * width],
        out_rest[:, 2 * width : 3 * width],
        out_ffnin,
        out_ffnout,
        out_small[:3],
        bias_grad,
    )


def solution(mesh):
    split = P("batch", "seq", None)
    shard = P(("seq", "batch"), None)
    flat = P(None, ("seq", "batch"))
    return jax.shard_map(
        functools.partial(body, Grid(mesh)),
        mesh=mesh,
        in_specs=(split, split, split, P("batch"), P("batch", None)) + (shard,) * 7 + (flat, flat),
        out_specs=(split, split, split) + (shard,) * 7 + (flat, flat),
        check_vma=False,
    )
```

```python
import functools

import jax
import jax.numpy as jnp
from jax import lax
from jax.experimental import pallas as pl
from jax.experimental.pallas import tpu as pltpu
from jax.sharding import PartitionSpec as P

HEADS = 12
HEAD_DIM = 64
BANK_BLOCK = 128
GROUPS = 4
GROUP_HEADS = HEADS // GROUPS
GROUP_WIDTH = GROUP_HEADS * HEAD_DIM
QUERY, SIDE = 256, 384
PACK = QUERY + SIDE
EPSILON = 1e-05
NEGATIVE = -1e30
SCALE = HEAD_DIM ** (-0.5)
LANES_IN = (((1,), (1,)), ((), ()))
ROWS_IN = (((0,), (0,)), ((), ()))
VMEM_LIMIT = 60 * 1024 * 1024


def layer_norm(values, gain, shift):
    centered = values - jnp.mean(values, axis=-1, keepdims=True)
    variance = jnp.mean(centered * centered, axis=-1, keepdims=True)
    return centered * lax.rsqrt(variance + EPSILON) * gain + shift


def gelu_exact(values):
    return jax.nn.gelu(values, approximate=False)


def rounded(values):
    return values.astype(jnp.bfloat16)


def wide(values):
    return values.astype(jnp.float32)


def matmul(left, right):
    return jnp.dot(left, right, preferred_element_type=jnp.float32)


def weight_grad(left, right):
    return lax.dot_general(left, right, ROWS_IN, preferred_element_type=jnp.float32)


def back_matmul(left, right):
    return lax.dot_general(left, right, LANES_IN, preferred_element_type=jnp.float32)


def column_sums(values):
    return jnp.sum(wide(values), axis=0)


class Grid:
    def __init__(self, mesh):
        self.seq = mesh.shape["seq"]
        self.y = mesh.shape["batch"]
        self.z = GROUPS
        self.c = 2
        self.x = self.seq // (self.z * self.c)

    def coords(self, index):
        spot, y = divmod(index, self.y)
        spot, c = divmod(spot, self.c)
        z, x = divmod(spot, self.x)
        return z, x, c, y

    def index(self, z, x, c, y):
        return ((z * self.x + x) * self.c + c) * self.y + y

    def permute(self, array, target):
        pairs = []
        for index in range(self.seq * self.y):
            pairs.append((index, self.index(*target(*self.coords(index)))))
        return lax.ppermute(array, ("seq", "batch"), pairs)

    def send(self, array, axis, shift):
        size = getattr(self, axis)
        place = "zxcy".index(axis)

        def target(*spot):
            moved = list(spot)
            moved[place] = (moved[place] + shift) % size
            return tuple(moved)

        return self.permute(array, target)

    def fold(self, z, x, c, shift):
        if shift % 2 == 0:
            return z, x, c
        return z, self.x - 1 - x, self.c - 1 - c


def roll_pieces(pieces, me, axis=0):
    count = len(pieces)
    both = jnp.stack(list(pieces) + list(pieces[:-1]), axis=axis)
    return lax.dynamic_slice_in_dim(both, (count - me) % count, count, axis)


def take(array, index, axis):
    return lax.dynamic_index_in_dim(array, index, axis, keepdims=False)


def head_parts(block, scale, third_low):
    lane = lax.broadcasted_iota(jnp.int32, (block.shape[0], 128), 1)
    first = wide(block[:, 0:128]) * scale
    third = wide(block[:, 128:256]) * scale
    third = jnp.where(lane < 64, third, 0.0)
    if not third_low:
        third = pltpu.roll(third, 64, 1)
    return (
        rounded(jnp.where(lane < 64, first, 0.0)),
        rounded(jnp.where(lane >= 64, first, 0.0)),
        rounded(third),
    )


def key_tiles(ref, start, size):
    rows = pl.ds(start, size)
    keys = ref[rows, 0:128]
    values = ref[rows, 128:256]
    third = ref[rows, 256:384]
    return (keys, keys, third), (values, values, third)


def allowed_keys(key_first, query_first, prefix_len, shape):
    key_pos = key_first + lax.broadcasted_iota(jnp.int32, shape, 0)
    query_pos = query_first + lax.broadcasted_iota(jnp.int32, shape, 1)
    return (key_pos <= query_pos) | (key_pos < prefix_len)


def each_block(table, refs, rows, query_first, prefix_len, work):
    count = refs[0].shape[0] // rows
    for part, ref in enumerate(refs):

        def step(local, carry, part=part, ref=ref):
            block = part * count + local
            key_first = table[block]
            last = key_first + rows - 1
            seen = (key_first <= query_first + rows - 1) | (key_first < prefix_len)
            whole = (last <= query_first) | (last < prefix_len)

            @pl.when(seen & whole)
            def _():
                work(ref, local * rows, block, key_first, False)

            @pl.when(seen & jnp.logical_not(whole))
            def _():
                work(ref, local * rows, block, key_first, True)

            return carry

        lax.fori_loop(0, count, step, 0)


def forward_kernel(rows, parts, first, last, table, query_in, *refs):
    refs = list(refs)
    sides = [refs.pop(0) for _ in range(parts)]
    if not first:
        accum_in, stats_in = refs.pop(0), refs.pop(0)
    out, state, query, accum, stats = refs
    m = pl.program_id(0)
    blocks = parts * (sides[0].shape[0] // rows)
    query_first = table[blocks + m]
    prefix_len = table[blocks + GROUPS]
    for head, part in enumerate(head_parts(query_in[0], SCALE, True)):
        query[head] = part
    if first:
        accum[...] = jnp.zeros_like(accum)
        stats[0:8, :] = jnp.full((8, rows), NEGATIVE, jnp.float32)
        stats[8:16, :] = jnp.zeros((8, rows), jnp.float32)
    else:
        accum[...] = accum_in[0]
        stats[...] = stats_in[0]

    def work(ref, start, block, key_first, masked):
        keys, values = key_tiles(ref, start, rows)
        if masked:
            mask = allowed_keys(key_first, query_first, prefix_len, (rows, rows))
        for head in range(GROUP_HEADS):
            scores = lax.dot_general(
                keys[head], query[head], LANES_IN, preferred_element_type=jnp.float32
            )
            if masked:
                scores = jnp.where(mask, scores, NEGATIVE)
            old = stats[head : head + 1, :]
            top = jnp.maximum(old, jnp.max(scores, axis=0, keepdims=True))
            weights = jnp.exp(scores - top)
            shrink = jnp.exp(old - top)
            stats[head : head + 1, :] = top
            stats[8 + head : 9 + head, :] = stats[8 + head : 9 + head, :] * shrink + jnp.sum(
                weights, axis=0, keepdims=True
            )
            accum[head] = accum[head] * shrink + lax.dot_general(
                values[head], rounded(weights), ROWS_IN, preferred_element_type=jnp.float32
            )

    each_block(table, sides, rows, query_first, prefix_len, work)
    if not last:
        out[0] = accum[...]
        state[0] = stats[...]
        return
    totals = stats[8 : 8 + GROUP_HEADS, :]
    final = [accum[head] / totals[head : head + 1, :] for head in range(GROUP_HEADS)]
    line = lax.broadcasted_iota(jnp.int32, (128, rows), 0)
    out[0, :, 0:128] = jnp.where(line < 64, final[0], final[1]).T
    third = jnp.concatenate([final[2][64:128], jnp.zeros((64, rows), jnp.float32)], axis=0)
    out[0, :, 128:256] = third.T
    state[0] = jnp.zeros((8, rows), jnp.float32)
    state[0, 0:GROUP_HEADS, :] = stats[0:GROUP_HEADS, :] + jnp.log(totals)


def backward_kernel(rows, parts, first, last, table, query_in, dout, state, *refs):
    refs = list(refs)
    sides = [refs.pop(0) for _ in range(parts)]
    carried = refs.pop(0)
    grads_out = [refs.pop(0) for _ in range(parts)]
    qgrad_out = refs.pop(0)
    if first:
        state_out = refs.pop(0)
    query, accum, qgrad, lines = refs
    m = pl.program_id(0)
    count = sides[0].shape[0] // rows
    blocks = parts * count
    query_first = table[blocks + m]
    prefix_len = table[blocks + GROUPS]

    @pl.when(m == 0)
    def _():
        def clear(index, carry):
            accum[pl.ds(index * rows, rows), :] = jnp.zeros((rows, SIDE), jnp.float32)
            return carry

        lax.fori_loop(0, blocks, clear, 0)

    for head, part in enumerate(head_parts(query_in[0], SCALE, True)):
        query[head] = part
    for head, part in enumerate(head_parts(dout[0], 1.0, False)):
        query[GROUP_HEADS + head] = part
    lines[...] = state[0]
    if first:
        pair_prod = (wide(dout[0, :, 0:128]) * carried[0, :, 0:128]).T
        third_prod = (wide(dout[0, :, 128:256]) * carried[0, :, 128:256]).T
        lines[3:4, :] = jnp.sum(pair_prod[0:64], axis=0, keepdims=True)
        lines[4:5, :] = jnp.sum(pair_prod[64:128], axis=0, keepdims=True)
        lines[5:6, :] = jnp.sum(third_prod[0:64], axis=0, keepdims=True)
        state_out[0] = lines[...]
        qgrad[...] = jnp.zeros_like(qgrad)
    else:
        qgrad[...] = carried[0]

    def work(ref, start, block, key_first, masked):
        keys, values = key_tiles(ref, start, rows)
        if masked:
            mask = allowed_keys(key_first, query_first, prefix_len, (rows, rows))
        key_parts, value_parts = [], []
        for head in range(GROUP_HEADS):
            scores = lax.dot_general(
                keys[head], query[head], LANES_IN, preferred_element_type=jnp.float32
            )
            if masked:
                scores = jnp.where(mask, scores, NEGATIVE)
            probs = jnp.exp(scores - lines[head : head + 1, :])
            slopes = lax.dot_general(
                values[head],
                query[GROUP_HEADS + head],
                LANES_IN,
                preferred_element_type=jnp.float32,
            )
            low = rounded(probs * (slopes - lines[3 + head : 4 + head, :]))
            value_parts.append(matmul(rounded(probs), query[GROUP_HEADS + head]))
            key_parts.append(matmul(low, query[head]))
            qgrad[head] += lax.dot_general(
                keys[head], low, ROWS_IN, preferred_element_type=jnp.float32
            )
        span = pl.ds(pl.multiple_of(block * rows, rows), rows)
        accum[span, 0:128] += key_parts[0] + key_parts[1]
        accum[span, 128:256] += value_parts[0] + value_parts[1]
        accum[span, 256:384] += key_parts[2] + value_parts[2]

    each_block(table, sides, rows, query_first, prefix_len, work)
    if last:
        line = lax.broadcasted_iota(jnp.int32, (128, rows), 0)
        qgrad_out[0, :, 0:128] = rounded(jnp.where(line < 64, qgrad[0], qgrad[1]).T * SCALE)
        qgrad_out[0, :, 128:256] = rounded(jnp.where(line < 64, qgrad[2], 0.0).T * SCALE)
    else:
        qgrad_out[0] = qgrad[...]

    @pl.when(m == GROUPS - 1)
    def _():
        for part, ref in enumerate(grads_out):

            def write(index, carry, part=part, ref=ref):
                source = pl.ds((part * count + index) * rows, rows)
                ref[pl.ds(index * rows, rows), :] = rounded(accum[source, :])
                return carry

            lax.fori_loop(0, count, write, 0)


def whole(shape):
    return pl.BlockSpec(shape, lambda *_: (0,) * len(shape), pipeline_mode=pl.Buffered(1))


def slab(shape):
    return pl.BlockSpec((1,) + shape, lambda m, *_: (m,) + (0,) * len(shape))


def self_forward(table, queries, sides, carried, last):
    rows = queries.shape[1]
    parts, length = len(sides), sides[0].shape[0]
    pairs = GROUPS * parts * length // rows * GROUP_HEADS // 2
    accum, stats = (GROUP_HEADS, 128, rows), (16, rows)
    outs = [(rows, 256), (8, rows)] if last else [accum, stats]
    first = carried is None
    return pl.pallas_call(
        functools.partial(forward_kernel, rows, parts, first, last),
        grid_spec=pltpu.PrefetchScalarGridSpec(
            num_scalar_prefetch=1,
            grid=(GROUPS,),
            in_specs=[slab((rows, QUERY))]
            + [whole((length, SIDE))] * parts
            + ([] if first else [slab(accum), slab(stats)]),
            out_specs=[slab(shape) for shape in outs],
            scratch_shapes=[
                pltpu.VMEM((GROUP_HEADS, rows, 128), jnp.bfloat16),
                pltpu.VMEM(accum, jnp.float32),
                pltpu.VMEM(stats, jnp.float32),
            ],
        ),
        out_shape=[jax.ShapeDtypeStruct((GROUPS,) + shape, jnp.float32) for shape in outs],
        compiler_params=pltpu.CompilerParams(vmem_limit_bytes=VMEM_LIMIT),
        cost_estimate=pl.CostEstimate(
            flops=pairs * rows * rows * 128 * 16,
            bytes_accessed=4 * length * parts * SIDE,
            transcendentals=pairs * rows * rows,
        ),
        name="self_forward",
    )(table, queries, *sides, *(() if first else carried))


def self_backward(table, queries, dout, state, sides, carried, first, last):
    rows = queries.shape[1]
    parts, length = len(sides), sides[0].shape[0]
    pairs = GROUPS * parts * length // rows * GROUP_HEADS // 2
    slope = (GROUP_HEADS, 128, rows)
    outs = [jax.ShapeDtypeStruct((length, SIDE), jnp.bfloat16)] * parts
    out_specs = [whole((length, SIDE))] * parts
    if last:
        outs = outs + [jax.ShapeDtypeStruct((GROUPS, rows, QUERY), jnp.bfloat16)]
        out_specs = out_specs + [slab((rows, QUERY))]
    else:
        outs = outs + [jax.ShapeDtypeStruct((GROUPS,) + slope, jnp.float32)]
        out_specs = out_specs + [slab(slope)]
    if first:
        outs = outs + [jax.ShapeDtypeStruct((GROUPS, 8, rows), jnp.float32)]
        out_specs = out_specs + [slab((8, rows))]
    return pl.pallas_call(
        functools.partial(backward_kernel, rows, parts, first, last),
        grid_spec=pltpu.PrefetchScalarGridSpec(
            num_scalar_prefetch=1,
            grid=(GROUPS,),
            in_specs=[slab((rows, QUERY)), slab((rows, 256)), slab((8, rows))]
            + [whole((length, SIDE))] * parts
            + [slab((rows, 256)) if first else slab(slope)],
            out_specs=out_specs,
            scratch_shapes=[
                pltpu.VMEM((2 * GROUP_HEADS, rows, 128), jnp.bfloat16),
                pltpu.VMEM((parts * length, SIDE), jnp.float32),
                pltpu.VMEM(slope, jnp.float32),
                pltpu.VMEM((8, rows), jnp.float32),
            ],
        ),
        out_shape=outs,
        compiler_params=pltpu.CompilerParams(vmem_limit_bytes=VMEM_LIMIT),
        cost_estimate=pl.CostEstimate(
            flops=pairs * rows * rows * 128 * 20,
            bytes_accessed=8 * length * parts * SIDE,
            transcendentals=pairs * rows * rows,
        ),
        name="self_backward",
    )(table, queries, dout, state, *sides, carried)


def pair_heads(block, scale=1.0):
    lane = lax.broadcasted_iota(jnp.int32, block.shape, 1)
    values = wide(block) * scale
    return rounded(jnp.where(lane < 64, values, 0.0)), rounded(jnp.where(lane >= 64, values, 0.0))


def cross_forward_kernel(query, keys, values, out, lse):
    rows = query.shape[0]
    parts = pair_heads(query[...], SCALE)
    sides = []
    lse[0] = jnp.zeros((8, rows), jnp.float32)
    for head in range(2):
        scores = lax.dot_general(
            keys[...], parts[head], LANES_IN, preferred_element_type=jnp.float32
        )
        top = jnp.max(scores, axis=0, keepdims=True)
        weights = jnp.exp(scores - top)
        total = jnp.sum(weights, axis=0, keepdims=True)
        mixed = lax.dot_general(
            values[...], rounded(weights), ROWS_IN, preferred_element_type=jnp.float32
        )
        sides.append(mixed / total)
        lse[0, head : head + 1, :] = top + jnp.log(total)
    line = lax.broadcasted_iota(jnp.int32, (128, rows), 0)
    out[...] = rounded(jnp.where(line < 64, sides[0], sides[1]).T)


def cross_backward_kernel(query, keys, values, dout, lse, qgrad, kgrad, vgrad):
    rows = query.shape[0]
    parts = pair_heads(query[...], SCALE)
    grads = pair_heads(dout[...])
    sides, key_parts, value_parts = [], [], []
    for head in range(2):
        scores = lax.dot_general(
            keys[...], parts[head], LANES_IN, preferred_element_type=jnp.float32
        )
        probs = jnp.exp(scores - lse[0, head : head + 1, :])
        slopes = lax.dot_general(
            values[...], grads[head], LANES_IN, preferred_element_type=jnp.float32
        )
        delta = jnp.sum(probs * slopes, axis=0, keepdims=True)
        low = rounded(probs * (slopes - delta))
        value_parts.append(matmul(rounded(probs), grads[head]))
        key_parts.append(matmul(low, parts[head]))
        sides.append(lax.dot_general(keys[...], low, ROWS_IN, preferred_element_type=jnp.float32))
    line = lax.broadcasted_iota(jnp.int32, (128, rows), 0)
    qgrad[...] = rounded(jnp.where(line < 64, sides[0], sides[1]).T * SCALE)
    kgrad[...] = rounded(key_parts[0] + key_parts[1])
    vgrad[...] = rounded(value_parts[0] + value_parts[1])


def cross_forward(query, pair):
    rows, width = query.shape
    count = width // 128
    kept = pair.shape[0]
    return pl.pallas_call(
        cross_forward_kernel,
        grid=(count,),
        in_specs=[
            pl.BlockSpec((rows, 128), lambda i: (0, i)),
            pl.BlockSpec((kept, 128), lambda i: (0, i)),
            pl.BlockSpec((kept, 128), lambda i: (0, count + i)),
        ],
        out_specs=[
            pl.BlockSpec((rows, 128), lambda i: (0, i)),
            pl.BlockSpec((1, 8, rows), lambda i: (i, 0, 0)),
        ],
        out_shape=[
            jax.ShapeDtypeStruct((rows, width), jnp.bfloat16),
            jax.ShapeDtypeStruct((count, 8, rows), jnp.float32),
        ],
        compiler_params=pltpu.CompilerParams(vmem_limit_bytes=VMEM_LIMIT),
        cost_estimate=pl.CostEstimate(
            flops=8 * rows * kept * width, bytes_accessed=4 * kept * width, transcendentals=12 * rows * kept
        ),
        name="cross_forward",
    )(query, pair, pair)


def cross_backward(query, pair, dout, lse):
    rows, width = query.shape
    count = width // 128
    kept = pair.shape[0]
    return pl.pallas_call(
        cross_backward_kernel,
        grid=(count,),
        in_specs=[
            pl.BlockSpec((rows, 128), lambda i: (0, i)),
            pl.BlockSpec((kept, 128), lambda i: (0, i)),
            pl.BlockSpec((kept, 128), lambda i: (0, count + i)),
            pl.BlockSpec((rows, 128), lambda i: (0, i)),
            pl.BlockSpec((1, 8, rows), lambda i: (i, 0, 0)),
        ],
        out_specs=[
            pl.BlockSpec((rows, 128), lambda i: (0, i)),
            pl.BlockSpec((kept, 128), lambda i: (0, i)),
            pl.BlockSpec((kept, 128), lambda i: (0, i)),
        ],
        out_shape=[
            jax.ShapeDtypeStruct((rows, width), jnp.bfloat16),
            jax.ShapeDtypeStruct((kept, width), jnp.bfloat16),
            jax.ShapeDtypeStruct((kept, width), jnp.bfloat16),
        ],
        compiler_params=pltpu.CompilerParams(vmem_limit_bytes=VMEM_LIMIT),
        cost_estimate=pl.CostEstimate(
            flops=20 * rows * kept * width, bytes_accessed=8 * kept * width, transcendentals=12 * rows * kept
        ),
        name="cross_backward",
    )(query, pair, pair, dout, lse)


def pick_kernel(table, bank, out):
    i = pl.program_id(0)
    keep = table[pl.num_programs(0) + i]
    out[0] = jnp.where(keep > 0, bank[0], jnp.zeros_like(bank[0]))


def pick_rows(chunks, spots, found):
    count = spots.shape[0]
    size = chunks.shape[1:]
    table = jnp.concatenate([spots, found.astype(jnp.int32)])
    return pl.pallas_call(
        pick_kernel,
        grid_spec=pltpu.PrefetchScalarGridSpec(
            num_scalar_prefetch=1,
            grid=(count,),
            in_specs=[pl.BlockSpec((1,) + size, lambda i, t: (t[i], 0, 0))],
            out_specs=pl.BlockSpec((1,) + size, lambda i, t: (i, 0, 0)),
        ),
        out_shape=jax.ShapeDtypeStruct((count,) + size, chunks.dtype),
        name="pick_rows",
    )(table, chunks)


def place_kernel(count, table, grads, out):
    spot = pl.program_id(0)
    out[...] = jnp.zeros_like(out)
    for i in range(count):

        @pl.when(table[i] == spot)
        def _(i=i):
            out[0] += wide(grads[i])


def place_rows(grads, spots, chunks):
    count = spots.shape[0]
    size = grads.shape[1:]
    return pl.pallas_call(
        functools.partial(place_kernel, count),
        grid_spec=pltpu.PrefetchScalarGridSpec(
            num_scalar_prefetch=1,
            grid=(chunks,),
            in_specs=[whole((count,) + size)],
            out_specs=pl.BlockSpec((1,) + size, lambda n, t: (n, 0, 0)),
        ),
        out_shape=jax.ShapeDtypeStruct((chunks,) + size, jnp.float32),
        name="place_rows",
    )(spots, grads)


class Chain:
    def __init__(self, stages):
        self.stages = stages
        self.result = None
        self.pending = next(stages)

    def step(self, pending):
        try:
            self.pending = self.stages.send(pending)
        except StopIteration as stop:
            self.pending, self.result = (), stop.value


def meet(values, *chains):
    values, pending = lax.optimization_barrier((values, [chain.pending for chain in chains]))
    for chain, arrays in zip(chains, pending):
        chain.step(arrays)
    return values


def total_of(arrays):
    total = wide(arrays[0])
    for array in arrays[1:]:
        total = total + wide(array)
    return total


def body(
    grid,
    tokens,
    cotangent,
    bank,
    prefix,
    blocks,
    self_qkv,
    self_out,
    cross_q,
    cross_kv,
    cross_out,
    ffn_in,
    ffn_out,
    gains,
    biases,
):
    Z, X, C, Y = grid.z, grid.x, grid.c, grid.y
    devices = grid.seq * Y
    seq_index = lax.axis_index("seq")
    me = {
        "y": lax.axis_index("batch"),
        "c": seq_index % C,
        "x": (seq_index // C) % X,
        "z": seq_index // (C * X),
    }
    my_z, my_x, my_c = me["z"], me["x"], me["c"]
    rows, width = tokens.shape[1:]
    hidden = ffn_in.shape[1]
    part = width // devices
    fan = hidden // width
    inputs = tokens[0]

    def parted(array, axis, place):
        size = getattr(grid, axis)
        kept = [take(array, me[axis], place)]
        for shift in range(1, size):
            kept.append(grid.send(take(array, (me[axis] + shift) % size, place), axis, shift))
        return kept

    def reduction(array, axes, lead=0, final=True):
        names = ["z", "x", "c", "y"]
        for axis in axes:
            place = lead + names.index(axis)
            names.remove(axis)
            arrays = yield parted(array, axis, place)
            total = total_of(arrays)
            array = rounded(total)
        return total if final else array

    def sharded(array):
        return array.reshape(Z, X, C, Y, array.shape[0] // devices, array.shape[1])

    grouped = self_qkv.reshape(part, 3, GROUPS, GROUP_WIDTH)
    extra = jnp.stack([biases[3], biases[4]], axis=1)
    extra = jnp.broadcast_to(
        jnp.pad(extra, ((0, 0), (0, QUERY - GROUP_WIDTH - 2)))[:, None],
        (part, GROUPS, QUERY - GROUP_WIDTH),
    )
    packed = jnp.concatenate(
        [
            grouped[:, 0],
            extra,
            grouped[:, 1, :, :128],
            grouped[:, 2, :, :128],
            grouped[:, 1, :, 128:],
            grouped[:, 2, :, 128:],
        ],
        axis=2,
    ).transpose(1, 0, 2)
    pieces = parted(packed, "z", 0)

    small = jnp.concatenate([gains, biases], axis=0).T
    small = jnp.pad(small, ((0, 0), (0, 128 - small.shape[1])))
    first_pack = jnp.concatenate([self_out, cross_q, cross_out, cross_kv, small], axis=1)
    inner_columns = (
        ffn_in.reshape(part, devices, fan, part).transpose(0, 2, 1, 3).reshape(part, hidden)
    )
    outer_blocks = ffn_out.reshape(fan, part, width).transpose(1, 0, 2).reshape(part, hidden)
    second_pack = jnp.stack([inner_columns, outer_blocks])
    first_all = lax.all_gather(first_pack, ("seq", "batch"), axis=0, tiled=True)
    second_all = lax.all_gather(second_pack, ("seq", "batch"), axis=1, tiled=True)

    pieces, inputs = lax.optimization_barrier((pieces, inputs))
    token_parts = [inputs] + [grid.send(inputs, "z", m) for m in range(1, Z)]

    gathered = roll_pieces([pieces[(-m) % Z] for m in range(Z)], my_z)
    for axis in "yxc":
        size = getattr(grid, axis)
        pieces = [gathered] + [grid.send(gathered, axis, m) for m in range(1, size)]
        gathered = roll_pieces([pieces[(-m) % size] for m in range(size)], me[axis])
    qkv_group = gathered.transpose(3, 1, 0, 2, 4, 5).reshape(width, PACK)
    column = jnp.arange(PACK, dtype=jnp.int32)
    real = (column < GROUP_WIDTH) | (column >= QUERY)
    is_query = column < GROUP_WIDTH
    is_pair_value = (column >= QUERY + 128) & (column < QUERY + 256)
    is_value = is_pair_value | (column >= QUERY + 320)
    local = jnp.where(is_query, column, column - jnp.where(is_pair_value, QUERY + 128, QUERY + 192))
    line = jnp.where(is_query | is_value, local + my_z * GROUP_WIDTH, -1)
    chosen = (jnp.arange(width, dtype=jnp.int32)[:, None] == line[None]).astype(jnp.bfloat16)
    picked_bias = weight_grad(qkv_group[:, GROUP_WIDTH:QUERY], chosen)
    qkv_bias = jnp.where(is_query, picked_bias[0], picked_bias[1])
    qkv_weight = jnp.where(real[None], qkv_group, jnp.zeros_like(qkv_group))

    chunk = BANK_BLOCK * blocks.shape[1] // grid.seq
    per_block = BANK_BLOCK // chunk
    local_chunks = bank.shape[1] // chunk
    local_blocks = bank.shape[1] // BANK_BLOCK
    bank_chunks = bank[0].reshape(local_chunks, chunk, width)
    home = seq_index * local_blocks
    every = jnp.arange(grid.seq, dtype=jnp.int32)
    wanted = jnp.take(blocks[0], every // per_block) - home
    found = (wanted >= 0) & (wanted < local_blocks)
    spots = jnp.where(found, wanted * per_block + every % per_block, 0)
    picked = pick_rows(bank_chunks, spots, found).reshape(Z, X, C, 1, chunk, width)

    def spreading(own):
        array = jnp.stack((yield [own] + [grid.send(own, "z", m) for m in range(1, Z)]))
        array = jnp.stack((yield [array] + [grid.send(array, "x", m) for m in range(1, X)]))
        return jnp.stack((yield [array, grid.send(array, "c", 1)]))

    def retrieval():
        own = (yield from reduction(picked, "cxz", final=False))[0]
        every_row = yield from spreading(own)
        return own, every_row.reshape(grid.seq * chunk, width)

    retrieve = Chain(retrieval())

    token_column = jnp.concatenate(token_parts, axis=0)
    own_queries = rounded(matmul(token_column, qkv_weight[:, :QUERY]) + qkv_bias[:QUERY])
    own_side = rounded(matmul(token_column, qkv_weight[:, QUERY:]) + qkv_bias[QUERY:])
    own_queries, own_side = meet((own_queries, own_side), retrieve)
    own_queries = own_queries.reshape(GROUPS, rows, QUERY)

    def mirrored(array):
        return grid.permute(array, lambda z, x, c, y: (z, X - 1 - x, C - 1 - c, y))

    far_queries = mirrored(own_queries[1::2])
    near_other = grid.send(own_side, "c", 1)
    far_own = [grid.send(own_side, "x", m) for m in range(1, X)]
    queries = jnp.stack(
        [own_queries[m] if m % 2 == 0 else far_queries[m // 2] for m in range(GROUPS)]
    )

    turn = jnp.arange(GROUPS, dtype=jnp.int32)
    turn_z = (my_z - turn) % Z

    def key_firsts(x, c):
        return ((turn_z * X + x) * C + c) * rows

    query_firsts = jnp.where(
        turn % 2 == 0, key_firsts(my_x, my_c), key_firsts(X - 1 - my_x, C - 1 - my_c)
    )

    def table_of(shifts, c):
        keys = [key_firsts((my_x - m) % X, c) for m in shifts]
        return jnp.concatenate(keys + [query_firsts, prefix]).astype(jnp.int32)

    far = list(range(1, X))
    tables = {
        "near own": table_of([0], my_c),
        "near other": table_of([0], C - 1 - my_c),
        "far own": table_of(far, my_c),
        "far other": table_of(far, C - 1 - my_c),
    }

    carry = self_forward(tables["near own"], queries, [own_side], None, False)
    carry, near_other = meet((carry, near_other), retrieve)
    carry = self_forward(tables["near other"], queries, [near_other], carry, False)
    carry, far_own = meet((carry, far_own), retrieve)
    far_other = [grid.send(side, "c", 1) for side in far_own]
    carry = self_forward(tables["far own"], queries, far_own, carry, False)
    carry, far_other = meet((carry, far_other), retrieve)
    attention, lse = self_forward(tables["far other"], queries, far_other, carry, True)
    attention, lse = meet((attention, lse), retrieve)
    attention_mine = rounded(attention)

    def to_owner(array, m):
        def target(z, x, c, y):
            z, x, c = grid.fold((z - m) % Z, x, c, m)
            return z, x, c, y

        return grid.permute(array, target)

    def to_worker(array, m):
        def target(z, x, c, y):
            z, x, c = grid.fold((z + m) % Z, x, c, m)
            return z, x, c, y

        return grid.permute(array, target)

    pieces = [attention_mine[0]] + [to_owner(attention_mine[m], m) for m in range(1, Z)]
    pieces = meet(pieces, retrieve)
    own_rows, all_rows = retrieve.result
    attention_low = (
        roll_pieces(pieces, my_z)[:, :, :GROUP_WIDTH].transpose(1, 0, 2).reshape(rows, width)
    )

    selfout_full = first_all[:, :width]
    crossq_full = first_all[:, width : 2 * width]
    crossout_full = first_all[:, 2 * width : 3 * width]
    crosskv_full = first_all[:, 3 * width : 5 * width]
    small_full = wide(first_all[:, 5 * width :].T)
    gain = small_full[:3]
    bias = small_full[3:17]
    ffnin_full = second_all[0]
    outer = [second_all[1, :, f * width : (f + 1) * width] for f in range(fan)]
    inner_bias = bias[10:14].reshape(devices, fan, part).transpose(1, 0, 2).reshape(-1)

    resid_one = wide(inputs) + matmul(attention_low, selfout_full) + bias[5]
    hidden_one = layer_norm(resid_one, gain[0], bias[0])
    hidden_one_low = rounded(hidden_one)
    cross_query = rounded(matmul(hidden_one_low, crossq_full) + bias[6])
    cross_pair = rounded(
        matmul(all_rows, crosskv_full) + jnp.concatenate([jnp.zeros((width,), jnp.float32), bias[7]])
    )
    cross_att, cross_lse = cross_forward(cross_query, cross_pair)
    resid_two = hidden_one + matmul(cross_att, crossout_full) + bias[8]
    hidden_two = layer_norm(resid_two, gain[1], bias[1])
    hidden_two_low = rounded(hidden_two)
    inner = matmul(hidden_two_low, ffnin_full) + inner_bias
    activated = rounded(gelu_exact(inner))

    def fan_part(array, f):
        return array[:, f * width : (f + 1) * width]

    resid_three = hidden_two + bias[9]
    for f in range(fan):
        resid_three = resid_three + matmul(fan_part(activated, f), outer[f])
    output = layer_norm(resid_three, gain[2], bias[2])

    _unused, norm_three = jax.vjp(layer_norm, resid_three, gain[2], bias[2])
    dresid_three, dgain_three, dshift_three = norm_three(wide(cotangent[0]))
    douter_low = rounded(dresid_three)
    grad_ffnout = rounded(weight_grad(activated, douter_low))
    reduce_ffnout = Chain(
        reduction(grad_ffnout.reshape(fan, Z, X, C, Y, part, width), "cyxz", lead=1)
    )
    _unused, gelu_back = jax.vjp(gelu_exact, inner)
    dactivated = jnp.concatenate([back_matmul(douter_low, block) for block in outer], axis=1)
    dinner_low = rounded(gelu_back(dactivated)[0])
    grad_ffnin = rounded(weight_grad(hidden_two_low, dinner_low))
    reduce_ffnin = Chain(reduction(sharded(grad_ffnin), "cxyz"))

    _unused, norm_two = jax.vjp(layer_norm, resid_two, gain[1], bias[1])
    dresid_two, dgain_two, dshift_two = norm_two(dresid_three + back_matmul(dinner_low, ffnin_full))
    dcross_low = rounded(dresid_two)
    dcross_att = rounded(back_matmul(dcross_low, crossout_full))
    dcross_query, dcross_key, dcross_value = cross_backward(
        cross_query, cross_pair, dcross_att, cross_lse
    )
    dcross_query, dcross_key, dcross_value = meet(
        (dcross_query, dcross_key, dcross_value), reduce_ffnout, reduce_ffnin
    )

    dcross_all = jnp.concatenate([dcross_key, dcross_value], axis=1)
    dcross_all = dcross_all.reshape(C, X, Z, chunk, 2 * width)

    def unspreading(array):
        for axis in "cxz":
            size = getattr(grid, axis)
            arrays = yield [array[0]] + [grid.send(array[m], axis, -m) for m in range(1, size)]
            array = rounded(total_of(arrays))
        return array

    unspread = Chain(unspreading(dcross_all))

    _unused, norm_one = jax.vjp(layer_norm, resid_one, gain[0], bias[0])
    dresid_one, dgain_one, dshift_one = norm_one(dresid_two + back_matmul(dcross_query, crossq_full))
    dbranch_low = rounded(dresid_one)
    datt_low = rounded(back_matmul(dbranch_low, selfout_full))
    datt_groups = jnp.pad(
        datt_low.reshape(rows, GROUPS, GROUP_WIDTH).transpose(1, 0, 2),
        ((0, 0), (0, 0), (0, 256 - GROUP_WIDTH)),
    )
    pieces = [take(datt_groups, my_z, 0)]
    for m in range(1, Z):
        pieces.append(to_worker(take(datt_groups, (my_z + m) % Z, 0), m))
    grad_mid = jnp.concatenate(
        [
            rounded(weight_grad(attention_low, dbranch_low)),
            rounded(weight_grad(hidden_one_low, dcross_query)),
            rounded(weight_grad(cross_att, dcross_low)),
        ],
        axis=1,
    )
    grad_mid, pieces = meet((grad_mid, pieces), unspread)
    reduce_mid = Chain(reduction(sharded(grad_mid), "cyxz"))
    dout = jnp.stack(pieces)

    *far_other_grad, slopes, state = self_backward(
        tables["far other"], queries, dout, lse, far_other, attention, True, False
    )
    far_other_grad, slopes = meet(
        (far_other_grad, slopes), reduce_ffnout, reduce_ffnin, reduce_mid
    )
    far_moved = [grid.send(grad, "c", 1) for grad in far_other_grad]
    *far_own_grad, slopes = self_backward(
        tables["far own"], queries, dout, state, far_own, slopes, False, False
    )
    far_own_grad, far_moved, slopes = meet(
        (far_own_grad, far_moved, slopes), unspread, reduce_ffnout, reduce_ffnin
    )
    far_grad = [rounded(total_of(pair)) for pair in zip(far_own_grad, far_moved)]
    far_moved = [grid.send(grad, "x", -m) for m, grad in zip(far, far_grad)]
    near_other_grad, slopes = self_backward(
        tables["near other"], queries, dout, state, [near_other], slopes, False, False
    )
    near_other_grad, slopes = meet((near_other_grad, slopes), unspread, reduce_mid)
    near_moved = grid.send(near_other_grad, "c", 1)

    dcross_pair = unspread.result
    bias_rows = jnp.stack(
        [
            dgain_one,
            dgain_two,
            dgain_three,
            dshift_one,
            dshift_two,
            dshift_three,
            column_sums(dbranch_low),
            column_sums(dcross_query),
            column_sums(dcross_pair[:, width:]),
            column_sums(dcross_low),
            column_sums(douter_low),
        ]
    )
    inner_sums = column_sums(dinner_low).reshape(fan, devices, part).transpose(1, 0, 2)
    bias_rows = jnp.concatenate([bias_rows, inner_sums.reshape(fan, width)], axis=0)
    bias_columns = jnp.pad(rounded(bias_rows.T), ((0, 0), (0, 128 - bias_rows.shape[0])))
    grad_late = jnp.concatenate([rounded(weight_grad(own_rows, dcross_pair)), bias_columns], axis=1)
    reduce_late = Chain(reduction(sharded(grad_late), "cyxz"))
    spread_back = Chain(spreading(rounded(back_matmul(dcross_pair, crosskv_full))))

    near_own_grad, query_grad = self_backward(
        tables["near own"], queries, dout, state, [own_side], slopes, False, True
    )
    near_own_grad, near_moved, far_moved, query_grad = meet(
        (near_own_grad, near_moved, far_moved, query_grad), reduce_late, reduce_mid, spread_back
    )

    far_query_grad = mirrored(query_grad[1::2])
    side_grad = rounded(total_of([near_own_grad, near_moved] + far_moved))
    far_query_grad, side_grad = meet((far_query_grad, side_grad))
    query_grad = jnp.stack(
        [query_grad[m] if m % 2 == 0 else far_query_grad[m // 2] for m in range(GROUPS)]
    )
    dqkv = jnp.concatenate([query_grad.reshape(GROUPS * rows, QUERY), side_grad], axis=1)
    far_tokens_grad = rounded(back_matmul(dqkv[rows:], qkv_weight)).reshape(Z - 1, rows, width)
    far_tokens_grad = [grid.send(far_tokens_grad[m - 1], "z", -m) for m in range(1, Z)]
    grad_group = weight_grad(token_column, dqkv)
    sums = jnp.sum(wide(dqkv), axis=0)
    sums = jnp.stack([jnp.where(is_query, sums, 0.0), jnp.where(is_value, sums, 0.0)])
    sums = jnp.pad(rounded(sums), ((0, QUERY - GROUP_WIDTH - 2), (0, 0)))
    grad_group = jnp.concatenate(
        [grad_group[:, :GROUP_WIDTH], back_matmul(chosen, sums), grad_group[:, QUERY:]], axis=1
    )
    reduce_group = Chain(reduction(sharded(rounded(grad_group)).reshape(Z, X, C, Y, part, PACK), "cxy", final=False))
    tokens_base = dresid_one + back_matmul(dqkv[:rows], qkv_weight)
    tokens_base = meet(tokens_base, reduce_group, spread_back)
    tokens_base = meet(tokens_base, reduce_group, reduce_late, spread_back)
    tokens_base = meet(tokens_base, reduce_group, reduce_late)
    pieces = parted(reduce_group.result, "z", 0)
    tokens_grad = total_of([tokens_base] + far_tokens_grad)
    for chain in (reduce_ffnout, reduce_ffnin, reduce_mid, reduce_late):
        chain.step(chain.pending)

    source_x = (my_x - (jnp.arange(X * Z, dtype=jnp.int32) // Z)) % X
    source_z = (my_z - jnp.arange(X * Z, dtype=jnp.int32) % Z) % Z
    source = jnp.concatenate(
        [(source_z * X + source_x) * C + (my_c + c) % C for c in range(C)]
    )
    target = jnp.take(blocks[0], source // per_block) - home
    inside = (target >= 0) & (target < local_blocks)
    places = jnp.where(inside, target * per_block + source % per_block, -1)
    drows = spread_back.result.reshape(grid.seq, chunk, width)
    bank_grad = place_rows(drows, places, local_chunks).reshape(bank.shape[1], width)

    grad_groups = wide(roll_pieces([pieces[(-m) % Z] for m in range(Z)], my_z))
    sides = grad_groups[:, :, QUERY:]
    out_qkv = jnp.stack(
        [
            grad_groups[:, :, :GROUP_WIDTH],
            jnp.concatenate([sides[:, :, :128], sides[:, :, 256:320]], axis=2),
            jnp.concatenate([sides[:, :, 128:256], sides[:, :, 320:384]], axis=2),
        ]
    )
    out_qkv = out_qkv.transpose(2, 0, 1, 3).reshape(part, 3 * width)
    late_bias = jnp.sum(grad_groups[:, :, GROUP_WIDTH : GROUP_WIDTH + 2], axis=0)

    out_late, out_mid = reduce_late.result, reduce_mid.result
    out_ffnin = (
        reduce_ffnin.result.reshape(part, fan, devices, part)
        .transpose(0, 2, 1, 3)
        .reshape(part, hidden)
    )
    out_small = out_late[:, 2 * width :].T
    bias_grad = jnp.concatenate([out_small[3:6], late_bias.T, out_small[6:15]], axis=0)
    return (
        rounded(output)[None],
        tokens_grad[None],
        bank_grad[None],
        out_qkv,
        out_mid[:, :width],
        out_mid[:, width : 2 * width],
        out_late[:, : 2 * width],
        out_mid[:, 2 * width :],
        out_ffnin,
        reduce_ffnout.result.reshape(fan * part, width),
        out_small[:3],
        bias_grad,
    )


def solution(mesh):
    split = P("batch", "seq", None)
    shard = P(("seq", "batch"), None)
    flat = P(None, ("seq", "batch"))
    return jax.shard_map(
        functools.partial(body, Grid(mesh)),
        mesh=mesh,
        in_specs=(split, split, split, P("batch"), P("batch", None)) + (shard,) * 7 + (flat, flat),
        out_specs=(split, split, split) + (shard,) * 7 + (flat, flat),
        check_vma=False,
    )
```

```python
import functools

import jax
import jax.numpy as jnp
from jax import lax
from jax.experimental import pallas as pl
from jax.experimental.pallas import tpu as pltpu
from jax.sharding import PartitionSpec as P

HEADS = 12
HEAD_DIM = 64
BANK_BLOCK = 128
GROUPS = 4
GROUP_HEADS = HEADS // GROUPS
GROUP_WIDTH = GROUP_HEADS * HEAD_DIM
QUERY, SIDE = 256, 384
PACK = QUERY + SIDE
EPSILON = 1e-05
NEGATIVE = -1e30
SCALE = HEAD_DIM ** (-0.5)
LANES_IN = (((1,), (1,)), ((), ()))
ROWS_IN = (((0,), (0,)), ((), ()))
VMEM_LIMIT = 60 * 1024 * 1024


def layer_norm(values, gain, shift):
    centered = values - jnp.mean(values, axis=-1, keepdims=True)
    variance = jnp.mean(centered * centered, axis=-1, keepdims=True)
    return centered * lax.rsqrt(variance + EPSILON) * gain + shift


def gelu_exact(values):
    return jax.nn.gelu(values, approximate=False)


def rounded(values):
    return values.astype(jnp.bfloat16)


def wide(values):
    return values.astype(jnp.float32)


def matmul(left, right):
    return jnp.dot(left, right, preferred_element_type=jnp.float32)


def weight_grad(left, right):
    return lax.dot_general(left, right, ROWS_IN, preferred_element_type=jnp.float32)


def back_matmul(left, right):
    return lax.dot_general(left, right, LANES_IN, preferred_element_type=jnp.float32)


def column_sums(values):
    return jnp.sum(wide(values), axis=0)


class Grid:
    def __init__(self, mesh):
        self.seq = mesh.shape["seq"]
        self.y = mesh.shape["batch"]
        self.z = GROUPS
        self.c = self.h = self.l = 2
        self.x = self.seq // (self.z * self.c)

    def coords(self, index):
        spot, y = divmod(index, self.y)
        spot, c = divmod(spot, self.c)
        z, x = divmod(spot, self.x)
        return z, x, c, y

    def index(self, z, x, c, y):
        return ((z * self.x + x) * self.c + c) * self.y + y

    def send(self, array, axis, shift, mirror=False):
        if axis in "hl":
            axis, shift = "z", shift * (2 if axis == "h" else 1)
        place = "zxcy".index(axis)
        pairs = []
        for index in range(self.seq * self.y):
            spot = list(self.coords(index))
            spot[place] ^= shift
            if mirror:
                spot[1], spot[2] = self.x - 1 - spot[1], self.c - 1 - spot[2]
            pairs.append((index, self.index(*spot)))
        return lax.ppermute(array, ("seq", "batch"), pairs)


def in_order(pieces, me):
    pieces = list(pieces)
    bit = 1
    while bit < len(pieces):
        swap = (me & bit) != 0
        pieces = [jnp.where(swap, pieces[j ^ bit], piece) for j, piece in enumerate(pieces)]
        bit *= 2
    return jnp.stack(pieces)


def take(array, index, axis):
    return lax.dynamic_index_in_dim(array, index, axis, keepdims=False)


def head_parts(block, scale, third_low):
    lane = lax.broadcasted_iota(jnp.int32, (block.shape[0], 128), 1)
    first = wide(block[:, 0:128]) * scale
    third = wide(block[:, 128:256]) * scale
    third = jnp.where(lane < 64, third, 0.0)
    if not third_low:
        third = pltpu.roll(third, 64, 1)
    return (
        rounded(jnp.where(lane < 64, first, 0.0)),
        rounded(jnp.where(lane >= 64, first, 0.0)),
        rounded(third),
    )


def key_tiles(ref, start, size):
    rows = pl.ds(start, size)
    keys = ref[rows, 0:128]
    values = ref[rows, 128:256]
    third = ref[rows, 256:384]
    return (keys, keys, third), (values, values, third)


def allowed_keys(key_first, query_first, prefix_len, shape):
    key_pos = key_first + lax.broadcasted_iota(jnp.int32, shape, 0)
    query_pos = query_first + lax.broadcasted_iota(jnp.int32, shape, 1)
    return (key_pos <= query_pos) | (key_pos < prefix_len)


def each_block(table, refs, rows, query_first, prefix_len, work):
    count = refs[0].shape[0] // rows
    for part, ref in enumerate(refs):

        def step(local, carry, part=part, ref=ref):
            block = part * count + local
            key_first = table[block]
            last = key_first + rows - 1
            seen = (key_first <= query_first + rows - 1) | (key_first < prefix_len)
            whole = (last <= query_first) | (last < prefix_len)

            @pl.when(seen & whole)
            def _():
                work(ref, local * rows, block, key_first, False)

            @pl.when(seen & jnp.logical_not(whole))
            def _():
                work(ref, local * rows, block, key_first, True)

            return carry

        lax.fori_loop(0, count, step, 0)


def forward_kernel(rows, parts, first, last, table, query_in, *refs):
    refs = list(refs)
    sides = [refs.pop(0) for _ in range(parts)]
    if not first:
        accum_in, stats_in = refs.pop(0), refs.pop(0)
    out, state, query, accum, stats = refs
    m = pl.program_id(0)
    blocks = parts * (sides[0].shape[0] // rows)
    query_first = table[blocks + m]
    prefix_len = table[blocks + GROUPS]
    for head, part in enumerate(head_parts(query_in[0], SCALE, True)):
        query[head] = part
    if first:
        accum[...] = jnp.zeros_like(accum)
        stats[0:8, :] = jnp.full((8, rows), NEGATIVE, jnp.float32)
        stats[8:16, :] = jnp.zeros((8, rows), jnp.float32)
    else:
        accum[...] = accum_in[0]
        stats[...] = stats_in[0]

    def work(ref, start, block, key_first, masked):
        keys, values = key_tiles(ref, start, rows)
        if masked:
            mask = allowed_keys(key_first, query_first, prefix_len, (rows, rows))
        for head in range(GROUP_HEADS):
            scores = lax.dot_general(
                keys[head], query[head], LANES_IN, preferred_element_type=jnp.float32
            )
            if masked:
                scores = jnp.where(mask, scores, NEGATIVE)
            old = stats[head : head + 1, :]
            top = jnp.maximum(old, jnp.max(scores, axis=0, keepdims=True))
            weights = jnp.exp(scores - top)
            shrink = jnp.exp(old - top)
            stats[head : head + 1, :] = top
            stats[8 + head : 9 + head, :] = stats[8 + head : 9 + head, :] * shrink + jnp.sum(
                weights, axis=0, keepdims=True
            )
            accum[head] = accum[head] * shrink + lax.dot_general(
                values[head], rounded(weights), ROWS_IN, preferred_element_type=jnp.float32
            )

    each_block(table, sides, rows, query_first, prefix_len, work)
    if not last:
        out[0] = accum[...]
        state[0] = stats[...]
        return
    totals = stats[8 : 8 + GROUP_HEADS, :]
    final = [accum[head] / totals[head : head + 1, :] for head in range(GROUP_HEADS)]
    line = lax.broadcasted_iota(jnp.int32, (128, rows), 0)
    out[0, :, 0:128] = jnp.where(line < 64, final[0], final[1]).T
    third = jnp.concatenate([final[2][64:128], jnp.zeros((64, rows), jnp.float32)], axis=0)
    out[0, :, 128:256] = third.T
    state[0] = jnp.zeros((8, rows), jnp.float32)
    state[0, 0:GROUP_HEADS, :] = stats[0:GROUP_HEADS, :] + jnp.log(totals)


def backward_kernel(rows, parts, first, last, table, query_in, dout, state, *refs):
    refs = list(refs)
    sides = [refs.pop(0) for _ in range(parts)]
    carried = refs.pop(0)
    grads_out = [refs.pop(0) for _ in range(parts)]
    qgrad_out = refs.pop(0)
    if first:
        state_out = refs.pop(0)
    query, accum, qgrad, lines = refs
    m = pl.program_id(0)
    count = sides[0].shape[0] // rows
    blocks = parts * count
    query_first = table[blocks + m]
    prefix_len = table[blocks + GROUPS]

    @pl.when(m == 0)
    def _():
        def clear(index, carry):
            accum[pl.ds(index * rows, rows), :] = jnp.zeros((rows, SIDE), jnp.float32)
            return carry

        lax.fori_loop(0, blocks, clear, 0)

    for head, part in enumerate(head_parts(query_in[0], SCALE, True)):
        query[head] = part
    for head, part in enumerate(head_parts(dout[0], 1.0, False)):
        query[GROUP_HEADS + head] = part
    lines[...] = state[0]
    if first:
        pair_prod = (wide(dout[0, :, 0:128]) * carried[0, :, 0:128]).T
        third_prod = (wide(dout[0, :, 128:256]) * carried[0, :, 128:256]).T
        lines[3:4, :] = jnp.sum(pair_prod[0:64], axis=0, keepdims=True)
        lines[4:5, :] = jnp.sum(pair_prod[64:128], axis=0, keepdims=True)
        lines[5:6, :] = jnp.sum(third_prod[0:64], axis=0, keepdims=True)
        state_out[0] = lines[...]
        qgrad[...] = jnp.zeros_like(qgrad)
    else:
        qgrad[...] = carried[0]

    def work(ref, start, block, key_first, masked):
        keys, values = key_tiles(ref, start, rows)
        if masked:
            mask = allowed_keys(key_first, query_first, prefix_len, (rows, rows))
        key_parts, value_parts = [], []
        for head in range(GROUP_HEADS):
            scores = lax.dot_general(
                keys[head], query[head], LANES_IN, preferred_element_type=jnp.float32
            )
            if masked:
                scores = jnp.where(mask, scores, NEGATIVE)
            probs = jnp.exp(scores - lines[head : head + 1, :])
            slopes = lax.dot_general(
                values[head],
                query[GROUP_HEADS + head],
                LANES_IN,
                preferred_element_type=jnp.float32,
            )
            low = rounded(probs * (slopes - lines[3 + head : 4 + head, :]))
            value_parts.append(matmul(rounded(probs), query[GROUP_HEADS + head]))
            key_parts.append(matmul(low, query[head]))
            qgrad[head] += lax.dot_general(
                keys[head], low, ROWS_IN, preferred_element_type=jnp.float32
            )
        span = pl.ds(pl.multiple_of(block * rows, rows), rows)
        accum[span, 0:128] += key_parts[0] + key_parts[1]
        accum[span, 128:256] += value_parts[0] + value_parts[1]
        accum[span, 256:384] += key_parts[2] + value_parts[2]

    each_block(table, sides, rows, query_first, prefix_len, work)
    if last:
        line = lax.broadcasted_iota(jnp.int32, (128, rows), 0)
        qgrad_out[0, :, 0:128] = rounded(jnp.where(line < 64, qgrad[0], qgrad[1]).T * SCALE)
        qgrad_out[0, :, 128:256] = rounded(jnp.where(line < 64, qgrad[2], 0.0).T * SCALE)
    else:
        qgrad_out[0] = qgrad[...]

    @pl.when(m == GROUPS - 1)
    def _():
        for part, ref in enumerate(grads_out):

            def write(index, carry, part=part, ref=ref):
                source = pl.ds((part * count + index) * rows, rows)
                ref[pl.ds(index * rows, rows), :] = rounded(accum[source, :])
                return carry

            lax.fori_loop(0, count, write, 0)


def whole(shape):
    return pl.BlockSpec(shape, lambda *_: (0,) * len(shape), pipeline_mode=pl.Buffered(1))


def slab(shape):
    return pl.BlockSpec((1,) + shape, lambda m, *_: (m,) + (0,) * len(shape))


def self_forward(table, queries, sides, carried, last):
    rows = queries.shape[1]
    parts, length = len(sides), sides[0].shape[0]
    pairs = GROUPS * parts * length // rows * GROUP_HEADS // 2
    accum, stats = (GROUP_HEADS, 128, rows), (16, rows)
    outs = [(rows, 256), (8, rows)] if last else [accum, stats]
    first = carried is None
    return pl.pallas_call(
        functools.partial(forward_kernel, rows, parts, first, last),
        grid_spec=pltpu.PrefetchScalarGridSpec(
            num_scalar_prefetch=1,
            grid=(GROUPS,),
            in_specs=[slab((rows, QUERY))]
            + [whole((length, SIDE))] * parts
            + ([] if first else [slab(accum), slab(stats)]),
            out_specs=[slab(shape) for shape in outs],
            scratch_shapes=[
                pltpu.VMEM((GROUP_HEADS, rows, 128), jnp.bfloat16),
                pltpu.VMEM(accum, jnp.float32),
                pltpu.VMEM(stats, jnp.float32),
            ],
        ),
        out_shape=[jax.ShapeDtypeStruct((GROUPS,) + shape, jnp.float32) for shape in outs],
        compiler_params=pltpu.CompilerParams(vmem_limit_bytes=VMEM_LIMIT),
        cost_estimate=pl.CostEstimate(
            flops=pairs * rows * rows * 128 * 16,
            bytes_accessed=4 * length * parts * SIDE,
            transcendentals=pairs * rows * rows,
        ),
        name="self_forward",
    )(table, queries, *sides, *(() if first else carried))


def self_backward(table, queries, dout, state, sides, carried, first, last):
    rows = queries.shape[1]
    parts, length = len(sides), sides[0].shape[0]
    pairs = GROUPS * parts * length // rows * GROUP_HEADS // 2
    slope = (GROUP_HEADS, 128, rows)
    outs = [jax.ShapeDtypeStruct((length, SIDE), jnp.bfloat16)] * parts
    out_specs = [whole((length, SIDE))] * parts
    if last:
        outs = outs + [jax.ShapeDtypeStruct((GROUPS, rows, QUERY), jnp.bfloat16)]
        out_specs = out_specs + [slab((rows, QUERY))]
    else:
        outs = outs + [jax.ShapeDtypeStruct((GROUPS,) + slope, jnp.float32)]
        out_specs = out_specs + [slab(slope)]
    if first:
        outs = outs + [jax.ShapeDtypeStruct((GROUPS, 8, rows), jnp.float32)]
        out_specs = out_specs + [slab((8, rows))]
    return pl.pallas_call(
        functools.partial(backward_kernel, rows, parts, first, last),
        grid_spec=pltpu.PrefetchScalarGridSpec(
            num_scalar_prefetch=1,
            grid=(GROUPS,),
            in_specs=[slab((rows, QUERY)), slab((rows, 256)), slab((8, rows))]
            + [whole((length, SIDE))] * parts
            + [slab((rows, 256)) if first else slab(slope)],
            out_specs=out_specs,
            scratch_shapes=[
                pltpu.VMEM((2 * GROUP_HEADS, rows, 128), jnp.bfloat16),
                pltpu.VMEM((parts * length, SIDE), jnp.float32),
                pltpu.VMEM(slope, jnp.float32),
                pltpu.VMEM((8, rows), jnp.float32),
            ],
        ),
        out_shape=outs,
        compiler_params=pltpu.CompilerParams(vmem_limit_bytes=VMEM_LIMIT),
        cost_estimate=pl.CostEstimate(
            flops=pairs * rows * rows * 128 * 20,
            bytes_accessed=8 * length * parts * SIDE,
            transcendentals=pairs * rows * rows,
        ),
        name="self_backward",
    )(table, queries, dout, state, *sides, carried)


def pair_heads(block, scale=1.0):
    lane = lax.broadcasted_iota(jnp.int32, block.shape, 1)
    values = wide(block) * scale
    return rounded(jnp.where(lane < 64, values, 0.0)), rounded(jnp.where(lane >= 64, values, 0.0))


def cross_forward_kernel(query, keys, values, out, lse):
    rows = query.shape[0]
    parts = pair_heads(query[...], SCALE)
    sides = []
    lse[0] = jnp.zeros((8, rows), jnp.float32)
    for head in range(2):
        scores = lax.dot_general(
            keys[...], parts[head], LANES_IN, preferred_element_type=jnp.float32
        )
        top = jnp.max(scores, axis=0, keepdims=True)
        weights = jnp.exp(scores - top)
        total = jnp.sum(weights, axis=0, keepdims=True)
        mixed = lax.dot_general(
            values[...], rounded(weights), ROWS_IN, preferred_element_type=jnp.float32
        )
        sides.append(mixed / total)
        lse[0, head : head + 1, :] = top + jnp.log(total)
    line = lax.broadcasted_iota(jnp.int32, (128, rows), 0)
    out[...] = rounded(jnp.where(line < 64, sides[0], sides[1]).T)


def cross_backward_kernel(query, keys, values, dout, lse, qgrad, kgrad, vgrad):
    rows = query.shape[0]
    parts = pair_heads(query[...], SCALE)
    grads = pair_heads(dout[...])
    sides, key_parts, value_parts = [], [], []
    for head in range(2):
        scores = lax.dot_general(
            keys[...], parts[head], LANES_IN, preferred_element_type=jnp.float32
        )
        probs = jnp.exp(scores - lse[0, head : head + 1, :])
        slopes = lax.dot_general(
            values[...], grads[head], LANES_IN, preferred_element_type=jnp.float32
        )
        delta = jnp.sum(probs * slopes, axis=0, keepdims=True)
        low = rounded(probs * (slopes - delta))
        value_parts.append(matmul(rounded(probs), grads[head]))
        key_parts.append(matmul(low, parts[head]))
        sides.append(lax.dot_general(keys[...], low, ROWS_IN, preferred_element_type=jnp.float32))
    line = lax.broadcasted_iota(jnp.int32, (128, rows), 0)
    qgrad[...] = rounded(jnp.where(line < 64, sides[0], sides[1]).T * SCALE)
    kgrad[...] = rounded(key_parts[0] + key_parts[1])
    vgrad[...] = rounded(value_parts[0] + value_parts[1])


def cross_forward(query, pair):
    rows, width = query.shape
    count = width // 128
    kept = pair.shape[0]
    return pl.pallas_call(
        cross_forward_kernel,
        grid=(count,),
        in_specs=[
            pl.BlockSpec((rows, 128), lambda i: (0, i)),
            pl.BlockSpec((kept, 128), lambda i: (0, i)),
            pl.BlockSpec((kept, 128), lambda i: (0, count + i)),
        ],
        out_specs=[
            pl.BlockSpec((rows, 128), lambda i: (0, i)),
            pl.BlockSpec((1, 8, rows), lambda i: (i, 0, 0)),
        ],
        out_shape=[
            jax.ShapeDtypeStruct((rows, width), jnp.bfloat16),
            jax.ShapeDtypeStruct((count, 8, rows), jnp.float32),
        ],
        compiler_params=pltpu.CompilerParams(vmem_limit_bytes=VMEM_LIMIT),
        cost_estimate=pl.CostEstimate(
            flops=8 * rows * kept * width, bytes_accessed=4 * kept * width, transcendentals=12 * rows * kept
        ),
        name="cross_forward",
    )(query, pair, pair)


def cross_backward(query, pair, dout, lse):
    rows, width = query.shape
    count = width // 128
    kept = pair.shape[0]
    return pl.pallas_call(
        cross_backward_kernel,
        grid=(count,),
        in_specs=[
            pl.BlockSpec((rows, 128), lambda i: (0, i)),
            pl.BlockSpec((kept, 128), lambda i: (0, i)),
            pl.BlockSpec((kept, 128), lambda i: (0, count + i)),
            pl.BlockSpec((rows, 128), lambda i: (0, i)),
            pl.BlockSpec((1, 8, rows), lambda i: (i, 0, 0)),
        ],
        out_specs=[
            pl.BlockSpec((rows, 128), lambda i: (0, i)),
            pl.BlockSpec((kept, 128), lambda i: (0, i)),
            pl.BlockSpec((kept, 128), lambda i: (0, i)),
        ],
        out_shape=[
            jax.ShapeDtypeStruct((rows, width), jnp.bfloat16),
            jax.ShapeDtypeStruct((kept, width), jnp.bfloat16),
            jax.ShapeDtypeStruct((kept, width), jnp.bfloat16),
        ],
        compiler_params=pltpu.CompilerParams(vmem_limit_bytes=VMEM_LIMIT),
        cost_estimate=pl.CostEstimate(
            flops=20 * rows * kept * width, bytes_accessed=8 * kept * width, transcendentals=12 * rows * kept
        ),
        name="cross_backward",
    )(query, pair, pair, dout, lse)


def pick_kernel(table, bank, out):
    i = pl.program_id(0)
    keep = table[pl.num_programs(0) + i]
    out[0] = jnp.where(keep > 0, bank[0], jnp.zeros_like(bank[0]))


def pick_rows(chunks, spots, found):
    count = spots.shape[0]
    size = chunks.shape[1:]
    table = jnp.concatenate([spots, found.astype(jnp.int32)])
    return pl.pallas_call(
        pick_kernel,
        grid_spec=pltpu.PrefetchScalarGridSpec(
            num_scalar_prefetch=1,
            grid=(count,),
            in_specs=[pl.BlockSpec((1,) + size, lambda i, t: (t[i], 0, 0))],
            out_specs=pl.BlockSpec((1,) + size, lambda i, t: (i, 0, 0)),
        ),
        out_shape=jax.ShapeDtypeStruct((count,) + size, chunks.dtype),
        name="pick_rows",
    )(table, chunks)


def place_kernel(count, table, grads, out):
    spot = pl.program_id(0)
    out[...] = jnp.zeros_like(out)
    for i in range(count):

        @pl.when(table[i] == spot)
        def _(i=i):
            out[0] += wide(grads[i])


def place_rows(grads, spots, chunks):
    count = spots.shape[0]
    size = grads.shape[1:]
    return pl.pallas_call(
        functools.partial(place_kernel, count),
        grid_spec=pltpu.PrefetchScalarGridSpec(
            num_scalar_prefetch=1,
            grid=(chunks,),
            in_specs=[whole((count,) + size)],
            out_specs=pl.BlockSpec((1,) + size, lambda n, t: (n, 0, 0)),
        ),
        out_shape=jax.ShapeDtypeStruct((chunks,) + size, jnp.float32),
        name="place_rows",
    )(spots, grads)


class Chain:
    def __init__(self, stages):
        self.stages = stages
        self.result = None
        self.pending = next(stages)

    def step(self, pending):
        try:
            self.pending = self.stages.send(pending)
        except StopIteration as stop:
            self.pending, self.result = (), stop.value


def meet(values, *chains):
    values, pending = lax.optimization_barrier((values, [chain.pending for chain in chains]))
    for chain, arrays in zip(chains, pending):
        chain.step(arrays)
    return values


def total_of(arrays):
    total = wide(arrays[0])
    for array in arrays[1:]:
        total = total + wide(array)
    return total


def body(
    grid,
    tokens,
    cotangent,
    bank,
    prefix,
    blocks,
    self_qkv,
    self_out,
    cross_q,
    cross_kv,
    cross_out,
    ffn_in,
    ffn_out,
    gains,
    biases,
):
    Z, X, C, Y = grid.z, grid.x, grid.c, grid.y
    devices = grid.seq * Y
    seq_index = lax.axis_index("seq")
    me = {
        "y": lax.axis_index("batch"),
        "c": seq_index % C,
        "x": (seq_index // C) % X,
        "z": seq_index // (C * X),
        "h": seq_index // (2 * C * X),
        "l": seq_index // (C * X) % 2,
    }
    my_z, my_x, my_c = me["z"], me["x"], me["c"]
    rows, width = tokens.shape[1:]
    hidden = ffn_in.shape[1]
    part = width // devices
    fan = hidden // width
    inputs = tokens[0]

    def parted(array, axis, place):
        size = getattr(grid, axis)
        kept = [take(array, me[axis], place)]
        for shift in range(1, size):
            kept.append(grid.send(take(array, me[axis] ^ shift, place), axis, shift))
        return kept

    def reduction(array, axes, lead=0, final=True):
        names = ["h", "l", "x", "c", "y"]
        for axis in axes:
            place = lead + names.index(axis)
            names.remove(axis)
            arrays = yield parted(array, axis, place)
            total = total_of(arrays)
            array = rounded(total)
        return total if final else array

    def sharded(array):
        return array.reshape(2, 2, X, C, Y, array.shape[0] // devices, array.shape[1])

    grouped = self_qkv.reshape(part, 3, GROUPS, GROUP_WIDTH)
    extra = jnp.stack([biases[3], biases[4]], axis=1)
    extra = jnp.broadcast_to(
        jnp.pad(extra, ((0, 0), (0, QUERY - GROUP_WIDTH - 2)))[:, None],
        (part, GROUPS, QUERY - GROUP_WIDTH),
    )
    packed = jnp.concatenate(
        [
            grouped[:, 0],
            extra,
            grouped[:, 1, :, :128],
            grouped[:, 2, :, :128],
            grouped[:, 1, :, 128:],
            grouped[:, 2, :, 128:],
        ],
        axis=2,
    ).transpose(1, 0, 2)
    pieces = parted(packed, "z", 0)

    small = jnp.concatenate([gains, biases], axis=0).T
    small = jnp.pad(small, ((0, 0), (0, 128 - small.shape[1])))
    first_pack = jnp.concatenate([self_out, cross_q, cross_out, cross_kv, small], axis=1)
    inner_columns = (
        ffn_in.reshape(part, devices, fan, part).transpose(0, 2, 1, 3).reshape(part, hidden)
    )
    outer_blocks = ffn_out.reshape(fan, part, width).transpose(1, 0, 2).reshape(part, hidden)
    second_pack = jnp.stack([inner_columns, outer_blocks])
    first_all = lax.all_gather(first_pack, ("seq", "batch"), axis=0, tiled=True)
    second_all = lax.all_gather(second_pack, ("seq", "batch"), axis=1, tiled=True)

    pieces, inputs = lax.optimization_barrier((pieces, inputs))
    across = grid.send(inputs, "h", 1)
    token_parts = [inputs, grid.send(inputs, "l", 1), across, grid.send(across, "l", 1)]

    chunk = BANK_BLOCK * blocks.shape[1] // grid.seq
    per_block = BANK_BLOCK // chunk
    local_chunks = bank.shape[1] // chunk
    local_blocks = bank.shape[1] // BANK_BLOCK
    bank_chunks = bank[0].reshape(local_chunks, chunk, width)
    home = seq_index * local_blocks
    every = jnp.arange(grid.seq, dtype=jnp.int32)
    wanted = jnp.take(blocks[0], every // per_block) - home
    found = (wanted >= 0) & (wanted < local_blocks)
    spots = jnp.where(found, wanted * per_block + every % per_block, 0)
    picked = pick_rows(bank_chunks, spots, found).reshape(2, 2, X, C, 1, chunk, width)

    def spreading(own):
        array = own
        for axis in "hlxc":
            size = getattr(grid, axis)
            array = jnp.stack((yield [array] + [grid.send(array, axis, m) for m in range(1, size)]))
        return array

    def retrieval():
        own = (yield from reduction(picked, "cxlh", final=False))[0]
        every_row = yield from spreading(own)
        return own, every_row.reshape(grid.seq * chunk, width)

    retrieve = Chain(retrieval())
    gathered = in_order(pieces, my_z)
    for axis in "yxc":
        pieces = [gathered] + [grid.send(gathered, axis, m) for m in range(1, getattr(grid, axis))]
        if axis == "y":
            pieces = meet(pieces, retrieve)
        gathered = in_order(pieces, me[axis])
    qkv_group = gathered.transpose(3, 1, 0, 2, 4, 5).reshape(width, PACK)
    column = jnp.arange(PACK, dtype=jnp.int32)
    real = (column < GROUP_WIDTH) | (column >= QUERY)
    is_query = column < GROUP_WIDTH
    is_pair_value = (column >= QUERY + 128) & (column < QUERY + 256)
    is_value = is_pair_value | (column >= QUERY + 320)
    local = jnp.where(is_query, column, column - jnp.where(is_pair_value, QUERY + 128, QUERY + 192))
    line = jnp.where(is_query | is_value, local + my_z * GROUP_WIDTH, -1)
    chosen = (jnp.arange(width, dtype=jnp.int32)[:, None] == line[None]).astype(jnp.bfloat16)
    picked_bias = weight_grad(qkv_group[:, GROUP_WIDTH:QUERY], chosen)
    qkv_bias = jnp.where(is_query, picked_bias[0], picked_bias[1])
    qkv_weight = jnp.where(real[None], qkv_group, jnp.zeros_like(qkv_group))

    qkv_weight, qkv_bias, token_parts = meet((qkv_weight, qkv_bias, token_parts), retrieve)

    token_column = jnp.concatenate(token_parts, axis=0)
    own_queries = rounded(matmul(token_column, qkv_weight[:, :QUERY]) + qkv_bias[:QUERY])
    own_side = rounded(matmul(token_column, qkv_weight[:, QUERY:]) + qkv_bias[QUERY:])
    own_queries = own_queries.reshape(GROUPS, rows, QUERY)

    far_queries = grid.send(own_queries[1::2], "z", 0, mirror=True)
    near_other = grid.send(own_side, "c", 1)
    far_queries, side = lax.optimization_barrier((far_queries, own_side))
    far_own = [grid.send(side, "x", m) for m in range(1, X)]
    queries = jnp.stack(
        [own_queries[m] if m % 2 == 0 else far_queries[m // 2] for m in range(GROUPS)]
    )

    turn = jnp.arange(GROUPS, dtype=jnp.int32)
    turn_z = my_z ^ turn

    def key_firsts(x, c):
        return ((turn_z * X + x) * C + c) * rows

    query_firsts = jnp.where(
        turn % 2 == 0, key_firsts(my_x, my_c), key_firsts(X - 1 - my_x, C - 1 - my_c)
    )

    def table_of(shifts, c):
        keys = [key_firsts(my_x ^ m, c) for m in shifts]
        return jnp.concatenate(keys + [query_firsts, prefix]).astype(jnp.int32)

    far = list(range(1, X))
    tables = {
        "near own": table_of([0], my_c),
        "near other": table_of([0], C - 1 - my_c),
        "far own": table_of(far, my_c),
        "far other": table_of(far, C - 1 - my_c),
    }

    carry = self_forward(tables["near own"], queries, [own_side], None, False)
    carry, near_other = meet((carry, near_other), retrieve)
    carry = self_forward(tables["near other"], queries, [near_other], carry, False)
    carry, far_own = meet((carry, far_own), retrieve)
    far_other = [grid.send(side, "c", 1) for side in far_own]
    carry = self_forward(tables["far own"], queries, far_own, carry, False)
    carry, far_other = meet((carry, far_other), retrieve)
    attention, lse = self_forward(tables["far other"], queries, far_other, carry, True)
    attention, lse = meet((attention, lse), retrieve)
    attention_mine = rounded(attention)

    def swapped(array, m):
        return grid.send(array, "z", m, mirror=m % 2 == 1)

    pieces = [attention_mine[0]] + [swapped(attention_mine[m], m) for m in range(1, Z)]
    pieces = meet(pieces, retrieve)
    retrieve.step(retrieve.pending)
    own_rows, all_rows = retrieve.result
    attention_low = (
        in_order(pieces, my_z)[:, :, :GROUP_WIDTH].transpose(1, 0, 2).reshape(rows, width)
    )

    selfout_full = first_all[:, :width]
    crossq_full = first_all[:, width : 2 * width]
    crossout_full = first_all[:, 2 * width : 3 * width]
    crosskv_full = first_all[:, 3 * width : 5 * width]
    small_full = wide(first_all[:, 5 * width :].T)
    gain = small_full[:3]
    bias = small_full[3:17]
    ffnin_full = second_all[0]
    outer = [second_all[1, :, f * width : (f + 1) * width] for f in range(fan)]
    inner_bias = bias[10:14].reshape(devices, fan, part).transpose(1, 0, 2).reshape(-1)

    resid_one = wide(inputs) + matmul(attention_low, selfout_full) + bias[5]
    hidden_one = layer_norm(resid_one, gain[0], bias[0])
    hidden_one_low = rounded(hidden_one)
    cross_query = rounded(matmul(hidden_one_low, crossq_full) + bias[6])
    cross_pair = rounded(
        matmul(all_rows, crosskv_full) + jnp.concatenate([jnp.zeros((width,), jnp.float32), bias[7]])
    )
    cross_att, cross_lse = cross_forward(cross_query, cross_pair)
    resid_two = hidden_one + matmul(cross_att, crossout_full) + bias[8]
    hidden_two = layer_norm(resid_two, gain[1], bias[1])
    hidden_two_low = rounded(hidden_two)
    inner = matmul(hidden_two_low, ffnin_full) + inner_bias
    activated = rounded(gelu_exact(inner))

    def fan_part(array, f):
        return array[:, f * width : (f + 1) * width]

    resid_three = hidden_two + bias[9]
    for f in range(fan):
        resid_three = resid_three + matmul(fan_part(activated, f), outer[f])
    output = layer_norm(resid_three, gain[2], bias[2])

    _unused, norm_three = jax.vjp(layer_norm, resid_three, gain[2], bias[2])
    dresid_three, dgain_three, dshift_three = norm_three(wide(cotangent[0]))
    douter_low = rounded(dresid_three)
    grad_ffnout = rounded(weight_grad(activated, douter_low))
    reduce_ffnout = Chain(
        reduction(grad_ffnout.reshape(fan, 2, 2, X, C, Y, part, width), "cyxlh", lead=1)
    )
    _unused, gelu_back = jax.vjp(gelu_exact, inner)
    dactivated = jnp.concatenate([back_matmul(douter_low, block) for block in outer], axis=1)
    dinner_low = rounded(gelu_back(dactivated)[0])
    grad_ffnin = rounded(weight_grad(hidden_two_low, dinner_low))
    reduce_ffnin = Chain(reduction(sharded(grad_ffnin), "cyxlh"))

    _unused, norm_two = jax.vjp(layer_norm, resid_two, gain[1], bias[1])
    dresid_two, dgain_two, dshift_two = norm_two(dresid_three + back_matmul(dinner_low, ffnin_full))
    dcross_low = rounded(dresid_two)
    dcross_att = rounded(back_matmul(dcross_low, crossout_full))
    dcross_query, dcross_key, dcross_value = cross_backward(
        cross_query, cross_pair, dcross_att, cross_lse
    )
    dcross_query, dcross_key, dcross_value = meet(
        (dcross_query, dcross_key, dcross_value), reduce_ffnout, reduce_ffnin
    )

    dcross_all = jnp.concatenate([dcross_key, dcross_value], axis=1)
    dcross_all = dcross_all.reshape(C, X, 2, 2, chunk, 2 * width)

    def unspreading(array):
        for axis in "cxlh":
            size = getattr(grid, axis)
            arrays = yield [array[0]] + [grid.send(array[m], axis, m) for m in range(1, size)]
            array = rounded(total_of(arrays))
        return array

    unspread = Chain(unspreading(dcross_all))

    _unused, norm_one = jax.vjp(layer_norm, resid_one, gain[0], bias[0])
    dresid_one, dgain_one, dshift_one = norm_one(dresid_two + back_matmul(dcross_query, crossq_full))
    dbranch_low = rounded(dresid_one)
    datt_low = rounded(back_matmul(dbranch_low, selfout_full))
    datt_groups = jnp.pad(
        datt_low.reshape(rows, GROUPS, GROUP_WIDTH).transpose(1, 0, 2),
        ((0, 0), (0, 0), (0, 256 - GROUP_WIDTH)),
    )
    pieces = [take(datt_groups, my_z, 0)]
    for m in range(1, Z):
        pieces.append(swapped(take(datt_groups, my_z ^ m, 0), m))
    grad_mid = jnp.stack(
        [
            rounded(weight_grad(attention_low, dbranch_low)),
            rounded(weight_grad(hidden_one_low, dcross_query)),
            rounded(weight_grad(cross_att, dcross_low)),
        ]
    )
    grad_mid, pieces = meet((grad_mid, pieces), unspread)
    reduce_mid = Chain(reduction(grad_mid.reshape(3, 2, 2, X, C, Y, part, width), "cyxlh", lead=1))
    dout = jnp.stack(pieces)

    *far_other_grad, slopes, state = self_backward(
        tables["far other"], queries, dout, lse, far_other, attention, True, False
    )
    far_other_grad, slopes = meet(
        (far_other_grad, slopes), reduce_ffnout, reduce_mid, unspread
    )
    far_moved = [grid.send(grad, "c", 1) for grad in far_other_grad]
    *far_own_grad, slopes = self_backward(
        tables["far own"], queries, dout, state, far_own, slopes, False, False
    )
    far_own_grad, far_moved, slopes = meet(
        (far_own_grad, far_moved, slopes), unspread, reduce_ffnout, reduce_ffnin
    )
    far_grad = [rounded(total_of(pair)) for pair in zip(far_own_grad, far_moved)]
    far_moved = [grid.send(grad, "x", m) for m, grad in zip(far, far_grad)]
    near_other_grad, slopes = self_backward(
        tables["near other"], queries, dout, state, [near_other], slopes, False, False
    )
    near_other_grad, slopes = meet(
        (near_other_grad, slopes), unspread, reduce_ffnout, reduce_ffnin, reduce_mid
    )
    near_moved = grid.send(near_other_grad, "c", 1)

    dcross_pair = unspread.result
    bias_rows = jnp.stack(
        [
            dgain_one,
            dgain_two,
            dgain_three,
            dshift_one,
            dshift_two,
            dshift_three,
            column_sums(dbranch_low),
            column_sums(dcross_query),
            column_sums(dcross_pair[:, width:]),
            column_sums(dcross_low),
            column_sums(douter_low),
        ]
    )
    inner_sums = column_sums(dinner_low).reshape(fan, devices, part).transpose(1, 0, 2)
    bias_rows = jnp.concatenate([bias_rows, inner_sums.reshape(fan, width)], axis=0)
    bias_columns = jnp.pad(rounded(bias_rows.T), ((0, 0), (0, 128 - bias_rows.shape[0])))
    grad_late = jnp.concatenate([rounded(weight_grad(own_rows, dcross_pair)), bias_columns], axis=1)
    reduce_late = Chain(reduction(sharded(grad_late), "cyxlh"))
    spread_back = Chain(spreading(rounded(back_matmul(dcross_pair, crosskv_full))))

    near_own_grad, query_grad = self_backward(
        tables["near own"], queries, dout, state, [own_side], slopes, False, True
    )
    near_own_grad, near_moved, far_moved, query_grad = meet(
        (near_own_grad, near_moved, far_moved, query_grad)
    )

    far_query_grad = grid.send(query_grad[1::2], "z", 0, mirror=True)
    side_grad = rounded(total_of([near_own_grad, near_moved] + far_moved))
    query_grad = jnp.stack(
        [query_grad[m] if m % 2 == 0 else far_query_grad[m // 2] for m in range(GROUPS)]
    )
    dqkv = jnp.concatenate([query_grad.reshape(GROUPS * rows, QUERY), side_grad], axis=1)
    far_tokens_grad = rounded(back_matmul(dqkv[rows:], qkv_weight)).reshape(Z - 1, rows, width)
    dqkv, far_tokens_grad = meet(
        (dqkv, far_tokens_grad), reduce_ffnout, reduce_ffnin, reduce_mid, reduce_late, spread_back
    )
    third = grid.send(far_tokens_grad[2], "l", 1)
    first = grid.send(far_tokens_grad[0], "l", 1)
    grad_group = weight_grad(token_column, dqkv)
    sums = jnp.sum(wide(dqkv), axis=0)
    sums = jnp.stack([jnp.where(is_query, sums, 0.0), jnp.where(is_value, sums, 0.0)])
    sums = jnp.pad(rounded(sums), ((0, QUERY - GROUP_WIDTH - 2), (0, 0)))
    grad_group = jnp.concatenate(
        [grad_group[:, :GROUP_WIDTH], back_matmul(chosen, sums), grad_group[:, QUERY:]], axis=1
    )
    reduce_group = Chain(reduction(sharded(rounded(grad_group)), "cyx", final=False))
    tokens_base = dresid_one + back_matmul(dqkv[:rows], qkv_weight)
    second = grid.send(rounded(total_of([far_tokens_grad[1], third])), "h", 1)
    tokens_base = meet(tokens_base, reduce_group, spread_back, reduce_late)
    tokens_base = meet(tokens_base, reduce_group, spread_back, reduce_mid)
    tokens_base = meet(tokens_base, reduce_group, spread_back, reduce_late)
    pieces = parted(reduce_group.result.reshape(Z, part, PACK), "z", 0)
    tokens_grad = total_of([tokens_base, first, second])
    for chain in (reduce_ffnin, reduce_mid, reduce_late, reduce_late):
        chain.step(chain.pending)

    spot = jnp.arange(grid.seq, dtype=jnp.int32)
    spot_z = my_z ^ (spot % 2 * 2 + spot // 2 % 2)
    source = (spot_z * X + (my_x ^ (spot // Z % X))) * C + (my_c ^ (spot // (Z * X)))
    target = jnp.take(blocks[0], source // per_block) - home
    inside = (target >= 0) & (target < local_blocks)
    places = jnp.where(inside, target * per_block + source % per_block, -1)
    drows = spread_back.result.reshape(grid.seq, chunk, width)
    bank_grad = place_rows(drows, places, local_chunks).reshape(bank.shape[1], width)

    grad_groups = wide(in_order(pieces, my_z))
    sides = grad_groups[:, :, QUERY:]
    out_qkv = jnp.stack(
        [
            grad_groups[:, :, :GROUP_WIDTH],
            jnp.concatenate([sides[:, :, :128], sides[:, :, 256:320]], axis=2),
            jnp.concatenate([sides[:, :, 128:256], sides[:, :, 320:384]], axis=2),
        ]
    )
    out_qkv = out_qkv.transpose(2, 0, 1, 3).reshape(part, 3 * width)
    late_bias = jnp.sum(grad_groups[:, :, GROUP_WIDTH : GROUP_WIDTH + 2], axis=0)

    out_late, out_mid = reduce_late.result, reduce_mid.result
    out_ffnin = (
        reduce_ffnin.result.reshape(part, fan, devices, part)
        .transpose(0, 2, 1, 3)
        .reshape(part, hidden)
    )
    out_small = out_late[:, 2 * width :].T
    bias_grad = jnp.concatenate([out_small[3:6], late_bias.T, out_small[6:15]], axis=0)
    return (
        rounded(output)[None],
        tokens_grad[None],
        bank_grad[None],
        out_qkv,
        out_mid[0],
        out_mid[1],
        out_late[:, : 2 * width],
        out_mid[2],
        out_ffnin,
        reduce_ffnout.result.reshape(fan * part, width),
        out_small[:3],
        bias_grad,
    )


def solution(mesh):
    split = P("batch", "seq", None)
    shard = P(("seq", "batch"), None)
    flat = P(None, ("seq", "batch"))
    return jax.shard_map(
        functools.partial(body, Grid(mesh)),
        mesh=mesh,
        in_specs=(split, split, split, P("batch"), P("batch", None)) + (shard,) * 7 + (flat, flat),
        out_specs=(split, split, split) + (shard,) * 7 + (flat, flat),
        check_vma=False,
    )
```

```python
import functools

import jax
import jax.numpy as jnp
from jax import lax
from jax.experimental import pallas as pl
from jax.experimental.pallas import tpu as pltpu
from jax.sharding import PartitionSpec as P

HEADS = 12
HEAD_DIM = 64
BANK_BLOCK = 128
GROUPS = 4
GROUP_HEADS = HEADS // GROUPS
GROUP_WIDTH = GROUP_HEADS * HEAD_DIM
QUERY, SIDE = 256, 384
PACK = QUERY + SIDE
EPSILON = 1e-05
NEGATIVE = -1e30
SCALE = HEAD_DIM ** (-0.5)
LANES_IN = (((1,), (1,)), ((), ()))
ROWS_IN = (((0,), (0,)), ((), ()))
VMEM_LIMIT = 60 * 1024 * 1024


def layer_norm(values, gain, shift):
    centered = values - jnp.mean(values, axis=-1, keepdims=True)
    variance = jnp.mean(centered * centered, axis=-1, keepdims=True)
    return centered * lax.rsqrt(variance + EPSILON) * gain + shift


def gelu_exact(values):
    return jax.nn.gelu(values, approximate=False)


def rounded(values):
    return values.astype(jnp.bfloat16)


def wide(values):
    return values.astype(jnp.float32)


def matmul(left, right):
    return jnp.dot(left, right, preferred_element_type=jnp.float32)


def weight_grad(left, right):
    return lax.dot_general(left, right, ROWS_IN, preferred_element_type=jnp.float32)


def back_matmul(left, right):
    return lax.dot_general(left, right, LANES_IN, preferred_element_type=jnp.float32)


def column_sums(values):
    return jnp.sum(wide(values), axis=0)


class Grid:
    def __init__(self, mesh):
        self.seq = mesh.shape["seq"]
        self.y = mesh.shape["batch"]
        self.z = GROUPS
        self.c = self.h = self.l = 2
        self.x = self.seq // (self.z * self.c)

    def coords(self, index):
        spot, y = divmod(index, self.y)
        spot, c = divmod(spot, self.c)
        z, x = divmod(spot, self.x)
        return z, x, c, y

    def index(self, z, x, c, y):
        return ((z * self.x + x) * self.c + c) * self.y + y

    def send(self, array, axis, shift, mirror=False):
        if axis in "hl":
            axis, shift = "z", shift * (2 if axis == "h" else 1)
        place = "zxcy".index(axis)
        pairs = []
        for index in range(self.seq * self.y):
            spot = list(self.coords(index))
            spot[place] ^= shift
            if mirror:
                spot[1], spot[2] = self.x - 1 - spot[1], self.c - 1 - spot[2]
            pairs.append((index, self.index(*spot)))
        return lax.ppermute(array, ("seq", "batch"), pairs)


def in_order(pieces, me):
    pieces = list(pieces)
    bit = 1
    while bit < len(pieces):
        swap = (me & bit) != 0
        pieces = [jnp.where(swap, pieces[j ^ bit], piece) for j, piece in enumerate(pieces)]
        bit *= 2
    return jnp.stack(pieces)


def take(array, index, axis):
    return lax.dynamic_index_in_dim(array, index, axis, keepdims=False)


def head_parts(block, scale, third_low):
    lane = lax.broadcasted_iota(jnp.int32, (block.shape[0], 128), 1)
    first = wide(block[:, 0:128]) * scale
    third = wide(block[:, 128:256]) * scale
    third = jnp.where(lane < 64, third, 0.0)
    if not third_low:
        third = pltpu.roll(third, 64, 1)
    return (
        rounded(jnp.where(lane < 64, first, 0.0)),
        rounded(jnp.where(lane >= 64, first, 0.0)),
        rounded(third),
    )


def key_tiles(ref, start, size):
    rows = pl.ds(start, size)
    keys = ref[rows, 0:128]
    values = ref[rows, 128:256]
    third = ref[rows, 256:384]
    return (keys, keys, third), (values, values, third)


def allowed_keys(key_first, query_first, prefix_len, shape):
    key_pos = key_first + lax.broadcasted_iota(jnp.int32, shape, 0)
    query_pos = query_first + lax.broadcasted_iota(jnp.int32, shape, 1)
    return (key_pos <= query_pos) | (key_pos < prefix_len)


def each_block(table, refs, rows, query_first, prefix_len, work):
    count = refs[0].shape[0] // rows
    for part, ref in enumerate(refs):

        def step(local, carry, part=part, ref=ref):
            block = part * count + local
            key_first = table[block]
            last = key_first + rows - 1
            seen = (key_first <= query_first + rows - 1) | (key_first < prefix_len)
            whole = (last <= query_first) | (last < prefix_len)

            @pl.when(seen & whole)
            def _():
                work(ref, local * rows, block, key_first, False)

            @pl.when(seen & jnp.logical_not(whole))
            def _():
                work(ref, local * rows, block, key_first, True)

            return carry

        lax.fori_loop(0, count, step, 0)


def forward_kernel(rows, parts, first, last, table, query_in, *refs):
    refs = list(refs)
    sides = [refs.pop(0) for _ in range(parts)]
    if not first:
        accum_in, stats_in = refs.pop(0), refs.pop(0)
    out, state, query, accum, stats = refs
    m = pl.program_id(0)
    blocks = parts * (sides[0].shape[0] // rows)
    query_first = table[blocks + m]
    prefix_len = table[blocks + GROUPS]
    for head, part in enumerate(head_parts(query_in[0], SCALE, True)):
        query[head] = part
    if first:
        accum[...] = jnp.zeros_like(accum)
        stats[0:8, :] = jnp.full((8, rows), NEGATIVE, jnp.float32)
        stats[8:16, :] = jnp.zeros((8, rows), jnp.float32)
    else:
        accum[...] = accum_in[0]
        stats[...] = stats_in[0]

    def work(ref, start, block, key_first, masked):
        keys, values = key_tiles(ref, start, rows)
        if masked:
            mask = allowed_keys(key_first, query_first, prefix_len, (rows, rows))
        for head in range(GROUP_HEADS):
            scores = lax.dot_general(
                keys[head], query[head], LANES_IN, preferred_element_type=jnp.float32
            )
            if masked:
                scores = jnp.where(mask, scores, NEGATIVE)
            old = stats[head : head + 1, :]
            top = jnp.maximum(old, jnp.max(scores, axis=0, keepdims=True))
            weights = jnp.exp(scores - top)
            shrink = jnp.exp(old - top)
            stats[head : head + 1, :] = top
            stats[8 + head : 9 + head, :] = stats[8 + head : 9 + head, :] * shrink + jnp.sum(
                weights, axis=0, keepdims=True
            )
            accum[head] = accum[head] * shrink + lax.dot_general(
                values[head], rounded(weights), ROWS_IN, preferred_element_type=jnp.float32
            )

    each_block(table, sides, rows, query_first, prefix_len, work)
    if not last:
        out[0] = accum[...]
        state[0] = stats[...]
        return
    totals = stats[8 : 8 + GROUP_HEADS, :]
    final = [accum[head] / totals[head : head + 1, :] for head in range(GROUP_HEADS)]
    line = lax.broadcasted_iota(jnp.int32, (128, rows), 0)
    out[0, :, 0:128] = jnp.where(line < 64, final[0], final[1]).T
    third = jnp.concatenate([final[2][64:128], jnp.zeros((64, rows), jnp.float32)], axis=0)
    out[0, :, 128:256] = third.T
    state[0] = jnp.zeros((8, rows), jnp.float32)
    state[0, 0:GROUP_HEADS, :] = stats[0:GROUP_HEADS, :] + jnp.log(totals)


def backward_kernel(rows, parts, first, last, table, query_in, dout, state, *refs):
    refs = list(refs)
    sides = [refs.pop(0) for _ in range(parts)]
    carried = refs.pop(0)
    grads_out = [refs.pop(0) for _ in range(parts)]
    qgrad_out = refs.pop(0)
    if first:
        state_out = refs.pop(0)
    query, accum, qgrad, lines = refs
    m = pl.program_id(0)
    count = sides[0].shape[0] // rows
    blocks = parts * count
    query_first = table[blocks + m]
    prefix_len = table[blocks + GROUPS]

    @pl.when(m == 0)
    def _():
        def clear(index, carry):
            accum[pl.ds(index * rows, rows), :] = jnp.zeros((rows, SIDE), jnp.float32)
            return carry

        lax.fori_loop(0, blocks, clear, 0)

    for head, part in enumerate(head_parts(query_in[0], SCALE, True)):
        query[head] = part
    for head, part in enumerate(head_parts(dout[0], 1.0, False)):
        query[GROUP_HEADS + head] = part
    lines[...] = state[0]
    if first:
        pair_prod = (wide(dout[0, :, 0:128]) * carried[0, :, 0:128]).T
        third_prod = (wide(dout[0, :, 128:256]) * carried[0, :, 128:256]).T
        lines[3:4, :] = jnp.sum(pair_prod[0:64], axis=0, keepdims=True)
        lines[4:5, :] = jnp.sum(pair_prod[64:128], axis=0, keepdims=True)
        lines[5:6, :] = jnp.sum(third_prod[0:64], axis=0, keepdims=True)
        state_out[0] = lines[...]
        qgrad[...] = jnp.zeros_like(qgrad)
    else:
        qgrad[...] = carried[0]

    def work(ref, start, block, key_first, masked):
        keys, values = key_tiles(ref, start, rows)
        if masked:
            mask = allowed_keys(key_first, query_first, prefix_len, (rows, rows))
        key_parts, value_parts = [], []
        for head in range(GROUP_HEADS):
            scores = lax.dot_general(
                keys[head], query[head], LANES_IN, preferred_element_type=jnp.float32
            )
            if masked:
                scores = jnp.where(mask, scores, NEGATIVE)
            probs = jnp.exp(scores - lines[head : head + 1, :])
            slopes = lax.dot_general(
                values[head],
                query[GROUP_HEADS + head],
                LANES_IN,
                preferred_element_type=jnp.float32,
            )
            low = rounded(probs * (slopes - lines[3 + head : 4 + head, :]))
            value_parts.append(matmul(rounded(probs), query[GROUP_HEADS + head]))
            key_parts.append(matmul(low, query[head]))
            qgrad[head] += lax.dot_general(
                keys[head], low, ROWS_IN, preferred_element_type=jnp.float32
            )
        span = pl.ds(pl.multiple_of(block * rows, rows), rows)
        accum[span, 0:128] += key_parts[0] + key_parts[1]
        accum[span, 128:256] += value_parts[0] + value_parts[1]
        accum[span, 256:384] += key_parts[2] + value_parts[2]

    each_block(table, sides, rows, query_first, prefix_len, work)
    if last:
        line = lax.broadcasted_iota(jnp.int32, (128, rows), 0)
        qgrad_out[0, :, 0:128] = rounded(jnp.where(line < 64, qgrad[0], qgrad[1]).T * SCALE)
        qgrad_out[0, :, 128:256] = rounded(jnp.where(line < 64, qgrad[2], 0.0).T * SCALE)
    else:
        qgrad_out[0] = qgrad[...]

    @pl.when(m == GROUPS - 1)
    def _():
        for part, ref in enumerate(grads_out):

            def write(index, carry, part=part, ref=ref):
                source = pl.ds((part * count + index) * rows, rows)
                ref[pl.ds(index * rows, rows), :] = rounded(accum[source, :])
                return carry

            lax.fori_loop(0, count, write, 0)


def whole(shape):
    return pl.BlockSpec(shape, lambda *_: (0,) * len(shape), pipeline_mode=pl.Buffered(1))


def slab(shape):
    return pl.BlockSpec((1,) + shape, lambda m, *_: (m,) + (0,) * len(shape))


def self_forward(table, queries, sides, carried, last):
    rows = queries.shape[1]
    parts, length = len(sides), sides[0].shape[0]
    pairs = GROUPS * parts * length // rows * GROUP_HEADS // 2
    accum, stats = (GROUP_HEADS, 128, rows), (16, rows)
    outs = [(rows, 256), (8, rows)] if last else [accum, stats]
    first = carried is None
    return pl.pallas_call(
        functools.partial(forward_kernel, rows, parts, first, last),
        grid_spec=pltpu.PrefetchScalarGridSpec(
            num_scalar_prefetch=1,
            grid=(GROUPS,),
            in_specs=[slab((rows, QUERY))]
            + [whole((length, SIDE))] * parts
            + ([] if first else [slab(accum), slab(stats)]),
            out_specs=[slab(shape) for shape in outs],
            scratch_shapes=[
                pltpu.VMEM((GROUP_HEADS, rows, 128), jnp.bfloat16),
                pltpu.VMEM(accum, jnp.float32),
                pltpu.VMEM(stats, jnp.float32),
            ],
        ),
        out_shape=[jax.ShapeDtypeStruct((GROUPS,) + shape, jnp.float32) for shape in outs],
        compiler_params=pltpu.CompilerParams(vmem_limit_bytes=VMEM_LIMIT),
        cost_estimate=pl.CostEstimate(
            flops=pairs * rows * rows * 128 * 16,
            bytes_accessed=4 * length * parts * SIDE,
            transcendentals=pairs * rows * rows,
        ),
        name="self_forward",
    )(table, queries, *sides, *(() if first else carried))


def self_backward(table, queries, dout, state, sides, carried, first, last):
    rows = queries.shape[1]
    parts, length = len(sides), sides[0].shape[0]
    pairs = GROUPS * parts * length // rows * GROUP_HEADS // 2
    slope = (GROUP_HEADS, 128, rows)
    outs = [jax.ShapeDtypeStruct((length, SIDE), jnp.bfloat16)] * parts
    out_specs = [whole((length, SIDE))] * parts
    if last:
        outs = outs + [jax.ShapeDtypeStruct((GROUPS, rows, QUERY), jnp.bfloat16)]
        out_specs = out_specs + [slab((rows, QUERY))]
    else:
        outs = outs + [jax.ShapeDtypeStruct((GROUPS,) + slope, jnp.float32)]
        out_specs = out_specs + [slab(slope)]
    if first:
        outs = outs + [jax.ShapeDtypeStruct((GROUPS, 8, rows), jnp.float32)]
        out_specs = out_specs + [slab((8, rows))]
    return pl.pallas_call(
        functools.partial(backward_kernel, rows, parts, first, last),
        grid_spec=pltpu.PrefetchScalarGridSpec(
            num_scalar_prefetch=1,
            grid=(GROUPS,),
            in_specs=[slab((rows, QUERY)), slab((rows, 256)), slab((8, rows))]
            + [whole((length, SIDE))] * parts
            + [slab((rows, 256)) if first else slab(slope)],
            out_specs=out_specs,
            scratch_shapes=[
                pltpu.VMEM((2 * GROUP_HEADS, rows, 128), jnp.bfloat16),
                pltpu.VMEM((parts * length, SIDE), jnp.float32),
                pltpu.VMEM(slope, jnp.float32),
                pltpu.VMEM((8, rows), jnp.float32),
            ],
        ),
        out_shape=outs,
        compiler_params=pltpu.CompilerParams(vmem_limit_bytes=VMEM_LIMIT),
        cost_estimate=pl.CostEstimate(
            flops=pairs * rows * rows * 128 * 20,
            bytes_accessed=8 * length * parts * SIDE,
            transcendentals=pairs * rows * rows,
        ),
        name="self_backward",
    )(table, queries, dout, state, *sides, carried)


def pair_heads(block, scale=1.0):
    lane = lax.broadcasted_iota(jnp.int32, block.shape, 1)
    values = wide(block) * scale
    return rounded(jnp.where(lane < 64, values, 0.0)), rounded(jnp.where(lane >= 64, values, 0.0))


def cross_forward_kernel(query, keys, values, out, lse):
    rows = query.shape[0]
    parts = pair_heads(query[...], SCALE)
    sides = []
    lse[0] = jnp.zeros((8, rows), jnp.float32)
    for head in range(2):
        scores = lax.dot_general(
            keys[...], parts[head], LANES_IN, preferred_element_type=jnp.float32
        )
        top = jnp.max(scores, axis=0, keepdims=True)
        weights = jnp.exp(scores - top)
        total = jnp.sum(weights, axis=0, keepdims=True)
        mixed = lax.dot_general(
            values[...], rounded(weights), ROWS_IN, preferred_element_type=jnp.float32
        )
        sides.append(mixed / total)
        lse[0, head : head + 1, :] = top + jnp.log(total)
    line = lax.broadcasted_iota(jnp.int32, (128, rows), 0)
    out[...] = rounded(jnp.where(line < 64, sides[0], sides[1]).T)


def cross_backward_kernel(query, keys, values, dout, lse, qgrad, kgrad, vgrad):
    rows = query.shape[0]
    parts = pair_heads(query[...], SCALE)
    grads = pair_heads(dout[...])
    sides, key_parts, value_parts = [], [], []
    for head in range(2):
        scores = lax.dot_general(
            keys[...], parts[head], LANES_IN, preferred_element_type=jnp.float32
        )
        probs = jnp.exp(scores - lse[0, head : head + 1, :])
        slopes = lax.dot_general(
            values[...], grads[head], LANES_IN, preferred_element_type=jnp.float32
        )
        delta = jnp.sum(probs * slopes, axis=0, keepdims=True)
        low = rounded(probs * (slopes - delta))
        value_parts.append(matmul(rounded(probs), grads[head]))
        key_parts.append(matmul(low, parts[head]))
        sides.append(lax.dot_general(keys[...], low, ROWS_IN, preferred_element_type=jnp.float32))
    line = lax.broadcasted_iota(jnp.int32, (128, rows), 0)
    qgrad[...] = rounded(jnp.where(line < 64, sides[0], sides[1]).T * SCALE)
    kgrad[...] = rounded(key_parts[0] + key_parts[1])
    vgrad[...] = rounded(value_parts[0] + value_parts[1])


def cross_forward(query, pair):
    rows, width = query.shape
    count = width // 128
    kept = pair.shape[0]
    return pl.pallas_call(
        cross_forward_kernel,
        grid=(count,),
        in_specs=[
            pl.BlockSpec((rows, 128), lambda i: (0, i)),
            pl.BlockSpec((kept, 128), lambda i: (0, i)),
            pl.BlockSpec((kept, 128), lambda i: (0, count + i)),
        ],
        out_specs=[
            pl.BlockSpec((rows, 128), lambda i: (0, i)),
            pl.BlockSpec((1, 8, rows), lambda i: (i, 0, 0)),
        ],
        out_shape=[
            jax.ShapeDtypeStruct((rows, width), jnp.bfloat16),
            jax.ShapeDtypeStruct((count, 8, rows), jnp.float32),
        ],
        compiler_params=pltpu.CompilerParams(vmem_limit_bytes=VMEM_LIMIT),
        cost_estimate=pl.CostEstimate(
            flops=8 * rows * kept * width, bytes_accessed=4 * kept * width, transcendentals=12 * rows * kept
        ),
        name="cross_forward",
    )(query, pair, pair)


def cross_backward(query, pair, dout, lse):
    rows, width = query.shape
    count = width // 128
    kept = pair.shape[0]
    return pl.pallas_call(
        cross_backward_kernel,
        grid=(count,),
        in_specs=[
            pl.BlockSpec((rows, 128), lambda i: (0, i)),
            pl.BlockSpec((kept, 128), lambda i: (0, i)),
            pl.BlockSpec((kept, 128), lambda i: (0, count + i)),
            pl.BlockSpec((rows, 128), lambda i: (0, i)),
            pl.BlockSpec((1, 8, rows), lambda i: (i, 0, 0)),
        ],
        out_specs=[
            pl.BlockSpec((rows, 128), lambda i: (0, i)),
            pl.BlockSpec((kept, 128), lambda i: (0, i)),
            pl.BlockSpec((kept, 128), lambda i: (0, i)),
        ],
        out_shape=[
            jax.ShapeDtypeStruct((rows, width), jnp.bfloat16),
            jax.ShapeDtypeStruct((kept, width), jnp.bfloat16),
            jax.ShapeDtypeStruct((kept, width), jnp.bfloat16),
        ],
        compiler_params=pltpu.CompilerParams(vmem_limit_bytes=VMEM_LIMIT),
        cost_estimate=pl.CostEstimate(
            flops=20 * rows * kept * width, bytes_accessed=8 * kept * width, transcendentals=12 * rows * kept
        ),
        name="cross_backward",
    )(query, pair, pair, dout, lse)


def pick_kernel(table, bank, out):
    i = pl.program_id(0)
    keep = table[pl.num_programs(0) + i]
    out[0] = jnp.where(keep > 0, bank[0], jnp.zeros_like(bank[0]))


def pick_rows(chunks, spots, found):
    count = spots.shape[0]
    size = chunks.shape[1:]
    table = jnp.concatenate([spots, found.astype(jnp.int32)])
    return pl.pallas_call(
        pick_kernel,
        grid_spec=pltpu.PrefetchScalarGridSpec(
            num_scalar_prefetch=1,
            grid=(count,),
            in_specs=[pl.BlockSpec((1,) + size, lambda i, t: (t[i], 0, 0))],
            out_specs=pl.BlockSpec((1,) + size, lambda i, t: (i, 0, 0)),
        ),
        out_shape=jax.ShapeDtypeStruct((count,) + size, chunks.dtype),
        name="pick_rows",
    )(table, chunks)


def place_kernel(count, table, grads, out):
    spot = pl.program_id(0)
    out[...] = jnp.zeros_like(out)
    for i in range(count):

        @pl.when(table[i] == spot)
        def _(i=i):
            out[0] += wide(grads[i])


def place_rows(grads, spots, chunks):
    count = spots.shape[0]
    size = grads.shape[1:]
    return pl.pallas_call(
        functools.partial(place_kernel, count),
        grid_spec=pltpu.PrefetchScalarGridSpec(
            num_scalar_prefetch=1,
            grid=(chunks,),
            in_specs=[whole((count,) + size)],
            out_specs=pl.BlockSpec((1,) + size, lambda n, t: (n, 0, 0)),
        ),
        out_shape=jax.ShapeDtypeStruct((chunks,) + size, jnp.float32),
        name="place_rows",
    )(spots, grads)


class Chain:
    def __init__(self, stages):
        self.stages = stages
        self.result = None
        self.pending = next(stages)

    def step(self, pending):
        try:
            self.pending = self.stages.send(pending)
        except StopIteration as stop:
            self.pending, self.result = (), stop.value


def meet(values, *chains):
    values, pending = lax.optimization_barrier((values, [chain.pending for chain in chains]))
    for chain, arrays in zip(chains, pending):
        chain.step(arrays)
    return values


def hold(values, *chains):
    values, pending = lax.optimization_barrier((values, [chain.pending for chain in chains]))
    for chain, arrays in zip(chains, pending):
        chain.pending = arrays
    return values


def total_of(arrays):
    total = wide(arrays[0])
    for array in arrays[1:]:
        total = total + wide(array)
    return total


def body(
    grid,
    tokens,
    cotangent,
    bank,
    prefix,
    blocks,
    self_qkv,
    self_out,
    cross_q,
    cross_kv,
    cross_out,
    ffn_in,
    ffn_out,
    gains,
    biases,
):
    Z, X, C, Y = grid.z, grid.x, grid.c, grid.y
    devices = grid.seq * Y
    seq_index = lax.axis_index("seq")
    me = {
        "y": lax.axis_index("batch"),
        "c": seq_index % C,
        "x": (seq_index // C) % X,
        "z": seq_index // (C * X),
        "h": seq_index // (2 * C * X),
        "l": seq_index // (C * X) % 2,
    }
    my_z, my_x, my_c = me["z"], me["x"], me["c"]
    rows, width = tokens.shape[1:]
    hidden = ffn_in.shape[1]
    part = width // devices
    fan = hidden // width
    inputs = tokens[0]

    def parted(array, axis, place):
        size = getattr(grid, axis)
        kept = [take(array, me[axis], place)]
        for shift in range(1, size):
            kept.append(grid.send(take(array, me[axis] ^ shift, place), axis, shift))
        return kept

    def reduction(array, axes, lead=0, final=True):
        names = ["h", "l", "x", "c", "y"]
        for axis in axes:
            place = lead + names.index(axis)
            names.remove(axis)
            arrays = yield parted(array, axis, place)
            total = total_of(arrays)
            array = rounded(total)
        return total if final else array

    def sharded(array):
        return array.reshape(2, 2, X, C, Y, array.shape[0] // devices, array.shape[1])

    grouped = self_qkv.reshape(part, 3, GROUPS, GROUP_WIDTH)
    spare = QUERY - GROUP_WIDTH
    small = jnp.concatenate([gains, biases], axis=0).T
    smalls = small.shape[1]
    extra = jnp.pad(small, ((0, 0), (0, spare - smalls)))
    extra = jnp.broadcast_to(extra[:, None], (part, GROUPS, spare))
    packed = jnp.concatenate(
        [
            grouped[:, 0],
            extra,
            grouped[:, 1, :, :128],
            grouped[:, 2, :, :128],
            grouped[:, 1, :, 128:],
            grouped[:, 2, :, 128:],
        ],
        axis=2,
    ).transpose(1, 0, 2)
    pieces = parted(packed, "z", 0)

    both = 2 * width
    halves = hidden // both
    planes = jnp.concatenate(
        [
            ffn_in.reshape(part, devices, halves, 2, part)
            .transpose(2, 0, 3, 1, 4)
            .reshape(halves, part, both),
            ffn_out.reshape(halves, 2, part, width).transpose(0, 2, 1, 3).reshape(halves, part, both),
            jnp.concatenate([self_out, cross_q], axis=1)[None],
            jnp.pad(cross_out, ((0, 0), (0, width)))[None],
            cross_kv[None],
        ]
    )
    planes = lax.all_gather(planes, ("seq", "batch"), axis=1, tiled=True)

    pieces, inputs = lax.optimization_barrier((pieces, inputs))
    across = grid.send(inputs, "h", 1)
    beside = grid.send(inputs, "l", 1)

    chunk = BANK_BLOCK * blocks.shape[1] // grid.seq
    per_block = BANK_BLOCK // chunk
    local_chunks = bank.shape[1] // chunk
    local_blocks = bank.shape[1] // BANK_BLOCK
    bank_chunks = bank[0].reshape(local_chunks, chunk, width)
    home = seq_index * local_blocks
    every = jnp.arange(grid.seq, dtype=jnp.int32)
    wanted = jnp.take(blocks[0], every // per_block) - home
    found = (wanted >= 0) & (wanted < local_blocks)
    spots = jnp.where(found, wanted * per_block + every % per_block, 0)
    picked = pick_rows(bank_chunks, spots, found).reshape(2, 2, X, C, 1, chunk, width)

    def spreading(own):
        array = own
        for axis in "hlxc":
            size = getattr(grid, axis)
            array = jnp.stack((yield [array] + [grid.send(array, axis, m) for m in range(1, size)]))
        return array

    def retrieval():
        own = (yield from reduction(picked, "cxlh", final=False))[0]
        every_row = yield from spreading(own)
        return own, every_row.reshape(grid.seq * chunk, width)

    retrieve = Chain(retrieval())
    gathered = in_order(pieces, my_z)
    for axis in "yxc":
        pieces = [gathered] + [grid.send(gathered, axis, m) for m in range(1, getattr(grid, axis))]
        if axis == "y":
            pieces, across = meet((pieces, across), retrieve)
        gathered = in_order(pieces, me[axis])
    token_parts = [inputs, beside, across, grid.send(across, "l", 1)]
    qkv_group = gathered.transpose(3, 1, 0, 2, 4, 5).reshape(width, PACK)
    column = jnp.arange(PACK, dtype=jnp.int32)
    real = (column < GROUP_WIDTH) | (column >= QUERY)
    is_query = column < GROUP_WIDTH
    is_pair_value = (column >= QUERY + 128) & (column < QUERY + 256)
    is_value = is_pair_value | (column >= QUERY + 320)
    local = jnp.where(is_query, column, column - jnp.where(is_pair_value, QUERY + 128, QUERY + 192))
    line = jnp.where(is_query | is_value, local + my_z * GROUP_WIDTH, -1)
    chosen = (jnp.arange(width, dtype=jnp.int32)[:, None] == line[None]).astype(jnp.bfloat16)
    picked_bias = weight_grad(qkv_group[:, GROUP_WIDTH:QUERY], chosen)
    qkv_bias = jnp.where(is_query, picked_bias[3 + 3], picked_bias[3 + 4])
    qkv_weight = jnp.where(real[None], qkv_group, jnp.zeros_like(qkv_group))

    qkv_weight, qkv_bias, token_parts = meet((qkv_weight, qkv_bias, token_parts), retrieve)

    token_column = jnp.concatenate(token_parts, axis=0)
    own_queries = rounded(matmul(token_column, qkv_weight[:, :QUERY]) + qkv_bias[:QUERY])
    own_side = rounded(matmul(token_column, qkv_weight[:, QUERY:]) + qkv_bias[QUERY:])
    own_queries = own_queries.reshape(GROUPS, rows, QUERY)

    far_queries = grid.send(own_queries[1::2], "z", 0, mirror=True)
    near_other = grid.send(own_side, "c", 1)
    far_queries, side = lax.optimization_barrier((far_queries, own_side))
    far_own = [grid.send(side, "x", m) for m in range(1, X)]
    queries = jnp.stack(
        [own_queries[m] if m % 2 == 0 else far_queries[m // 2] for m in range(GROUPS)]
    )

    turn = jnp.arange(GROUPS, dtype=jnp.int32)
    turn_z = my_z ^ turn

    def key_firsts(x, c):
        return ((turn_z * X + x) * C + c) * rows

    query_firsts = jnp.where(
        turn % 2 == 0, key_firsts(my_x, my_c), key_firsts(X - 1 - my_x, C - 1 - my_c)
    )

    def table_of(shifts, c):
        keys = [key_firsts(my_x ^ m, c) for m in shifts]
        return jnp.concatenate(keys + [query_firsts, prefix]).astype(jnp.int32)

    far = list(range(1, X))
    tables = {
        "near own": table_of([0], my_c),
        "near other": table_of([0], C - 1 - my_c),
        "far own": table_of(far, my_c),
        "far other": table_of(far, C - 1 - my_c),
    }

    carry = self_forward(tables["near own"], queries, [own_side], None, False)
    carry, near_other = meet((carry, near_other), retrieve)
    carry = self_forward(tables["near other"], queries, [near_other], carry, False)
    carry, far_own = meet((carry, far_own), retrieve)
    far_other = [grid.send(side, "c", 1) for side in far_own]
    carry = self_forward(tables["far own"], queries, far_own, carry, False)
    carry, far_other = meet((carry, far_other), retrieve)
    attention, lse = self_forward(tables["far other"], queries, far_other, carry, True)
    attention, lse = meet((attention, lse), retrieve)
    attention_mine = rounded(attention)

    def swapped(array, m):
        return grid.send(array, "z", m, mirror=m % 2 == 1)

    pieces = [attention_mine[0]] + [swapped(attention_mine[m], m) for m in range(1, Z)]
    pieces = meet(pieces, retrieve)
    retrieve.step(retrieve.pending)
    own_rows, all_rows = retrieve.result
    attention_low = (
        in_order(pieces, my_z)[:, :, :GROUP_WIDTH].transpose(1, 0, 2).reshape(rows, width)
    )

    ffnin_full = [planes[k] for k in range(halves)]
    outer = [
        [planes[halves + k, :, j * width : (j + 1) * width] for j in range(2)] for k in range(halves)
    ]
    selfout_full = planes[2 * halves, :, :width]
    crossq_full = planes[2 * halves, :, width:]
    crossout_full = planes[2 * halves + 1, :, :width]
    crosskv_full = planes[2 * halves + 2]
    small_full = wide(qkv_group[:, GROUP_WIDTH : GROUP_WIDTH + smalls].T)
    gain = small_full[:3]
    bias = small_full[3:]
    inner_bias = bias[10:14].reshape(devices, fan, part).transpose(1, 0, 2).reshape(halves, both)

    resid_one = wide(inputs) + matmul(attention_low, selfout_full) + bias[5]
    hidden_one = layer_norm(resid_one, gain[0], bias[0])
    hidden_one_low = rounded(hidden_one)
    cross_query = rounded(matmul(hidden_one_low, crossq_full) + bias[6])
    cross_pair = rounded(
        matmul(all_rows, crosskv_full) + jnp.concatenate([jnp.zeros((width,), jnp.float32), bias[7]])
    )
    cross_att, cross_lse = cross_forward(cross_query, cross_pair)
    resid_two = hidden_one + matmul(cross_att, crossout_full) + bias[8]
    hidden_two = layer_norm(resid_two, gain[1], bias[1])
    hidden_two_low = rounded(hidden_two)
    inner = [matmul(hidden_two_low, plane) + inner_bias[k] for k, plane in enumerate(ffnin_full)]
    activated = [rounded(gelu_exact(values)) for values in inner]
    resid_three = hidden_two + bias[9]
    for values, sides in zip(activated, outer):
        for j, plane in enumerate(sides):
            resid_three = resid_three + matmul(values[:, j * width : (j + 1) * width], plane)
    output = layer_norm(resid_three, gain[2], bias[2])

    _unused, norm_three = jax.vjp(layer_norm, resid_three, gain[2], bias[2])
    dresid_three, dgain_three, dshift_three = norm_three(wide(cotangent[0]))
    douter_low = rounded(dresid_three)
    grad_ffnout = jnp.stack([rounded(weight_grad(values, douter_low)) for values in activated])
    reduce_ffnout = Chain(
        reduction(grad_ffnout.reshape(fan, 2, 2, X, C, Y, part, width), "cyxlh", lead=1)
    )
    dinner_low = []
    for values, sides in zip(inner, outer):
        _unused, gelu_back = jax.vjp(gelu_exact, values)
        slopes = jnp.concatenate([back_matmul(douter_low, plane) for plane in sides], axis=1)
        dinner_low.append(rounded(gelu_back(slopes)[0]))
    grad_ffnin = jnp.stack([rounded(weight_grad(hidden_two_low, values)) for values in dinner_low])
    reduce_ffnin = Chain(
        reduction(grad_ffnin.reshape(halves, 2, 2, X, C, Y, part, both), "cxylh", lead=1)
    )

    _unused, norm_two = jax.vjp(layer_norm, resid_two, gain[1], bias[1])
    dresid_two, dgain_two, dshift_two = norm_two(
        sum((back_matmul(*pair) for pair in zip(dinner_low, ffnin_full)), dresid_three)
    )
    dcross_low = rounded(dresid_two)
    dcross_att = rounded(back_matmul(dcross_low, crossout_full))
    dcross_query, dcross_key, dcross_value = cross_backward(
        cross_query, cross_pair, dcross_att, cross_lse
    )
    dcross_query, dcross_key, dcross_value = meet(
        (dcross_query, dcross_key, dcross_value), reduce_ffnout, reduce_ffnin
    )

    dcross_all = jnp.concatenate([dcross_key, dcross_value], axis=1)
    dcross_all = dcross_all.reshape(C, X, 2, 2, chunk, 2 * width)

    def unspreading(array):
        for axis in "cxlh":
            size = getattr(grid, axis)
            arrays = yield [array[0]] + [grid.send(array[m], axis, m) for m in range(1, size)]
            array = rounded(total_of(arrays))
        return array

    unspread = Chain(unspreading(dcross_all))

    _unused, norm_one = jax.vjp(layer_norm, resid_one, gain[0], bias[0])
    dresid_one, dgain_one, dshift_one = norm_one(dresid_two + back_matmul(dcross_query, crossq_full))
    dbranch_low = rounded(dresid_one)
    datt_low = rounded(back_matmul(dbranch_low, selfout_full))
    datt_groups = jnp.pad(
        datt_low.reshape(rows, GROUPS, GROUP_WIDTH).transpose(1, 0, 2),
        ((0, 0), (0, 0), (0, 256 - GROUP_WIDTH)),
    )
    pieces = [take(datt_groups, my_z, 0)]
    for m in range(1, Z):
        pieces.append(swapped(take(datt_groups, my_z ^ m, 0), m))
    grad_mid = jnp.stack(
        [
            rounded(weight_grad(attention_low, dbranch_low)),
            rounded(weight_grad(hidden_one_low, dcross_query)),
            rounded(weight_grad(cross_att, dcross_low)),
        ]
    )
    grad_mid, pieces = meet((grad_mid, pieces), unspread)
    reduce_mid = Chain(reduction(grad_mid.reshape(3, 2, 2, X, C, Y, part, width), "cyxlh", lead=1))
    dout = jnp.stack(pieces)

    *far_other_grad, slopes, state = self_backward(
        tables["far other"], queries, dout, lse, far_other, attention, True, False
    )
    far_other_grad, slopes = meet(
        (far_other_grad, slopes), reduce_ffnout, reduce_mid, unspread
    )
    far_moved = [grid.send(grad, "c", 1) for grad in far_other_grad]
    *far_own_grad, slopes = self_backward(
        tables["far own"], queries, dout, state, far_own, slopes, False, False
    )
    far_own_grad, far_moved, slopes = meet(
        (far_own_grad, far_moved, slopes), unspread, reduce_ffnout, reduce_ffnin
    )
    far_grad = [rounded(total_of(pair)) for pair in zip(far_own_grad, far_moved)]
    far_moved = [grid.send(grad, "x", m) for m, grad in zip(far, far_grad)]
    near_other_grad, slopes = self_backward(
        tables["near other"], queries, dout, state, [near_other], slopes, False, False
    )
    near_other_grad, far_moved, slopes = meet(
        (near_other_grad, far_moved, slopes), unspread, reduce_ffnin, reduce_mid
    )
    near_moved = grid.send(near_other_grad, "c", 1)

    dcross_pair = unspread.result
    bias_rows = jnp.stack(
        [
            dgain_one,
            dgain_two,
            dgain_three,
            dshift_one,
            dshift_two,
            dshift_three,
            column_sums(dbranch_low),
            column_sums(dcross_query),
            column_sums(dcross_pair[:, width:]),
            column_sums(dcross_low),
            column_sums(douter_low),
        ]
    )
    inner_sums = jnp.concatenate([column_sums(values) for values in dinner_low])
    inner_sums = inner_sums.reshape(fan, devices, part).transpose(1, 0, 2)
    bias_rows = jnp.concatenate([bias_rows, inner_sums.reshape(fan, width)], axis=0)
    bias_columns = jnp.pad(rounded(bias_rows.T), ((0, 0), (0, 128 - bias_rows.shape[0])))
    grad_late = jnp.concatenate([rounded(weight_grad(own_rows, dcross_pair)), bias_columns], axis=1)
    reduce_late = Chain(reduction(sharded(grad_late), "cyxlh"))
    spread_back = Chain(spreading(rounded(back_matmul(dcross_pair, crosskv_full))))

    near_own_grad, query_grad = self_backward(
        tables["near own"], queries, dout, state, [own_side], slopes, False, True
    )
    near_own_grad, near_moved, query_grad = hold(
        (near_own_grad, near_moved, query_grad), reduce_late, spread_back, reduce_ffnin, reduce_mid
    )

    far_query_grad = grid.send(query_grad[1::2], "z", 0, mirror=True)
    side_grad = rounded(total_of([near_own_grad, near_moved] + far_moved))
    query_grad = jnp.stack(
        [query_grad[m] if m % 2 == 0 else far_query_grad[m // 2] for m in range(GROUPS)]
    )
    dqkv = jnp.concatenate([query_grad.reshape(GROUPS * rows, QUERY), side_grad], axis=1)
    far_tokens_grad = rounded(back_matmul(dqkv[rows:], qkv_weight)).reshape(Z - 1, rows, width)
    dqkv, far_tokens_grad = meet(
        (dqkv, far_tokens_grad), reduce_ffnout, reduce_ffnin, reduce_mid, reduce_late, spread_back
    )
    third = grid.send(far_tokens_grad[2], "l", 1)
    first = grid.send(far_tokens_grad[0], "l", 1)
    grad_group = weight_grad(token_column, dqkv)
    sums = jnp.sum(wide(dqkv), axis=0)
    sums = jnp.stack([jnp.where(is_query, sums, 0.0), jnp.where(is_value, sums, 0.0)])
    sums = jnp.pad(rounded(sums), ((0, spare - 2), (0, 0)))
    grad_group = jnp.concatenate(
        [grad_group[:, :GROUP_WIDTH], back_matmul(chosen, sums), grad_group[:, QUERY:]], axis=1
    )
    reduce_group = Chain(reduction(sharded(rounded(grad_group)), "cyx", final=False))
    tokens_base = dresid_one + back_matmul(dqkv[:rows], qkv_weight)
    tokens_base, third = meet((tokens_base, third), reduce_group, spread_back, reduce_late)
    second = grid.send(rounded(total_of([far_tokens_grad[1], third])), "h", 1)
    tokens_base = meet(tokens_base, reduce_group, spread_back, reduce_late, reduce_mid)
    tokens_base = meet(tokens_base, reduce_group, spread_back, reduce_ffnin)
    pieces = parted(reduce_group.result.reshape(Z, part, PACK), "z", 0)
    tokens_grad = total_of([tokens_base, first, second])
    for chain in (reduce_ffnout, reduce_mid, reduce_late, reduce_late):
        chain.step(chain.pending)

    spot = jnp.arange(grid.seq, dtype=jnp.int32)
    spot_z = my_z ^ (spot % 2 * 2 + spot // 2 % 2)
    source = (spot_z * X + (my_x ^ (spot // Z % X))) * C + (my_c ^ (spot // (Z * X)))
    target = jnp.take(blocks[0], source // per_block) - home
    inside = (target >= 0) & (target < local_blocks)
    places = jnp.where(inside, target * per_block + source % per_block, -1)
    drows = spread_back.result.reshape(grid.seq, chunk, width)
    bank_grad = place_rows(drows, places, local_chunks).reshape(bank.shape[1], width)

    grad_groups = wide(in_order(pieces, my_z))
    sides = grad_groups[:, :, QUERY:]
    out_qkv = jnp.stack(
        [
            grad_groups[:, :, :GROUP_WIDTH],
            jnp.concatenate([sides[:, :, :128], sides[:, :, 256:320]], axis=2),
            jnp.concatenate([sides[:, :, 128:256], sides[:, :, 320:384]], axis=2),
        ]
    )
    out_qkv = out_qkv.transpose(2, 0, 1, 3).reshape(part, 3 * width)
    late_bias = jnp.sum(grad_groups[:, :, GROUP_WIDTH : GROUP_WIDTH + 2], axis=0)

    out_late, out_mid = reduce_late.result, reduce_mid.result
    out_ffnin = (
        reduce_ffnin.result.reshape(halves, part, 2, devices, part)
        .transpose(1, 3, 0, 2, 4)
        .reshape(part, hidden)
    )
    out_small = out_late[:, 2 * width :].T
    bias_grad = jnp.concatenate([out_small[3:6], late_bias.T, out_small[6:15]], axis=0)
    return (
        rounded(output)[None],
        tokens_grad[None],
        bank_grad[None],
        out_qkv,
        out_mid[0],
        out_mid[1],
        out_late[:, : 2 * width],
        out_mid[2],
        out_ffnin,
        reduce_ffnout.result.reshape(fan * part, width),
        out_small[:3],
        bias_grad,
    )


def solution(mesh):
    split = P("batch", "seq", None)
    shard = P(("seq", "batch"), None)
    flat = P(None, ("seq", "batch"))
    return jax.shard_map(
        functools.partial(body, Grid(mesh)),
        mesh=mesh,
        in_specs=(split, split, split, P("batch"), P("batch", None)) + (shard,) * 7 + (flat, flat),
        out_specs=(split, split, split) + (shard,) * 7 + (flat, flat),
        check_vma=False,
    )
```

```python
import functools

import jax
import jax.numpy as jnp
from jax import lax
from jax.experimental import pallas as pl
from jax.experimental.pallas import tpu as pltpu
from jax.sharding import PartitionSpec as P

HEADS = 12
HEAD_DIM = 64
BANK_BLOCK = 128
GROUPS = 4
GROUP_HEADS = HEADS // GROUPS
GROUP_WIDTH = GROUP_HEADS * HEAD_DIM
QUERY, SIDE = 256, 384
PACK = QUERY + SIDE
EPSILON = 1e-05
NEGATIVE = -1e30
SCALE = HEAD_DIM ** (-0.5)
LANES_IN = (((1,), (1,)), ((), ()))
ROWS_IN = (((0,), (0,)), ((), ()))
VMEM_LIMIT = 60 * 1024 * 1024


def layer_norm(values, gain, shift):
    centered = values - jnp.mean(values, axis=-1, keepdims=True)
    variance = jnp.mean(centered * centered, axis=-1, keepdims=True)
    return centered * lax.rsqrt(variance + EPSILON) * gain + shift


def gelu_exact(values):
    return jax.nn.gelu(values, approximate=False)


def rounded(values):
    return values.astype(jnp.bfloat16)


def wide(values):
    return values.astype(jnp.float32)


def matmul(left, right):
    return jnp.dot(left, right, preferred_element_type=jnp.float32)


def weight_grad(left, right):
    return lax.dot_general(left, right, ROWS_IN, preferred_element_type=jnp.float32)


def back_matmul(left, right):
    return lax.dot_general(left, right, LANES_IN, preferred_element_type=jnp.float32)


def column_sums(values):
    return jnp.sum(wide(values), axis=0)


class Grid:
    def __init__(self, mesh):
        self.seq = mesh.shape["seq"]
        self.y = mesh.shape["batch"]
        self.z = GROUPS
        self.c = self.h = self.l = 2
        self.x = self.seq // (self.z * self.c)

    def coords(self, index):
        spot, y = divmod(index, self.y)
        spot, c = divmod(spot, self.c)
        z, x = divmod(spot, self.x)
        return z, x, c, y

    def index(self, z, x, c, y):
        return ((z * self.x + x) * self.c + c) * self.y + y

    def send(self, array, axis, shift, mirror=False):
        if axis in "hl":
            axis, shift = "z", shift * (2 if axis == "h" else 1)
        place = "zxcy".index(axis)
        pairs = []
        for index in range(self.seq * self.y):
            spot = list(self.coords(index))
            spot[place] ^= shift
            if mirror:
                spot[1], spot[2] = self.x - 1 - spot[1], self.c - 1 - spot[2]
            pairs.append((index, self.index(*spot)))
        return lax.ppermute(array, ("seq", "batch"), pairs)


def in_order(pieces, me):
    pieces = list(pieces)
    bit = 1
    while bit < len(pieces):
        swap = (me & bit) != 0
        pieces = [jnp.where(swap, pieces[j ^ bit], piece) for j, piece in enumerate(pieces)]
        bit *= 2
    return jnp.stack(pieces)


def take(array, index, axis):
    return lax.dynamic_index_in_dim(array, index, axis, keepdims=False)


def head_parts(block, scale, third_low):
    lane = lax.broadcasted_iota(jnp.int32, (block.shape[0], 128), 1)
    first = wide(block[:, 0:128]) * scale
    third = wide(block[:, 128:256]) * scale
    third = jnp.where(lane < 64, third, 0.0)
    if not third_low:
        third = pltpu.roll(third, 64, 1)
    return (
        rounded(jnp.where(lane < 64, first, 0.0)),
        rounded(jnp.where(lane >= 64, first, 0.0)),
        rounded(third),
    )


def key_tiles(ref, start, size):
    rows = pl.ds(start, size)
    keys = ref[rows, 0:128]
    values = ref[rows, 128:256]
    third = ref[rows, 256:384]
    return (keys, keys, third), (values, values, third)


def allowed_keys(key_first, query_first, prefix_len, shape):
    key_pos = key_first + lax.broadcasted_iota(jnp.int32, shape, 0)
    query_pos = query_first + lax.broadcasted_iota(jnp.int32, shape, 1)
    return (key_pos <= query_pos) | (key_pos < prefix_len)


def each_block(table, refs, rows, query_first, prefix_len, work):
    count = refs[0].shape[0] // rows
    for part, ref in enumerate(refs):

        def step(local, carry, part=part, ref=ref):
            block = part * count + local
            key_first = table[block]
            last = key_first + rows - 1
            seen = (key_first <= query_first + rows - 1) | (key_first < prefix_len)
            whole = (last <= query_first) | (last < prefix_len)

            @pl.when(seen & whole)
            def _():
                work(ref, local * rows, block, key_first, False)

            @pl.when(seen & jnp.logical_not(whole))
            def _():
                work(ref, local * rows, block, key_first, True)

            return carry

        lax.fori_loop(0, count, step, 0)


def forward_kernel(rows, parts, first, last, table, query_in, *refs):
    refs = list(refs)
    sides = [refs.pop(0) for _ in range(parts)]
    if not first:
        accum_in, stats_in = refs.pop(0), refs.pop(0)
    out, state, query, accum, stats = refs
    m = pl.program_id(0)
    blocks = parts * (sides[0].shape[0] // rows)
    query_first = table[blocks + m]
    prefix_len = table[blocks + GROUPS]
    for head, part in enumerate(head_parts(query_in[0], SCALE, True)):
        query[head] = part
    if first:
        accum[...] = jnp.zeros_like(accum)
        stats[0:8, :] = jnp.full((8, rows), NEGATIVE, jnp.float32)
        stats[8:16, :] = jnp.zeros((8, rows), jnp.float32)
    else:
        accum[...] = accum_in[0]
        stats[...] = stats_in[0]

    def work(ref, start, block, key_first, masked):
        keys, values = key_tiles(ref, start, rows)
        if masked:
            mask = allowed_keys(key_first, query_first, prefix_len, (rows, rows))
        for head in range(GROUP_HEADS):
            scores = lax.dot_general(
                keys[head], query[head], LANES_IN, preferred_element_type=jnp.float32
            )
            if masked:
                scores = jnp.where(mask, scores, NEGATIVE)
            old = stats[head : head + 1, :]
            top = jnp.maximum(old, jnp.max(scores, axis=0, keepdims=True))
            weights = jnp.exp(scores - top)
            shrink = jnp.exp(old - top)
            stats[head : head + 1, :] = top
            stats[8 + head : 9 + head, :] = stats[8 + head : 9 + head, :] * shrink + jnp.sum(
                weights, axis=0, keepdims=True
            )
            accum[head] = accum[head] * shrink + lax.dot_general(
                values[head], rounded(weights), ROWS_IN, preferred_element_type=jnp.float32
            )

    each_block(table, sides, rows, query_first, prefix_len, work)
    if not last:
        out[0] = accum[...]
        state[0] = stats[...]
        return
    totals = stats[8 : 8 + GROUP_HEADS, :]
    final = [accum[head] / totals[head : head + 1, :] for head in range(GROUP_HEADS)]
    line = lax.broadcasted_iota(jnp.int32, (128, rows), 0)
    out[0, :, 0:128] = jnp.where(line < 64, final[0], final[1]).T
    third = jnp.concatenate([final[2][64:128], jnp.zeros((64, rows), jnp.float32)], axis=0)
    out[0, :, 128:256] = third.T
    state[0] = jnp.zeros((8, rows), jnp.float32)
    state[0, 0:GROUP_HEADS, :] = stats[0:GROUP_HEADS, :] + jnp.log(totals)


def backward_kernel(rows, parts, first, last, table, query_in, dout, state, *refs):
    refs = list(refs)
    sides = [refs.pop(0) for _ in range(parts)]
    carried = refs.pop(0)
    grads_out = [refs.pop(0) for _ in range(parts)]
    qgrad_out = refs.pop(0)
    if first:
        state_out = refs.pop(0)
    query, accum, qgrad, lines = refs
    m = pl.program_id(0)
    count = sides[0].shape[0] // rows
    blocks = parts * count
    query_first = table[blocks + m]
    prefix_len = table[blocks + GROUPS]

    @pl.when(m == 0)
    def _():
        def clear(index, carry):
            accum[pl.ds(index * rows, rows), :] = jnp.zeros((rows, SIDE), jnp.float32)
            return carry

        lax.fori_loop(0, blocks, clear, 0)

    for head, part in enumerate(head_parts(query_in[0], SCALE, True)):
        query[head] = part
    for head, part in enumerate(head_parts(dout[0], 1.0, False)):
        query[GROUP_HEADS + head] = part
    lines[...] = state[0]
    if first:
        pair_prod = (wide(dout[0, :, 0:128]) * carried[0, :, 0:128]).T
        third_prod = (wide(dout[0, :, 128:256]) * carried[0, :, 128:256]).T
        lines[3:4, :] = jnp.sum(pair_prod[0:64], axis=0, keepdims=True)
        lines[4:5, :] = jnp.sum(pair_prod[64:128], axis=0, keepdims=True)
        lines[5:6, :] = jnp.sum(third_prod[0:64], axis=0, keepdims=True)
        state_out[0] = lines[...]
        qgrad[...] = jnp.zeros_like(qgrad)
    else:
        qgrad[...] = carried[0]

    def work(ref, start, block, key_first, masked):
        keys, values = key_tiles(ref, start, rows)
        if masked:
            mask = allowed_keys(key_first, query_first, prefix_len, (rows, rows))
        key_parts, value_parts = [], []
        for head in range(GROUP_HEADS):
            scores = lax.dot_general(
                keys[head], query[head], LANES_IN, preferred_element_type=jnp.float32
            )
            if masked:
                scores = jnp.where(mask, scores, NEGATIVE)
            probs = jnp.exp(scores - lines[head : head + 1, :])
            slopes = lax.dot_general(
                values[head],
                query[GROUP_HEADS + head],
                LANES_IN,
                preferred_element_type=jnp.float32,
            )
            low = rounded(probs * (slopes - lines[3 + head : 4 + head, :]))
            value_parts.append(matmul(rounded(probs), query[GROUP_HEADS + head]))
            key_parts.append(matmul(low, query[head]))
            qgrad[head] += lax.dot_general(
                keys[head], low, ROWS_IN, preferred_element_type=jnp.float32
            )
        span = pl.ds(pl.multiple_of(block * rows, rows), rows)
        accum[span, 0:128] += key_parts[0] + key_parts[1]
        accum[span, 128:256] += value_parts[0] + value_parts[1]
        accum[span, 256:384] += key_parts[2] + value_parts[2]

    each_block(table, sides, rows, query_first, prefix_len, work)
    if last:
        line = lax.broadcasted_iota(jnp.int32, (128, rows), 0)
        qgrad_out[0, :, 0:128] = rounded(jnp.where(line < 64, qgrad[0], qgrad[1]).T * SCALE)
        qgrad_out[0, :, 128:256] = rounded(jnp.where(line < 64, qgrad[2], 0.0).T * SCALE)
    else:
        qgrad_out[0] = qgrad[...]

    @pl.when(m == GROUPS - 1)
    def _():
        for part, ref in enumerate(grads_out):

            def write(index, carry, part=part, ref=ref):
                source = pl.ds((part * count + index) * rows, rows)
                ref[pl.ds(index * rows, rows), :] = rounded(accum[source, :])
                return carry

            lax.fori_loop(0, count, write, 0)


def whole(shape):
    return pl.BlockSpec(shape, lambda *_: (0,) * len(shape), pipeline_mode=pl.Buffered(1))


def slab(shape):
    return pl.BlockSpec((1,) + shape, lambda m, *_: (m,) + (0,) * len(shape))


def self_forward(table, queries, sides, carried, last):
    rows = queries.shape[1]
    parts, length = len(sides), sides[0].shape[0]
    pairs = GROUPS * parts * length // rows * GROUP_HEADS // 2
    accum, stats = (GROUP_HEADS, 128, rows), (16, rows)
    outs = [(rows, 256), (8, rows)] if last else [accum, stats]
    first = carried is None
    return pl.pallas_call(
        functools.partial(forward_kernel, rows, parts, first, last),
        grid_spec=pltpu.PrefetchScalarGridSpec(
            num_scalar_prefetch=1,
            grid=(GROUPS,),
            in_specs=[slab((rows, QUERY))]
            + [whole((length, SIDE))] * parts
            + ([] if first else [slab(accum), slab(stats)]),
            out_specs=[slab(shape) for shape in outs],
            scratch_shapes=[
                pltpu.VMEM((GROUP_HEADS, rows, 128), jnp.bfloat16),
                pltpu.VMEM(accum, jnp.float32),
                pltpu.VMEM(stats, jnp.float32),
            ],
        ),
        out_shape=[jax.ShapeDtypeStruct((GROUPS,) + shape, jnp.float32) for shape in outs],
        compiler_params=pltpu.CompilerParams(vmem_limit_bytes=VMEM_LIMIT),
        cost_estimate=pl.CostEstimate(
            flops=pairs * rows * rows * 128 * 16,
            bytes_accessed=4 * length * parts * SIDE,
            transcendentals=pairs * rows * rows,
        ),
        name="self_forward",
    )(table, queries, *sides, *(() if first else carried))


def self_backward(table, queries, dout, state, sides, carried, first, last):
    rows = queries.shape[1]
    parts, length = len(sides), sides[0].shape[0]
    pairs = GROUPS * parts * length // rows * GROUP_HEADS // 2
    slope = (GROUP_HEADS, 128, rows)
    outs = [jax.ShapeDtypeStruct((length, SIDE), jnp.bfloat16)] * parts
    out_specs = [whole((length, SIDE))] * parts
    if last:
        outs = outs + [jax.ShapeDtypeStruct((GROUPS, rows, QUERY), jnp.bfloat16)]
        out_specs = out_specs + [slab((rows, QUERY))]
    else:
        outs = outs + [jax.ShapeDtypeStruct((GROUPS,) + slope, jnp.float32)]
        out_specs = out_specs + [slab(slope)]
    if first:
        outs = outs + [jax.ShapeDtypeStruct((GROUPS, 8, rows), jnp.float32)]
        out_specs = out_specs + [slab((8, rows))]
    return pl.pallas_call(
        functools.partial(backward_kernel, rows, parts, first, last),
        grid_spec=pltpu.PrefetchScalarGridSpec(
            num_scalar_prefetch=1,
            grid=(GROUPS,),
            in_specs=[slab((rows, QUERY)), slab((rows, 256)), slab((8, rows))]
            + [whole((length, SIDE))] * parts
            + [slab((rows, 256)) if first else slab(slope)],
            out_specs=out_specs,
            scratch_shapes=[
                pltpu.VMEM((2 * GROUP_HEADS, rows, 128), jnp.bfloat16),
                pltpu.VMEM((parts * length, SIDE), jnp.float32),
                pltpu.VMEM(slope, jnp.float32),
                pltpu.VMEM((8, rows), jnp.float32),
            ],
        ),
        out_shape=outs,
        compiler_params=pltpu.CompilerParams(vmem_limit_bytes=VMEM_LIMIT),
        cost_estimate=pl.CostEstimate(
            flops=pairs * rows * rows * 128 * 20,
            bytes_accessed=8 * length * parts * SIDE,
            transcendentals=pairs * rows * rows,
        ),
        name="self_backward",
    )(table, queries, dout, state, *sides, carried)


def pair_heads(block, scale=1.0):
    lane = lax.broadcasted_iota(jnp.int32, block.shape, 1)
    values = wide(block) * scale
    return rounded(jnp.where(lane < 64, values, 0.0)), rounded(jnp.where(lane >= 64, values, 0.0))


def cross_forward_kernel(query, keys, values, out, lse):
    rows = query.shape[0]
    parts = pair_heads(query[...], SCALE)
    sides = []
    lse[0] = jnp.zeros((8, rows), jnp.float32)
    for head in range(2):
        scores = lax.dot_general(
            keys[...], parts[head], LANES_IN, preferred_element_type=jnp.float32
        )
        top = jnp.max(scores, axis=0, keepdims=True)
        weights = jnp.exp(scores - top)
        total = jnp.sum(weights, axis=0, keepdims=True)
        mixed = lax.dot_general(
            values[...], rounded(weights), ROWS_IN, preferred_element_type=jnp.float32
        )
        sides.append(mixed / total)
        lse[0, head : head + 1, :] = top + jnp.log(total)
    line = lax.broadcasted_iota(jnp.int32, (128, rows), 0)
    out[...] = rounded(jnp.where(line < 64, sides[0], sides[1]).T)


def cross_backward_kernel(query, keys, values, dout, lse, qgrad, kgrad, vgrad):
    rows = query.shape[0]
    parts = pair_heads(query[...], SCALE)
    grads = pair_heads(dout[...])
    sides, key_parts, value_parts = [], [], []
    for head in range(2):
        scores = lax.dot_general(
            keys[...], parts[head], LANES_IN, preferred_element_type=jnp.float32
        )
        probs = jnp.exp(scores - lse[0, head : head + 1, :])
        slopes = lax.dot_general(
            values[...], grads[head], LANES_IN, preferred_element_type=jnp.float32
        )
        delta = jnp.sum(probs * slopes, axis=0, keepdims=True)
        low = rounded(probs * (slopes - delta))
        value_parts.append(matmul(rounded(probs), grads[head]))
        key_parts.append(matmul(low, parts[head]))
        sides.append(lax.dot_general(keys[...], low, ROWS_IN, preferred_element_type=jnp.float32))
    line = lax.broadcasted_iota(jnp.int32, (128, rows), 0)
    qgrad[...] = rounded(jnp.where(line < 64, sides[0], sides[1]).T * SCALE)
    kgrad[...] = rounded(key_parts[0] + key_parts[1])
    vgrad[...] = rounded(value_parts[0] + value_parts[1])


def cross_forward(query, pair):
    rows, width = query.shape
    count = width // 128
    kept = pair.shape[0]
    return pl.pallas_call(
        cross_forward_kernel,
        grid=(count,),
        in_specs=[
            pl.BlockSpec((rows, 128), lambda i: (0, i)),
            pl.BlockSpec((kept, 128), lambda i: (0, i)),
            pl.BlockSpec((kept, 128), lambda i: (0, count + i)),
        ],
        out_specs=[
            pl.BlockSpec((rows, 128), lambda i: (0, i)),
            pl.BlockSpec((1, 8, rows), lambda i: (i, 0, 0)),
        ],
        out_shape=[
            jax.ShapeDtypeStruct((rows, width), jnp.bfloat16),
            jax.ShapeDtypeStruct((count, 8, rows), jnp.float32),
        ],
        compiler_params=pltpu.CompilerParams(vmem_limit_bytes=VMEM_LIMIT),
        cost_estimate=pl.CostEstimate(
            flops=8 * rows * kept * width, bytes_accessed=4 * kept * width, transcendentals=12 * rows * kept
        ),
        name="cross_forward",
    )(query, pair, pair)


def cross_backward(query, pair, dout, lse):
    rows, width = query.shape
    count = width // 128
    kept = pair.shape[0]
    return pl.pallas_call(
        cross_backward_kernel,
        grid=(count,),
        in_specs=[
            pl.BlockSpec((rows, 128), lambda i: (0, i)),
            pl.BlockSpec((kept, 128), lambda i: (0, i)),
            pl.BlockSpec((kept, 128), lambda i: (0, count + i)),
            pl.BlockSpec((rows, 128), lambda i: (0, i)),
            pl.BlockSpec((1, 8, rows), lambda i: (i, 0, 0)),
        ],
        out_specs=[
            pl.BlockSpec((rows, 128), lambda i: (0, i)),
            pl.BlockSpec((kept, 128), lambda i: (0, i)),
            pl.BlockSpec((kept, 128), lambda i: (0, i)),
        ],
        out_shape=[
            jax.ShapeDtypeStruct((rows, width), jnp.bfloat16),
            jax.ShapeDtypeStruct((kept, width), jnp.bfloat16),
            jax.ShapeDtypeStruct((kept, width), jnp.bfloat16),
        ],
        compiler_params=pltpu.CompilerParams(vmem_limit_bytes=VMEM_LIMIT),
        cost_estimate=pl.CostEstimate(
            flops=20 * rows * kept * width, bytes_accessed=8 * kept * width, transcendentals=12 * rows * kept
        ),
        name="cross_backward",
    )(query, pair, pair, dout, lse)


def pick_kernel(table, bank, out):
    i = pl.program_id(0)
    keep = table[pl.num_programs(0) + i]
    out[0] = jnp.where(keep > 0, bank[0], jnp.zeros_like(bank[0]))


def pick_rows(chunks, spots, found):
    count = spots.shape[0]
    size = chunks.shape[1:]
    table = jnp.concatenate([spots, found.astype(jnp.int32)])
    return pl.pallas_call(
        pick_kernel,
        grid_spec=pltpu.PrefetchScalarGridSpec(
            num_scalar_prefetch=1,
            grid=(count,),
            in_specs=[pl.BlockSpec((1,) + size, lambda i, t: (t[i], 0, 0))],
            out_specs=pl.BlockSpec((1,) + size, lambda i, t: (i, 0, 0)),
        ),
        out_shape=jax.ShapeDtypeStruct((count,) + size, chunks.dtype),
        name="pick_rows",
    )(table, chunks)


def place_kernel(count, table, grads, out):
    spot = pl.program_id(0)
    out[...] = jnp.zeros_like(out)
    for i in range(count):

        @pl.when(table[i] == spot)
        def _(i=i):
            out[0] += wide(grads[i])


def place_rows(grads, spots, chunks):
    count = spots.shape[0]
    size = grads.shape[1:]
    return pl.pallas_call(
        functools.partial(place_kernel, count),
        grid_spec=pltpu.PrefetchScalarGridSpec(
            num_scalar_prefetch=1,
            grid=(chunks,),
            in_specs=[whole((count,) + size)],
            out_specs=pl.BlockSpec((1,) + size, lambda n, t: (n, 0, 0)),
        ),
        out_shape=jax.ShapeDtypeStruct((chunks,) + size, jnp.float32),
        name="place_rows",
    )(spots, grads)


class Chain:
    def __init__(self, stages):
        self.stages = stages
        self.result = None
        self.pending = next(stages)

    def step(self, pending):
        try:
            self.pending = self.stages.send(pending)
        except StopIteration as stop:
            self.pending, self.result = (), stop.value


def meet(values, *chains):
    values, pending = lax.optimization_barrier((values, [chain.pending for chain in chains]))
    for chain, arrays in zip(chains, pending):
        chain.step(arrays)
    return values


def total_of(arrays):
    total = wide(arrays[0])
    for array in arrays[1:]:
        total = total + wide(array)
    return total


def body(
    grid,
    tokens,
    cotangent,
    bank,
    prefix,
    blocks,
    self_qkv,
    self_out,
    cross_q,
    cross_kv,
    cross_out,
    ffn_in,
    ffn_out,
    gains,
    biases,
):
    Z, X, C, Y = grid.z, grid.x, grid.c, grid.y
    devices = grid.seq * Y
    seq_index = lax.axis_index("seq")
    me = {
        "y": lax.axis_index("batch"),
        "c": seq_index % C,
        "x": (seq_index // C) % X,
        "z": seq_index // (C * X),
        "h": seq_index // (2 * C * X),
        "l": seq_index // (C * X) % 2,
    }
    my_z, my_x, my_c = me["z"], me["x"], me["c"]
    rows, width = tokens.shape[1:]
    hidden = ffn_in.shape[1]
    part = width // devices
    fan = hidden // width
    inputs = tokens[0]

    def parted(array, axis, place):
        size = getattr(grid, axis)
        kept = [take(array, me[axis], place)]
        for shift in range(1, size):
            kept.append(grid.send(take(array, me[axis] ^ shift, place), axis, shift))
        return kept

    def reduction(array, axes, lead=0, final=True):
        names = ["h", "l", "x", "c", "y"]
        for axis in axes:
            place = lead + names.index(axis)
            names.remove(axis)
            arrays = yield parted(array, axis, place)
            total = total_of(arrays)
            array = rounded(total)
        return total if final else array

    def sharded(array):
        return array.reshape(2, 2, X, C, Y, array.shape[0] // devices, array.shape[1])

    grouped = self_qkv.reshape(part, 3, GROUPS, GROUP_WIDTH)
    extra = jnp.stack([biases[3], biases[4]], axis=1)
    extra = jnp.broadcast_to(
        jnp.pad(extra, ((0, 0), (0, QUERY - GROUP_WIDTH - 2)))[:, None],
        (part, GROUPS, QUERY - GROUP_WIDTH),
    )
    packed = jnp.concatenate(
        [
            grouped[:, 0],
            extra,
            grouped[:, 1, :, :128],
            grouped[:, 2, :, :128],
            grouped[:, 1, :, 128:],
            grouped[:, 2, :, 128:],
        ],
        axis=2,
    ).transpose(1, 0, 2)
    packed, later = lax.optimization_barrier(
        (packed, (self_out, cross_q, cross_out, cross_kv, ffn_in, ffn_out, gains, biases))
    )
    self_out, cross_q, cross_out, cross_kv, ffn_in, ffn_out, gains, biases = later
    pieces = parted(packed, "z", 0)

    small = jnp.concatenate([gains, biases], axis=0).T
    small = jnp.pad(small, ((0, 0), (0, 128 - small.shape[1])))
    first_pack = jnp.concatenate([self_out, cross_q, cross_out, cross_kv, small], axis=1)
    inner_columns = (
        ffn_in.reshape(part, devices, fan, part).transpose(0, 2, 1, 3).reshape(part, hidden)
    )
    outer_blocks = ffn_out.reshape(fan, part, width).transpose(1, 0, 2).reshape(part, hidden)
    second_pack = jnp.stack([inner_columns, outer_blocks])
    first_all = lax.all_gather(first_pack, ("seq", "batch"), axis=0, tiled=True)
    second_all = lax.all_gather(second_pack, ("seq", "batch"), axis=1, tiled=True)

    pieces, inputs, bank_rows = lax.optimization_barrier((pieces, inputs, bank[0]))
    across = grid.send(inputs, "h", 1)
    beside = grid.send(inputs, "l", 1)

    chunk = BANK_BLOCK * blocks.shape[1] // grid.seq
    per_block = BANK_BLOCK // chunk
    local_chunks = bank.shape[1] // chunk
    local_blocks = bank.shape[1] // BANK_BLOCK
    bank_chunks = bank_rows.reshape(local_chunks, chunk, width)
    home = seq_index * local_blocks
    every = jnp.arange(grid.seq, dtype=jnp.int32)
    wanted = jnp.take(blocks[0], every // per_block) - home
    found = (wanted >= 0) & (wanted < local_blocks)
    spots = jnp.where(found, wanted * per_block + every % per_block, 0)
    picked = pick_rows(bank_chunks, spots, found).reshape(2, 2, X, C, 1, chunk, width)

    def spreading(own):
        array = own
        for axis in "hlxc":
            size = getattr(grid, axis)
            array = jnp.stack((yield [array] + [grid.send(array, axis, m) for m in range(1, size)]))
        return array

    def retrieval():
        own = (yield from reduction(picked, "cxlh", final=False))[0]
        every_row = yield from spreading(own)
        return own, every_row.reshape(grid.seq * chunk, width)

    retrieve = Chain(retrieval())
    gathered = in_order(pieces, my_z)
    for axis in "yxc":
        pieces = [gathered] + [grid.send(gathered, axis, m) for m in range(1, getattr(grid, axis))]
        if axis == "x":
            pieces, across, beside = meet((pieces, across, beside), retrieve)
        gathered = in_order(pieces, me[axis])
    token_parts = [inputs, beside, across, grid.send(across, "l", 1)]
    qkv_group = gathered.transpose(3, 1, 0, 2, 4, 5).reshape(width, PACK)
    column = jnp.arange(PACK, dtype=jnp.int32)
    real = (column < GROUP_WIDTH) | (column >= QUERY)
    is_query = column < GROUP_WIDTH
    is_pair_value = (column >= QUERY + 128) & (column < QUERY + 256)
    is_value = is_pair_value | (column >= QUERY + 320)
    local = jnp.where(is_query, column, column - jnp.where(is_pair_value, QUERY + 128, QUERY + 192))
    line = jnp.where(is_query | is_value, local + my_z * GROUP_WIDTH, -1)
    chosen = (jnp.arange(width, dtype=jnp.int32)[:, None] == line[None]).astype(jnp.bfloat16)
    picked_bias = weight_grad(qkv_group[:, GROUP_WIDTH:QUERY], chosen)
    qkv_bias = jnp.where(is_query, picked_bias[0], picked_bias[1])
    qkv_weight = jnp.where(real[None], qkv_group, jnp.zeros_like(qkv_group))

    qkv_weight, qkv_bias, token_parts = meet((qkv_weight, qkv_bias, token_parts), retrieve)

    token_column = jnp.concatenate(token_parts, axis=0)
    own_queries = rounded(matmul(token_column, qkv_weight[:, :QUERY]) + qkv_bias[:QUERY])
    own_side = rounded(matmul(token_column, qkv_weight[:, QUERY:]) + qkv_bias[QUERY:])
    own_queries = own_queries.reshape(GROUPS, rows, QUERY)

    far_queries = grid.send(own_queries[1::2], "z", 0, mirror=True)
    near_other = grid.send(own_side, "c", 1)
    far_queries, side = lax.optimization_barrier((far_queries, own_side))
    far_own = [grid.send(side, "x", m) for m in range(1, X)]
    queries = jnp.stack(
        [own_queries[m] if m % 2 == 0 else far_queries[m // 2] for m in range(GROUPS)]
    )

    turn = jnp.arange(GROUPS, dtype=jnp.int32)
    turn_z = my_z ^ turn

    def key_firsts(x, c):
        return ((turn_z * X + x) * C + c) * rows

    query_firsts = jnp.where(
        turn % 2 == 0, key_firsts(my_x, my_c), key_firsts(X - 1 - my_x, C - 1 - my_c)
    )

    def table_of(shifts, c):
        keys = [key_firsts(my_x ^ m, c) for m in shifts]
        return jnp.concatenate(keys + [query_firsts, prefix]).astype(jnp.int32)

    far = list(range(1, X))
    tables = {
        "near own": table_of([0], my_c),
        "near other": table_of([0], C - 1 - my_c),
        "far own": table_of(far, my_c),
        "far other": table_of(far, C - 1 - my_c),
    }

    carry = self_forward(tables["near own"], queries, [own_side], None, False)
    carry, near_other = meet((carry, near_other), retrieve)
    carry = self_forward(tables["near other"], queries, [near_other], carry, False)
    carry, far_own = meet((carry, far_own), retrieve)
    far_other = [grid.send(side, "c", 1) for side in far_own]
    carry = self_forward(tables["far own"], queries, far_own, carry, False)
    carry, far_other = meet((carry, far_other), retrieve)
    attention, lse = self_forward(tables["far other"], queries, far_other, carry, True)
    attention, lse = meet((attention, lse), retrieve)
    attention_mine = rounded(attention)

    def swapped(array, m):
        return grid.send(array, "z", m, mirror=m % 2 == 1)

    pieces = [attention_mine[0]] + [swapped(attention_mine[m], m) for m in range(1, Z)]
    pieces = meet(pieces, retrieve)
    retrieve.step(retrieve.pending)
    own_rows, all_rows = retrieve.result
    attention_low = (
        in_order(pieces, my_z)[:, :, :GROUP_WIDTH].transpose(1, 0, 2).reshape(rows, width)
    )

    selfout_full = first_all[:, :width]
    crossq_full = first_all[:, width : 2 * width]
    crossout_full = first_all[:, 2 * width : 3 * width]
    crosskv_full = first_all[:, 3 * width : 5 * width]
    small_full = wide(first_all[:, 5 * width :].T)
    gain = small_full[:3]
    bias = small_full[3:17]
    ffnin_full = second_all[0]
    outer = [second_all[1, :, f * width : (f + 1) * width] for f in range(fan)]
    inner_bias = bias[10:14].reshape(devices, fan, part).transpose(1, 0, 2).reshape(-1)

    resid_one = wide(inputs) + matmul(attention_low, selfout_full) + bias[5]
    hidden_one = layer_norm(resid_one, gain[0], bias[0])
    hidden_one_low = rounded(hidden_one)
    cross_query = rounded(matmul(hidden_one_low, crossq_full) + bias[6])
    cross_pair = rounded(
        matmul(all_rows, crosskv_full) + jnp.concatenate([jnp.zeros((width,), jnp.float32), bias[7]])
    )
    cross_att, cross_lse = cross_forward(cross_query, cross_pair)
    resid_two = hidden_one + matmul(cross_att, crossout_full) + bias[8]
    hidden_two = layer_norm(resid_two, gain[1], bias[1])
    hidden_two_low = rounded(hidden_two)
    inner = matmul(hidden_two_low, ffnin_full) + inner_bias
    activated = rounded(gelu_exact(inner))

    def fan_part(array, f):
        return array[:, f * width : (f + 1) * width]

    resid_three = hidden_two + bias[9]
    for f in range(fan):
        resid_three = resid_three + matmul(fan_part(activated, f), outer[f])
    output = layer_norm(resid_three, gain[2], bias[2])

    _unused, norm_three = jax.vjp(layer_norm, resid_three, gain[2], bias[2])
    dresid_three, dgain_three, dshift_three = norm_three(wide(cotangent[0]))
    douter_low = rounded(dresid_three)
    grad_ffnout = rounded(weight_grad(activated, douter_low))
    reduce_ffnout = Chain(
        reduction(grad_ffnout.reshape(fan, 2, 2, X, C, Y, part, width), "cyxlh", lead=1)
    )
    _unused, gelu_back = jax.vjp(gelu_exact, inner)
    dactivated = jnp.concatenate([back_matmul(douter_low, block) for block in outer], axis=1)
    dinner_low = rounded(gelu_back(dactivated)[0])
    grad_ffnin = rounded(weight_grad(hidden_two_low, dinner_low))
    reduce_ffnin = Chain(reduction(sharded(grad_ffnin), "cyxlh"))

    _unused, norm_two = jax.vjp(layer_norm, resid_two, gain[1], bias[1])
    dresid_two, dgain_two, dshift_two = norm_two(dresid_three + back_matmul(dinner_low, ffnin_full))
    dcross_low = rounded(dresid_two)
    dcross_att = rounded(back_matmul(dcross_low, crossout_full))
    dcross_query, dcross_key, dcross_value = cross_backward(
        cross_query, cross_pair, dcross_att, cross_lse
    )
    dcross_query, dcross_key, dcross_value = meet(
        (dcross_query, dcross_key, dcross_value), reduce_ffnout, reduce_ffnin
    )

    dcross_all = jnp.concatenate([dcross_key, dcross_value], axis=1)
    dcross_all = dcross_all.reshape(C, X, 2, 2, chunk, 2 * width)

    def unspreading(array):
        for axis in "cxlh":
            size = getattr(grid, axis)
            arrays = yield [array[0]] + [grid.send(array[m], axis, m) for m in range(1, size)]
            array = rounded(total_of(arrays))
        return array

    unspread = Chain(unspreading(dcross_all))

    _unused, norm_one = jax.vjp(layer_norm, resid_one, gain[0], bias[0])
    dresid_one, dgain_one, dshift_one = norm_one(dresid_two + back_matmul(dcross_query, crossq_full))
    dbranch_low = rounded(dresid_one)
    datt_low = rounded(back_matmul(dbranch_low, selfout_full))
    datt_groups = jnp.pad(
        datt_low.reshape(rows, GROUPS, GROUP_WIDTH).transpose(1, 0, 2),
        ((0, 0), (0, 0), (0, 256 - GROUP_WIDTH)),
    )
    pieces = [take(datt_groups, my_z, 0)]
    for m in range(1, Z):
        pieces.append(swapped(take(datt_groups, my_z ^ m, 0), m))
    grad_mid = jnp.stack(
        [
            rounded(weight_grad(attention_low, dbranch_low)),
            rounded(weight_grad(hidden_one_low, dcross_query)),
            rounded(weight_grad(cross_att, dcross_low)),
        ]
    )
    grad_mid, pieces = meet((grad_mid, pieces), unspread)
    reduce_mid = Chain(reduction(grad_mid.reshape(3, 2, 2, X, C, Y, part, width), "cyxlh", lead=1))
    dout = jnp.stack(pieces)

    *far_other_grad, slopes, state = self_backward(
        tables["far other"], queries, dout, lse, far_other, attention, True, False
    )
    far_other_grad, slopes = meet(
        (far_other_grad, slopes), reduce_ffnout, reduce_mid, unspread
    )
    far_moved = [grid.send(grad, "c", 1) for grad in far_other_grad]
    *far_own_grad, slopes = self_backward(
        tables["far own"], queries, dout, state, far_own, slopes, False, False
    )
    far_own_grad, far_moved, slopes = meet(
        (far_own_grad, far_moved, slopes), unspread, reduce_ffnout, reduce_ffnin
    )
    far_grad = [rounded(total_of(pair)) for pair in zip(far_own_grad, far_moved)]
    far_moved = [grid.send(grad, "x", m) for m, grad in zip(far, far_grad)]
    near_other_grad, slopes = self_backward(
        tables["near other"], queries, dout, state, [near_other], slopes, False, False
    )
    near_other_grad, far_moved, slopes = meet(
        (near_other_grad, far_moved, slopes), unspread, reduce_ffnout, reduce_ffnin, reduce_mid
    )
    near_moved = grid.send(near_other_grad, "c", 1)

    dcross_pair = unspread.result
    bias_rows = jnp.stack(
        [
            dgain_one,
            dgain_two,
            dgain_three,
            dshift_one,
            dshift_two,
            dshift_three,
            column_sums(dbranch_low),
            column_sums(dcross_query),
            column_sums(dcross_pair[:, width:]),
            column_sums(dcross_low),
            column_sums(douter_low),
        ]
    )
    inner_sums = column_sums(dinner_low).reshape(fan, devices, part).transpose(1, 0, 2)
    bias_rows = jnp.concatenate([bias_rows, inner_sums.reshape(fan, width)], axis=0)
    bias_columns = jnp.pad(rounded(bias_rows.T), ((0, 0), (0, 128 - bias_rows.shape[0])))
    grad_late = jnp.concatenate([rounded(weight_grad(own_rows, dcross_pair)), bias_columns], axis=1)
    reduce_late = Chain(reduction(sharded(grad_late), "cyxlh"))
    spread_back = Chain(spreading(rounded(back_matmul(dcross_pair, crosskv_full))))

    near_own_grad, query_grad = self_backward(
        tables["near own"], queries, dout, state, [own_side], slopes, False, True
    )
    near_own_grad, near_moved, query_grad = meet(
        (near_own_grad, near_moved, query_grad), reduce_late, spread_back, reduce_ffnin, reduce_mid
    )

    far_query_grad = grid.send(query_grad[1::2], "z", 0, mirror=True)
    side_grad = rounded(total_of([near_own_grad, near_moved] + far_moved))
    query_grad = jnp.stack(
        [query_grad[m] if m % 2 == 0 else far_query_grad[m // 2] for m in range(GROUPS)]
    )
    dqkv = jnp.concatenate([query_grad.reshape(GROUPS * rows, QUERY), side_grad], axis=1)
    far_tokens_grad = rounded(back_matmul(dqkv[rows:], qkv_weight)).reshape(Z - 1, rows, width)
    dqkv, far_tokens_grad = meet(
        (dqkv, far_tokens_grad), reduce_ffnin, reduce_late, spread_back
    )
    third = grid.send(far_tokens_grad[2], "l", 1)
    first = grid.send(far_tokens_grad[0], "l", 1)
    grad_group = weight_grad(token_column, dqkv)
    sums = jnp.sum(wide(dqkv), axis=0)
    sums = jnp.stack([jnp.where(is_query, sums, 0.0), jnp.where(is_value, sums, 0.0)])
    sums = jnp.pad(rounded(sums), ((0, QUERY - GROUP_WIDTH - 2), (0, 0)))
    grad_group = jnp.concatenate(
        [grad_group[:, :GROUP_WIDTH], back_matmul(chosen, sums), grad_group[:, QUERY:]], axis=1
    )
    reduce_group = Chain(reduction(sharded(rounded(grad_group)), "cyx", final=False))
    tokens_base = dresid_one + back_matmul(dqkv[:rows], qkv_weight)
    tokens_base, first, third = meet(
        (tokens_base, first, third), reduce_group, reduce_late, spread_back, reduce_mid
    )
    second = grid.send(rounded(total_of([far_tokens_grad[1], third])), "h", 1)
    tokens_base, second = meet((tokens_base, second), reduce_group, reduce_late, spread_back, reduce_mid)
    tokens_grad = total_of([tokens_base, first, second])
    meet((), reduce_group, reduce_late, reduce_ffnout)
    pieces = parted(reduce_group.result.reshape(Z, part, PACK), "z", 0)

    spot = jnp.arange(grid.seq, dtype=jnp.int32)
    spot_z = my_z ^ (spot % 2 * 2 + spot // 2 % 2)
    source = (spot_z * X + (my_x ^ (spot // Z % X))) * C + (my_c ^ (spot // (Z * X)))
    target = jnp.take(blocks[0], source // per_block) - home
    inside = (target >= 0) & (target < local_blocks)
    places = jnp.where(inside, target * per_block + source % per_block, -1)
    drows = spread_back.result.reshape(grid.seq, chunk, width)
    bank_grad = place_rows(drows, places, local_chunks).reshape(bank.shape[1], width)

    grad_groups = wide(in_order(pieces, my_z))
    sides = grad_groups[:, :, QUERY:]
    out_qkv = jnp.stack(
        [
            grad_groups[:, :, :GROUP_WIDTH],
            jnp.concatenate([sides[:, :, :128], sides[:, :, 256:320]], axis=2),
            jnp.concatenate([sides[:, :, 128:256], sides[:, :, 320:384]], axis=2),
        ]
    )
    out_qkv = out_qkv.transpose(2, 0, 1, 3).reshape(part, 3 * width)
    late_bias = jnp.sum(grad_groups[:, :, GROUP_WIDTH : GROUP_WIDTH + 2], axis=0)

    out_late, out_mid = reduce_late.result, reduce_mid.result
    out_ffnin = (
        reduce_ffnin.result.reshape(part, fan, devices, part)
        .transpose(0, 2, 1, 3)
        .reshape(part, hidden)
    )
    out_small = out_late[:, 2 * width :].T
    bias_grad = jnp.concatenate([out_small[3:6], late_bias.T, out_small[6:15]], axis=0)
    return (
        rounded(output)[None],
        tokens_grad[None],
        bank_grad[None],
        out_qkv,
        out_mid[0],
        out_mid[1],
        out_late[:, : 2 * width],
        out_mid[2],
        out_ffnin,
        reduce_ffnout.result.reshape(fan * part, width),
        out_small[:3],
        bias_grad,
    )


def solution(mesh):
    split = P("batch", "seq", None)
    shard = P(("seq", "batch"), None)
    flat = P(None, ("seq", "batch"))
    return jax.shard_map(
        functools.partial(body, Grid(mesh)),
        mesh=mesh,
        in_specs=(split, split, split, P("batch"), P("batch", None)) + (shard,) * 7 + (flat, flat),
        out_specs=(split, split, split) + (shard,) * 7 + (flat, flat),
        check_vma=False,
    )
```

```python
import functools

import jax
import jax.numpy as jnp
from jax import lax
from jax.experimental import pallas as pl
from jax.experimental.pallas import tpu as pltpu
from jax.sharding import PartitionSpec as P

HEADS = 12
HEAD_DIM = 64
BANK_BLOCK = 128
GROUPS = 4
GROUP_HEADS = HEADS // GROUPS
GROUP_WIDTH = GROUP_HEADS * HEAD_DIM
QUERY, SIDE = 256, 384
PACK = QUERY + SIDE
EPSILON = 1e-05
NEGATIVE = -1e30
SCALE = HEAD_DIM ** (-0.5)
LANES_IN = (((1,), (1,)), ((), ()))
ROWS_IN = (((0,), (0,)), ((), ()))
VMEM_LIMIT = 60 * 1024 * 1024


def layer_norm(values, gain, shift):
    centered = values - jnp.mean(values, axis=-1, keepdims=True)
    variance = jnp.mean(centered * centered, axis=-1, keepdims=True)
    return centered * lax.rsqrt(variance + EPSILON) * gain + shift


def gelu_exact(values):
    return jax.nn.gelu(values, approximate=False)


def rounded(values):
    return values.astype(jnp.bfloat16)


def wide(values):
    return values.astype(jnp.float32)


def matmul(left, right):
    return jnp.dot(left, right, preferred_element_type=jnp.float32)


def weight_grad(left, right):
    return lax.dot_general(left, right, ROWS_IN, preferred_element_type=jnp.float32)


def back_matmul(left, right):
    return lax.dot_general(left, right, LANES_IN, preferred_element_type=jnp.float32)


def column_sums(values):
    return jnp.sum(wide(values), axis=0)


class Grid:
    def __init__(self, mesh):
        self.seq = mesh.shape["seq"]
        self.y = mesh.shape["batch"]
        self.z = GROUPS
        self.c = self.h = self.l = 2
        self.x = self.seq // (self.z * self.c)

    def coords(self, index):
        spot, y = divmod(index, self.y)
        spot, c = divmod(spot, self.c)
        z, x = divmod(spot, self.x)
        return z, x, c, y

    def index(self, z, x, c, y):
        return ((z * self.x + x) * self.c + c) * self.y + y

    def send(self, array, axis, shift, mirror=False):
        if axis in "hl":
            axis, shift = "z", shift * (2 if axis == "h" else 1)
        place = "zxcy".index(axis)
        pairs = []
        for index in range(self.seq * self.y):
            spot = list(self.coords(index))
            spot[place] ^= shift
            if mirror:
                spot[1], spot[2] = self.x - 1 - spot[1], self.c - 1 - spot[2]
            pairs.append((index, self.index(*spot)))
        return lax.ppermute(array, ("seq", "batch"), pairs)


def in_order(pieces, me):
    pieces = list(pieces)
    bit = 1
    while bit < len(pieces):
        swap = (me & bit) != 0
        pieces = [jnp.where(swap, pieces[j ^ bit], piece) for j, piece in enumerate(pieces)]
        bit *= 2
    return jnp.stack(pieces)


def take(array, index, axis):
    return lax.dynamic_index_in_dim(array, index, axis, keepdims=False)


def head_parts(block, scale, third_low):
    lane = lax.broadcasted_iota(jnp.int32, (block.shape[0], 128), 1)
    first = wide(block[:, 0:128]) * scale
    third = wide(block[:, 128:256]) * scale
    third = jnp.where(lane < 64, third, 0.0)
    if not third_low:
        third = pltpu.roll(third, 64, 1)
    return (
        rounded(jnp.where(lane < 64, first, 0.0)),
        rounded(jnp.where(lane >= 64, first, 0.0)),
        rounded(third),
    )


def key_tiles(ref, start, size):
    rows = pl.ds(start, size)
    keys = ref[rows, 0:128]
    values = ref[rows, 128:256]
    third = ref[rows, 256:384]
    return (keys, keys, third), (values, values, third)


def allowed_keys(key_first, query_first, prefix_len, shape):
    key_pos = key_first + lax.broadcasted_iota(jnp.int32, shape, 0)
    query_pos = query_first + lax.broadcasted_iota(jnp.int32, shape, 1)
    return (key_pos <= query_pos) | (key_pos < prefix_len)


def each_block(table, refs, rows, query_first, prefix_len, work):
    count = refs[0].shape[0] // rows
    for part, ref in enumerate(refs):

        def step(local, carry, part=part, ref=ref):
            block = part * count + local
            key_first = table[block]
            last = key_first + rows - 1
            seen = (key_first <= query_first + rows - 1) | (key_first < prefix_len)
            whole = (last <= query_first) | (last < prefix_len)

            @pl.when(seen & whole)
            def _():
                work(ref, local * rows, block, key_first, False)

            @pl.when(seen & jnp.logical_not(whole))
            def _():
                work(ref, local * rows, block, key_first, True)

            return carry

        lax.fori_loop(0, count, step, 0)


def forward_kernel(rows, parts, first, last, table, query_in, *refs):
    refs = list(refs)
    sides = [refs.pop(0) for _ in range(parts)]
    if not first:
        accum_in, stats_in = refs.pop(0), refs.pop(0)
    out, state, query, accum, stats = refs
    m = pl.program_id(0)
    blocks = parts * (sides[0].shape[0] // rows)
    query_first = table[blocks + m]
    prefix_len = table[blocks + GROUPS]
    for head, part in enumerate(head_parts(query_in[0], SCALE, True)):
        query[head] = part
    if first:
        accum[...] = jnp.zeros_like(accum)
        stats[0:8, :] = jnp.full((8, rows), NEGATIVE, jnp.float32)
        stats[8:16, :] = jnp.zeros((8, rows), jnp.float32)
    else:
        accum[...] = accum_in[0]
        stats[...] = stats_in[0]

    def work(ref, start, block, key_first, masked):
        keys, values = key_tiles(ref, start, rows)
        if masked:
            mask = allowed_keys(key_first, query_first, prefix_len, (rows, rows))
        for head in range(GROUP_HEADS):
            scores = lax.dot_general(
                keys[head], query[head], LANES_IN, preferred_element_type=jnp.float32
            )
            if masked:
                scores = jnp.where(mask, scores, NEGATIVE)
            old = stats[head : head + 1, :]
            top = jnp.maximum(old, jnp.max(scores, axis=0, keepdims=True))
            weights = jnp.exp(scores - top)
            shrink = jnp.exp(old - top)
            stats[head : head + 1, :] = top
            stats[8 + head : 9 + head, :] = stats[8 + head : 9 + head, :] * shrink + jnp.sum(
                weights, axis=0, keepdims=True
            )
            accum[head] = accum[head] * shrink + lax.dot_general(
                values[head], rounded(weights), ROWS_IN, preferred_element_type=jnp.float32
            )

    each_block(table, sides, rows, query_first, prefix_len, work)
    if not last:
        out[0] = accum[...]
        state[0] = stats[...]
        return
    totals = stats[8 : 8 + GROUP_HEADS, :]
    final = [accum[head] / totals[head : head + 1, :] for head in range(GROUP_HEADS)]
    line = lax.broadcasted_iota(jnp.int32, (128, rows), 0)
    out[0, :, 0:128] = jnp.where(line < 64, final[0], final[1]).T
    third = jnp.concatenate([final[2][64:128], jnp.zeros((64, rows), jnp.float32)], axis=0)
    out[0, :, 128:256] = third.T
    state[0] = jnp.zeros((8, rows), jnp.float32)
    state[0, 0:GROUP_HEADS, :] = stats[0:GROUP_HEADS, :] + jnp.log(totals)


def backward_kernel(rows, parts, first, last, table, query_in, dout, state, *refs):
    refs = list(refs)
    sides = [refs.pop(0) for _ in range(parts)]
    carried = refs.pop(0)
    grads_out = [refs.pop(0) for _ in range(parts)]
    qgrad_out = refs.pop(0)
    if first:
        state_out = refs.pop(0)
    query, accum, qgrad, lines = refs
    m = pl.program_id(0)
    count = sides[0].shape[0] // rows
    blocks = parts * count
    query_first = table[blocks + m]
    prefix_len = table[blocks + GROUPS]

    @pl.when(m == 0)
    def _():
        def clear(index, carry):
            accum[pl.ds(index * rows, rows), :] = jnp.zeros((rows, SIDE), jnp.float32)
            return carry

        lax.fori_loop(0, blocks, clear, 0)

    for head, part in enumerate(head_parts(query_in[0], SCALE, True)):
        query[head] = part
    for head, part in enumerate(head_parts(dout[0], 1.0, False)):
        query[GROUP_HEADS + head] = part
    lines[...] = state[0]
    if first:
        pair_prod = (wide(dout[0, :, 0:128]) * carried[0, :, 0:128]).T
        third_prod = (wide(dout[0, :, 128:256]) * carried[0, :, 128:256]).T
        lines[3:4, :] = jnp.sum(pair_prod[0:64], axis=0, keepdims=True)
        lines[4:5, :] = jnp.sum(pair_prod[64:128], axis=0, keepdims=True)
        lines[5:6, :] = jnp.sum(third_prod[0:64], axis=0, keepdims=True)
        state_out[0] = lines[...]
        qgrad[...] = jnp.zeros_like(qgrad)
    else:
        qgrad[...] = carried[0]

    def work(ref, start, block, key_first, masked):
        keys, values = key_tiles(ref, start, rows)
        if masked:
            mask = allowed_keys(key_first, query_first, prefix_len, (rows, rows))
        key_parts, value_parts = [], []
        for head in range(GROUP_HEADS):
            scores = lax.dot_general(
                keys[head], query[head], LANES_IN, preferred_element_type=jnp.float32
            )
            if masked:
                scores = jnp.where(mask, scores, NEGATIVE)
            probs = jnp.exp(scores - lines[head : head + 1, :])
            slopes = lax.dot_general(
                values[head],
                query[GROUP_HEADS + head],
                LANES_IN,
                preferred_element_type=jnp.float32,
            )
            low = rounded(probs * (slopes - lines[3 + head : 4 + head, :]))
            value_parts.append(matmul(rounded(probs), query[GROUP_HEADS + head]))
            key_parts.append(matmul(low, query[head]))
            qgrad[head] += lax.dot_general(
                keys[head], low, ROWS_IN, preferred_element_type=jnp.float32
            )
        span = pl.ds(pl.multiple_of(block * rows, rows), rows)
        accum[span, 0:128] += key_parts[0] + key_parts[1]
        accum[span, 128:256] += value_parts[0] + value_parts[1]
        accum[span, 256:384] += key_parts[2] + value_parts[2]

    each_block(table, sides, rows, query_first, prefix_len, work)
    if last:
        line = lax.broadcasted_iota(jnp.int32, (128, rows), 0)
        qgrad_out[0, :, 0:128] = rounded(jnp.where(line < 64, qgrad[0], qgrad[1]).T * SCALE)
        qgrad_out[0, :, 128:256] = rounded(jnp.where(line < 64, qgrad[2], 0.0).T * SCALE)
    else:
        qgrad_out[0] = qgrad[...]

    @pl.when(m == GROUPS - 1)
    def _():
        for part, ref in enumerate(grads_out):

            def write(index, carry, part=part, ref=ref):
                source = pl.ds((part * count + index) * rows, rows)
                ref[pl.ds(index * rows, rows), :] = rounded(accum[source, :])
                return carry

            lax.fori_loop(0, count, write, 0)


def whole(shape):
    return pl.BlockSpec(shape, lambda *_: (0,) * len(shape), pipeline_mode=pl.Buffered(1))


def slab(shape):
    return pl.BlockSpec((1,) + shape, lambda m, *_: (m,) + (0,) * len(shape))


def self_forward(table, queries, sides, carried, last):
    rows = queries.shape[1]
    parts, length = len(sides), sides[0].shape[0]
    pairs = GROUPS * parts * length // rows * GROUP_HEADS // 2
    accum, stats = (GROUP_HEADS, 128, rows), (16, rows)
    outs = [(rows, 256), (8, rows)] if last else [accum, stats]
    first = carried is None
    return pl.pallas_call(
        functools.partial(forward_kernel, rows, parts, first, last),
        grid_spec=pltpu.PrefetchScalarGridSpec(
            num_scalar_prefetch=1,
            grid=(GROUPS,),
            in_specs=[slab((rows, QUERY))]
            + [whole((length, SIDE))] * parts
            + ([] if first else [slab(accum), slab(stats)]),
            out_specs=[slab(shape) for shape in outs],
            scratch_shapes=[
                pltpu.VMEM((GROUP_HEADS, rows, 128), jnp.bfloat16),
                pltpu.VMEM(accum, jnp.float32),
                pltpu.VMEM(stats, jnp.float32),
            ],
        ),
        out_shape=[jax.ShapeDtypeStruct((GROUPS,) + shape, jnp.float32) for shape in outs],
        compiler_params=pltpu.CompilerParams(vmem_limit_bytes=VMEM_LIMIT),
        cost_estimate=pl.CostEstimate(
            flops=pairs * rows * rows * 128 * 16,
            bytes_accessed=4 * length * parts * SIDE,
            transcendentals=pairs * rows * rows,
        ),
        name="self_forward",
    )(table, queries, *sides, *(() if first else carried))


def self_backward(table, queries, dout, state, sides, carried, first, last):
    rows = queries.shape[1]
    parts, length = len(sides), sides[0].shape[0]
    pairs = GROUPS * parts * length // rows * GROUP_HEADS // 2
    slope = (GROUP_HEADS, 128, rows)
    outs = [jax.ShapeDtypeStruct((length, SIDE), jnp.bfloat16)] * parts
    out_specs = [whole((length, SIDE))] * parts
    if last:
        outs = outs + [jax.ShapeDtypeStruct((GROUPS, rows, QUERY), jnp.bfloat16)]
        out_specs = out_specs + [slab((rows, QUERY))]
    else:
        outs = outs + [jax.ShapeDtypeStruct((GROUPS,) + slope, jnp.float32)]
        out_specs = out_specs + [slab(slope)]
    if first:
        outs = outs + [jax.ShapeDtypeStruct((GROUPS, 8, rows), jnp.float32)]
        out_specs = out_specs + [slab((8, rows))]
    return pl.pallas_call(
        functools.partial(backward_kernel, rows, parts, first, last),
        grid_spec=pltpu.PrefetchScalarGridSpec(
            num_scalar_prefetch=1,
            grid=(GROUPS,),
            in_specs=[slab((rows, QUERY)), slab((rows, 256)), slab((8, rows))]
            + [whole((length, SIDE))] * parts
            + [slab((rows, 256)) if first else slab(slope)],
            out_specs=out_specs,
            scratch_shapes=[
                pltpu.VMEM((2 * GROUP_HEADS, rows, 128), jnp.bfloat16),
                pltpu.VMEM((parts * length, SIDE), jnp.float32),
                pltpu.VMEM(slope, jnp.float32),
                pltpu.VMEM((8, rows), jnp.float32),
            ],
        ),
        out_shape=outs,
        compiler_params=pltpu.CompilerParams(vmem_limit_bytes=VMEM_LIMIT),
        cost_estimate=pl.CostEstimate(
            flops=pairs * rows * rows * 128 * 20,
            bytes_accessed=8 * length * parts * SIDE,
            transcendentals=pairs * rows * rows,
        ),
        name="self_backward",
    )(table, queries, dout, state, *sides, carried)


def pair_heads(block, scale=1.0):
    lane = lax.broadcasted_iota(jnp.int32, block.shape, 1)
    values = wide(block) * scale
    return rounded(jnp.where(lane < 64, values, 0.0)), rounded(jnp.where(lane >= 64, values, 0.0))


def cross_forward_kernel(query, keys, values, out, lse):
    rows = query.shape[0]
    parts = pair_heads(query[...], SCALE)
    sides = []
    lse[0] = jnp.zeros((8, rows), jnp.float32)
    for head in range(2):
        scores = lax.dot_general(
            keys[...], parts[head], LANES_IN, preferred_element_type=jnp.float32
        )
        top = jnp.max(scores, axis=0, keepdims=True)
        weights = jnp.exp(scores - top)
        total = jnp.sum(weights, axis=0, keepdims=True)
        mixed = lax.dot_general(
            values[...], rounded(weights), ROWS_IN, preferred_element_type=jnp.float32
        )
        sides.append(mixed / total)
        lse[0, head : head + 1, :] = top + jnp.log(total)
    line = lax.broadcasted_iota(jnp.int32, (128, rows), 0)
    out[...] = rounded(jnp.where(line < 64, sides[0], sides[1]).T)


def cross_backward_kernel(query, keys, values, dout, lse, qgrad, kgrad, vgrad):
    rows = query.shape[0]
    parts = pair_heads(query[...], SCALE)
    grads = pair_heads(dout[...])
    sides, key_parts, value_parts = [], [], []
    for head in range(2):
        scores = lax.dot_general(
            keys[...], parts[head], LANES_IN, preferred_element_type=jnp.float32
        )
        probs = jnp.exp(scores - lse[0, head : head + 1, :])
        slopes = lax.dot_general(
            values[...], grads[head], LANES_IN, preferred_element_type=jnp.float32
        )
        delta = jnp.sum(probs * slopes, axis=0, keepdims=True)
        low = rounded(probs * (slopes - delta))
        value_parts.append(matmul(rounded(probs), grads[head]))
        key_parts.append(matmul(low, parts[head]))
        sides.append(lax.dot_general(keys[...], low, ROWS_IN, preferred_element_type=jnp.float32))
    line = lax.broadcasted_iota(jnp.int32, (128, rows), 0)
    qgrad[...] = rounded(jnp.where(line < 64, sides[0], sides[1]).T * SCALE)
    kgrad[...] = rounded(key_parts[0] + key_parts[1])
    vgrad[...] = rounded(value_parts[0] + value_parts[1])


def cross_forward(query, pair):
    rows, width = query.shape
    count = width // 128
    kept = pair.shape[0]
    return pl.pallas_call(
        cross_forward_kernel,
        grid=(count,),
        in_specs=[
            pl.BlockSpec((rows, 128), lambda i: (0, i)),
            pl.BlockSpec((kept, 128), lambda i: (0, i)),
            pl.BlockSpec((kept, 128), lambda i: (0, count + i)),
        ],
        out_specs=[
            pl.BlockSpec((rows, 128), lambda i: (0, i)),
            pl.BlockSpec((1, 8, rows), lambda i: (i, 0, 0)),
        ],
        out_shape=[
            jax.ShapeDtypeStruct((rows, width), jnp.bfloat16),
            jax.ShapeDtypeStruct((count, 8, rows), jnp.float32),
        ],
        compiler_params=pltpu.CompilerParams(vmem_limit_bytes=VMEM_LIMIT),
        cost_estimate=pl.CostEstimate(
            flops=8 * rows * kept * width, bytes_accessed=4 * kept * width, transcendentals=12 * rows * kept
        ),
        name="cross_forward",
    )(query, pair, pair)


def cross_backward(query, pair, dout, lse):
    rows, width = query.shape
    count = width // 128
    kept = pair.shape[0]
    return pl.pallas_call(
        cross_backward_kernel,
        grid=(count,),
        in_specs=[
            pl.BlockSpec((rows, 128), lambda i: (0, i)),
            pl.BlockSpec((kept, 128), lambda i: (0, i)),
            pl.BlockSpec((kept, 128), lambda i: (0, count + i)),
            pl.BlockSpec((rows, 128), lambda i: (0, i)),
            pl.BlockSpec((1, 8, rows), lambda i: (i, 0, 0)),
        ],
        out_specs=[
            pl.BlockSpec((rows, 128), lambda i: (0, i)),
            pl.BlockSpec((kept, 128), lambda i: (0, i)),
            pl.BlockSpec((kept, 128), lambda i: (0, i)),
        ],
        out_shape=[
            jax.ShapeDtypeStruct((rows, width), jnp.bfloat16),
            jax.ShapeDtypeStruct((kept, width), jnp.bfloat16),
            jax.ShapeDtypeStruct((kept, width), jnp.bfloat16),
        ],
        compiler_params=pltpu.CompilerParams(vmem_limit_bytes=VMEM_LIMIT),
        cost_estimate=pl.CostEstimate(
            flops=20 * rows * kept * width, bytes_accessed=8 * kept * width, transcendentals=12 * rows * kept
        ),
        name="cross_backward",
    )(query, pair, pair, dout, lse)


def pick_kernel(table, bank, out):
    i = pl.program_id(0)
    keep = table[pl.num_programs(0) + i]
    out[0] = jnp.where(keep > 0, bank[0], jnp.zeros_like(bank[0]))


def pick_rows(chunks, spots, found):
    count = spots.shape[0]
    size = chunks.shape[1:]
    table = jnp.concatenate([spots, found.astype(jnp.int32)])
    return pl.pallas_call(
        pick_kernel,
        grid_spec=pltpu.PrefetchScalarGridSpec(
            num_scalar_prefetch=1,
            grid=(count,),
            in_specs=[pl.BlockSpec((1,) + size, lambda i, t: (t[i], 0, 0))],
            out_specs=pl.BlockSpec((1,) + size, lambda i, t: (i, 0, 0)),
        ),
        out_shape=jax.ShapeDtypeStruct((count,) + size, chunks.dtype),
        name="pick_rows",
    )(table, chunks)


def place_kernel(count, table, grads, out):
    spot = pl.program_id(0)
    out[...] = jnp.zeros_like(out)
    for i in range(count):

        @pl.when(table[i] == spot)
        def _(i=i):
            out[0] += wide(grads[i])


def place_rows(grads, spots, chunks):
    count = spots.shape[0]
    size = grads.shape[1:]
    return pl.pallas_call(
        functools.partial(place_kernel, count),
        grid_spec=pltpu.PrefetchScalarGridSpec(
            num_scalar_prefetch=1,
            grid=(chunks,),
            in_specs=[whole((count,) + size)],
            out_specs=pl.BlockSpec((1,) + size, lambda n, t: (n, 0, 0)),
        ),
        out_shape=jax.ShapeDtypeStruct((chunks,) + size, jnp.float32),
        name="place_rows",
    )(spots, grads)


class Chain:
    def __init__(self, stages):
        self.stages = stages
        self.result = None
        self.pending = next(stages)

    def step(self, pending):
        try:
            self.pending = self.stages.send(pending)
        except StopIteration as stop:
            self.pending, self.result = (), stop.value


def meet(values, *chains):
    values, pending = lax.optimization_barrier((values, [chain.pending for chain in chains]))
    for chain, arrays in zip(chains, pending):
        chain.step(arrays)
    return values


def settle(values, *chains):
    values, kept = lax.optimization_barrier((values, [chain.pending[0] for chain in chains]))
    for chain, array in zip(chains, kept):
        chain.pending = [array] + list(chain.pending[1:])
    return values


def total_of(arrays):
    total = wide(arrays[0])
    for array in arrays[1:]:
        total = total + wide(array)
    return total


def body(
    grid,
    tokens,
    cotangent,
    bank,
    prefix,
    blocks,
    self_qkv,
    self_out,
    cross_q,
    cross_kv,
    cross_out,
    ffn_in,
    ffn_out,
    gains,
    biases,
):
    Z, X, C, Y = grid.z, grid.x, grid.c, grid.y
    devices = grid.seq * Y
    seq_index = lax.axis_index("seq")
    me = {
        "y": lax.axis_index("batch"),
        "c": seq_index % C,
        "x": (seq_index // C) % X,
        "z": seq_index // (C * X),
        "h": seq_index // (2 * C * X),
        "l": seq_index // (C * X) % 2,
    }
    my_z, my_x, my_c = me["z"], me["x"], me["c"]
    rows, width = tokens.shape[1:]
    hidden = ffn_in.shape[1]
    part = width // devices
    fan = hidden // width
    inputs = tokens[0]

    def parted(array, axis, place):
        size = getattr(grid, axis)
        kept = [take(array, me[axis], place)]
        for shift in range(1, size):
            kept.append(grid.send(take(array, me[axis] ^ shift, place), axis, shift))
        return kept

    def reduction(array, axes, lead=0, final=True):
        names = ["h", "l", "x", "c", "y"]
        for axis in axes:
            place = lead + names.index(axis)
            names.remove(axis)
            arrays = yield parted(array, axis, place)
            total = total_of(arrays)
            array = rounded(total)
        return total if final else array

    def sharded(array):
        return array.reshape(2, 2, X, C, Y, array.shape[0] // devices, array.shape[1])

    grouped = self_qkv.reshape(part, 3, GROUPS, GROUP_WIDTH)
    extra = jnp.stack([biases[3], biases[4]], axis=1)
    extra = jnp.broadcast_to(
        jnp.pad(extra, ((0, 0), (0, QUERY - GROUP_WIDTH - 2)))[:, None],
        (part, GROUPS, QUERY - GROUP_WIDTH),
    )
    packed = jnp.concatenate(
        [
            grouped[:, 0],
            extra,
            grouped[:, 1, :, :128],
            grouped[:, 2, :, :128],
            grouped[:, 1, :, 128:],
            grouped[:, 2, :, 128:],
        ],
        axis=2,
    ).transpose(1, 0, 2)
    packed, later = lax.optimization_barrier(
        (packed, (self_out, cross_q, cross_out, cross_kv, ffn_in, ffn_out, gains, biases))
    )
    self_out, cross_q, cross_out, cross_kv, ffn_in, ffn_out, gains, biases = later
    pieces = parted(packed, "z", 0)

    small = jnp.concatenate([gains, biases], axis=0).T
    small = jnp.pad(small, ((0, 0), (0, 128 - small.shape[1])))
    first_pack = jnp.concatenate([self_out, cross_q, cross_out, cross_kv, small], axis=1)
    inner_columns = (
        ffn_in.reshape(part, devices, fan, part).transpose(0, 2, 1, 3).reshape(part, hidden)
    )
    outer_blocks = ffn_out.reshape(fan, part, width).transpose(1, 0, 2).reshape(part, hidden)
    second_pack = jnp.stack([inner_columns, outer_blocks])
    first_all = lax.all_gather(first_pack, ("seq", "batch"), axis=0, tiled=True)
    second_all = lax.all_gather(second_pack, ("seq", "batch"), axis=1, tiled=True)

    pieces, inputs, bank_rows = lax.optimization_barrier((pieces, inputs, bank[0]))
    across = grid.send(inputs, "h", 1)
    beside = grid.send(inputs, "l", 1)

    chunk = BANK_BLOCK * blocks.shape[1] // grid.seq
    per_block = BANK_BLOCK // chunk
    local_chunks = bank.shape[1] // chunk
    local_blocks = bank.shape[1] // BANK_BLOCK
    bank_chunks = bank_rows.reshape(local_chunks, chunk, width)
    home = seq_index * local_blocks
    every = jnp.arange(grid.seq, dtype=jnp.int32)
    wanted = jnp.take(blocks[0], every // per_block) - home
    found = (wanted >= 0) & (wanted < local_blocks)
    spots = jnp.where(found, wanted * per_block + every % per_block, 0)
    picked = pick_rows(bank_chunks, spots, found).reshape(2, 2, X, C, 1, chunk, width)

    def spreading(own):
        array = own
        for axis in "hlxc":
            size = getattr(grid, axis)
            array = jnp.stack((yield [array] + [grid.send(array, axis, m) for m in range(1, size)]))
        return array

    def retrieval():
        own = (yield from reduction(picked, "cxlh", final=False))[0]
        every_row = yield from spreading(own)
        return own, every_row.reshape(grid.seq * chunk, width)

    retrieve = Chain(retrieval())
    gathered = in_order(pieces, my_z)
    for axis in "yxc":
        pieces = [gathered] + [grid.send(gathered, axis, m) for m in range(1, getattr(grid, axis))]
        if axis == "x":
            pieces, across, beside = meet((pieces, across, beside), retrieve)
        gathered = in_order(pieces, me[axis])
    token_parts = [inputs, beside, across, grid.send(across, "l", 1)]
    qkv_group = gathered.transpose(3, 1, 0, 2, 4, 5).reshape(width, PACK)
    column = jnp.arange(PACK, dtype=jnp.int32)
    real = (column < GROUP_WIDTH) | (column >= QUERY)
    is_query = column < GROUP_WIDTH
    is_pair_value = (column >= QUERY + 128) & (column < QUERY + 256)
    is_value = is_pair_value | (column >= QUERY + 320)
    local = jnp.where(is_query, column, column - jnp.where(is_pair_value, QUERY + 128, QUERY + 192))
    line = jnp.where(is_query | is_value, local + my_z * GROUP_WIDTH, -1)
    chosen = (jnp.arange(width, dtype=jnp.int32)[:, None] == line[None]).astype(jnp.bfloat16)
    picked_bias = weight_grad(qkv_group[:, GROUP_WIDTH:QUERY], chosen)
    qkv_bias = jnp.where(is_query, picked_bias[0], picked_bias[1])
    qkv_weight = jnp.where(real[None], qkv_group, jnp.zeros_like(qkv_group))

    qkv_weight, qkv_bias, token_parts = meet((qkv_weight, qkv_bias, token_parts), retrieve)

    token_column = jnp.concatenate(token_parts, axis=0)
    own_queries = rounded(matmul(token_column, qkv_weight[:, :QUERY]) + qkv_bias[:QUERY])
    own_side = rounded(matmul(token_column, qkv_weight[:, QUERY:]) + qkv_bias[QUERY:])
    own_queries = own_queries.reshape(GROUPS, rows, QUERY)

    far_queries = grid.send(own_queries[1::2], "z", 0, mirror=True)
    near_other = grid.send(own_side, "c", 1)
    far_queries, side = lax.optimization_barrier((far_queries, own_side))
    far_own = [grid.send(side, "x", m) for m in range(1, X)]
    queries = jnp.stack(
        [own_queries[m] if m % 2 == 0 else far_queries[m // 2] for m in range(GROUPS)]
    )

    turn = jnp.arange(GROUPS, dtype=jnp.int32)
    turn_z = my_z ^ turn

    def key_firsts(x, c):
        return ((turn_z * X + x) * C + c) * rows

    query_firsts = jnp.where(
        turn % 2 == 0, key_firsts(my_x, my_c), key_firsts(X - 1 - my_x, C - 1 - my_c)
    )

    def table_of(shifts, c):
        keys = [key_firsts(my_x ^ m, c) for m in shifts]
        return jnp.concatenate(keys + [query_firsts, prefix]).astype(jnp.int32)

    far = list(range(1, X))
    tables = {
        "near own": table_of([0], my_c),
        "near other": table_of([0], C - 1 - my_c),
        "far own": table_of(far, my_c),
        "far other": table_of(far, C - 1 - my_c),
    }

    carry = self_forward(tables["near own"], queries, [own_side], None, False)
    carry, near_other = meet((carry, near_other), retrieve)
    carry = self_forward(tables["near other"], queries, [near_other], carry, False)
    carry, far_own = meet((carry, far_own), retrieve)
    far_other = [grid.send(side, "c", 1) for side in far_own]
    carry = self_forward(tables["far own"], queries, far_own, carry, False)
    carry, far_other = meet((carry, far_other), retrieve)
    attention, lse = self_forward(tables["far other"], queries, far_other, carry, True)
    attention, lse = meet((attention, lse), retrieve)
    attention_mine = rounded(attention)

    def swapped(array, m):
        return grid.send(array, "z", m, mirror=m % 2 == 1)

    pieces = [attention_mine[0]] + [swapped(attention_mine[m], m) for m in range(1, Z)]
    pieces = meet(pieces, retrieve)
    retrieve.step(retrieve.pending)
    own_rows, all_rows = retrieve.result
    attention_low = (
        in_order(pieces, my_z)[:, :, :GROUP_WIDTH].transpose(1, 0, 2).reshape(rows, width)
    )

    selfout_full = first_all[:, :width]
    crossq_full = first_all[:, width : 2 * width]
    crossout_full = first_all[:, 2 * width : 3 * width]
    crosskv_full = first_all[:, 3 * width : 5 * width]
    small_full = wide(first_all[:, 5 * width :].T)
    gain = small_full[:3]
    bias = small_full[3:17]
    ffnin_full = second_all[0]
    outer = [second_all[1, :, f * width : (f + 1) * width] for f in range(fan)]
    inner_bias = bias[10:14].reshape(devices, fan, part).transpose(1, 0, 2).reshape(-1)

    resid_one = wide(inputs) + matmul(attention_low, selfout_full) + bias[5]
    hidden_one = layer_norm(resid_one, gain[0], bias[0])
    hidden_one_low = rounded(hidden_one)
    cross_query = rounded(matmul(hidden_one_low, crossq_full) + bias[6])
    cross_pair = rounded(
        matmul(all_rows, crosskv_full) + jnp.concatenate([jnp.zeros((width,), jnp.float32), bias[7]])
    )
    cross_att, cross_lse = cross_forward(cross_query, cross_pair)
    resid_two = hidden_one + matmul(cross_att, crossout_full) + bias[8]
    hidden_two = layer_norm(resid_two, gain[1], bias[1])
    hidden_two_low = rounded(hidden_two)
    inner = matmul(hidden_two_low, ffnin_full) + inner_bias
    activated = rounded(gelu_exact(inner))

    def fan_part(array, f):
        return array[:, f * width : (f + 1) * width]

    resid_three = hidden_two + bias[9]
    for f in range(fan):
        resid_three = resid_three + matmul(fan_part(activated, f), outer[f])
    output = layer_norm(resid_three, gain[2], bias[2])

    _unused, norm_three = jax.vjp(layer_norm, resid_three, gain[2], bias[2])
    dresid_three, dgain_three, dshift_three = norm_three(wide(cotangent[0]))
    douter_low = rounded(dresid_three)
    grad_ffnout = rounded(weight_grad(activated, douter_low))
    reduce_ffnout = Chain(
        reduction(grad_ffnout.reshape(fan, 2, 2, X, C, Y, part, width), "cyxlh", lead=1)
    )
    _unused, gelu_back = jax.vjp(gelu_exact, inner)
    dactivated = jnp.concatenate([back_matmul(douter_low, block) for block in outer], axis=1)
    dinner_low = rounded(gelu_back(dactivated)[0])
    grad_ffnin = rounded(weight_grad(hidden_two_low, dinner_low))
    reduce_ffnin = Chain(reduction(sharded(grad_ffnin), "cyxlh"))

    _unused, norm_two = jax.vjp(layer_norm, resid_two, gain[1], bias[1])
    dresid_two, dgain_two, dshift_two = norm_two(dresid_three + back_matmul(dinner_low, ffnin_full))
    dcross_low = rounded(dresid_two)
    dcross_att = rounded(back_matmul(dcross_low, crossout_full))
    dcross_query, dcross_key, dcross_value = cross_backward(
        cross_query, cross_pair, dcross_att, cross_lse
    )
    dcross_query, dcross_key, dcross_value = meet(
        (dcross_query, dcross_key, dcross_value), reduce_ffnout, reduce_ffnin
    )

    dcross_all = jnp.concatenate([dcross_key, dcross_value], axis=1)
    dcross_all = dcross_all.reshape(C, X, 2, 2, chunk, 2 * width)

    def unspreading(array):
        for axis in "cxlh":
            size = getattr(grid, axis)
            arrays = yield [array[0]] + [grid.send(array[m], axis, m) for m in range(1, size)]
            array = rounded(total_of(arrays))
        return array

    unspread = Chain(unspreading(dcross_all))

    _unused, norm_one = jax.vjp(layer_norm, resid_one, gain[0], bias[0])
    dresid_one, dgain_one, dshift_one = norm_one(dresid_two + back_matmul(dcross_query, crossq_full))
    dbranch_low = rounded(dresid_one)
    datt_low = rounded(back_matmul(dbranch_low, selfout_full))
    datt_groups = jnp.pad(
        datt_low.reshape(rows, GROUPS, GROUP_WIDTH).transpose(1, 0, 2),
        ((0, 0), (0, 0), (0, 256 - GROUP_WIDTH)),
    )
    pieces = [take(datt_groups, my_z, 0)]
    for m in range(1, Z):
        pieces.append(swapped(take(datt_groups, my_z ^ m, 0), m))
    grad_mid = jnp.stack(
        [
            rounded(weight_grad(attention_low, dbranch_low)),
            rounded(weight_grad(hidden_one_low, dcross_query)),
            rounded(weight_grad(cross_att, dcross_low)),
        ]
    )
    grad_mid, pieces = meet((grad_mid, pieces), unspread)
    reduce_mid = Chain(reduction(grad_mid.reshape(3, 2, 2, X, C, Y, part, width), "cyxlh", lead=1))
    dout = jnp.stack(pieces)

    *far_other_grad, slopes, state = self_backward(
        tables["far other"], queries, dout, lse, far_other, attention, True, False
    )
    far_other_grad, slopes = meet(
        (far_other_grad, slopes), reduce_ffnout, reduce_mid, unspread
    )
    far_moved = [grid.send(grad, "c", 1) for grad in far_other_grad]
    *far_own_grad, slopes = self_backward(
        tables["far own"], queries, dout, state, far_own, slopes, False, False
    )
    far_own_grad, far_moved, slopes = meet(
        (far_own_grad, far_moved, slopes), unspread, reduce_ffnout, reduce_ffnin
    )
    far_grad = [rounded(total_of(pair)) for pair in zip(far_own_grad, far_moved)]
    far_moved = [grid.send(grad, "x", m) for m, grad in zip(far, far_grad)]
    near_other_grad, slopes = self_backward(
        tables["near other"], queries, dout, state, [near_other], slopes, False, False
    )
    near_other_grad, far_moved, slopes = meet(
        (near_other_grad, far_moved, slopes), unspread, reduce_ffnout, reduce_ffnin, reduce_mid
    )
    near_moved = grid.send(near_other_grad, "c", 1)

    dcross_pair = unspread.result
    bias_rows = jnp.stack(
        [
            dgain_one,
            dgain_two,
            dgain_three,
            dshift_one,
            dshift_two,
            dshift_three,
            column_sums(dbranch_low),
            column_sums(dcross_query),
            column_sums(dcross_pair[:, width:]),
            column_sums(dcross_low),
            column_sums(douter_low),
        ]
    )
    inner_sums = column_sums(dinner_low).reshape(fan, devices, part).transpose(1, 0, 2)
    bias_rows = jnp.concatenate([bias_rows, inner_sums.reshape(fan, width)], axis=0)
    bias_columns = jnp.pad(rounded(bias_rows.T), ((0, 0), (0, 128 - bias_rows.shape[0])))
    grad_late = jnp.concatenate([rounded(weight_grad(own_rows, dcross_pair)), bias_columns], axis=1)
    reduce_late = Chain(reduction(sharded(grad_late), "cyxlh"))
    spread_back = Chain(spreading(rounded(back_matmul(dcross_pair, crosskv_full))))

    slopes = settle(slopes, reduce_late, spread_back, reduce_ffnin, reduce_mid)
    near_own_grad, query_grad = self_backward(
        tables["near own"], queries, dout, state, [own_side], slopes, False, True
    )
    near_own_grad, near_moved, query_grad = meet(
        (near_own_grad, near_moved, query_grad), reduce_late, spread_back, reduce_mid
    )

    far_query_grad = grid.send(query_grad[1::2], "z", 0, mirror=True)
    side_grad = rounded(total_of([near_own_grad, near_moved] + far_moved))
    query_grad = jnp.stack(
        [query_grad[m] if m % 2 == 0 else far_query_grad[m // 2] for m in range(GROUPS)]
    )
    dqkv = jnp.concatenate([query_grad.reshape(GROUPS * rows, QUERY), side_grad], axis=1)
    far_tokens_grad = rounded(back_matmul(dqkv[rows:], qkv_weight)).reshape(Z - 1, rows, width)
    dqkv, far_tokens_grad = meet(
        (dqkv, far_tokens_grad), reduce_ffnin, reduce_late, spread_back, reduce_mid
    )
    third = grid.send(far_tokens_grad[2], "l", 1)
    grad_group = weight_grad(token_column, dqkv)
    sums = jnp.sum(wide(dqkv), axis=0)
    sums = jnp.stack([jnp.where(is_query, sums, 0.0), jnp.where(is_value, sums, 0.0)])
    sums = jnp.pad(rounded(sums), ((0, QUERY - GROUP_WIDTH - 2), (0, 0)))
    grad_group = jnp.concatenate(
        [grad_group[:, :GROUP_WIDTH], back_matmul(chosen, sums), grad_group[:, QUERY:]], axis=1
    )
    reduce_group = Chain(reduction(sharded(rounded(grad_group)), "cyx", final=False))
    tokens_base = dresid_one + back_matmul(dqkv[:rows], qkv_weight)
    tokens_base, third, near_tokens_grad = meet(
        (tokens_base, third, far_tokens_grad[:2]),
        reduce_group,
        reduce_late,
        spread_back,
        reduce_mid,
    )
    second = grid.send(rounded(total_of([near_tokens_grad[1], third])), "h", 1)
    first = grid.send(near_tokens_grad[0], "l", 1)
    tokens_base, second = meet((tokens_base, second), reduce_group, reduce_late, spread_back)
    drows = spread_back.result
    meet((), reduce_group, reduce_late, reduce_ffnout, reduce_ffnin)
    pieces = parted(reduce_group.result.reshape(Z, part, PACK), "z", 0)
    drows, pieces[0] = lax.optimization_barrier((drows, pieces[0]))
    tokens_grad = total_of([tokens_base, first, second])

    spot = jnp.arange(grid.seq, dtype=jnp.int32)
    spot_z = my_z ^ (spot % 2 * 2 + spot // 2 % 2)
    source = (spot_z * X + (my_x ^ (spot // Z % X))) * C + (my_c ^ (spot // (Z * X)))
    target = jnp.take(blocks[0], source // per_block) - home
    inside = (target >= 0) & (target < local_blocks)
    places = jnp.where(inside, target * per_block + source % per_block, -1)
    drows = drows.reshape(grid.seq, chunk, width)
    bank_grad = place_rows(drows, places, local_chunks).reshape(bank.shape[1], width)

    grad_groups = wide(in_order(pieces, my_z))
    sides = grad_groups[:, :, QUERY:]
    out_qkv = jnp.stack(
        [
            grad_groups[:, :, :GROUP_WIDTH],
            jnp.concatenate([sides[:, :, :128], sides[:, :, 256:320]], axis=2),
            jnp.concatenate([sides[:, :, 128:256], sides[:, :, 320:384]], axis=2),
        ]
    )
    out_qkv = out_qkv.transpose(2, 0, 1, 3).reshape(part, 3 * width)
    late_bias = jnp.sum(grad_groups[:, :, GROUP_WIDTH : GROUP_WIDTH + 2], axis=0)

    out_late, out_mid = reduce_late.result, reduce_mid.result
    out_ffnin = (
        reduce_ffnin.result.reshape(part, fan, devices, part)
        .transpose(0, 2, 1, 3)
        .reshape(part, hidden)
    )
    out_small = out_late[:, 2 * width :].T
    bias_grad = jnp.concatenate([out_small[3:6], late_bias.T, out_small[6:15]], axis=0)
    return (
        rounded(output)[None],
        tokens_grad[None],
        bank_grad[None],
        out_qkv,
        out_mid[0],
        out_mid[1],
        out_late[:, : 2 * width],
        out_mid[2],
        out_ffnin,
        reduce_ffnout.result.reshape(fan * part, width),
        out_small[:3],
        bias_grad,
    )


def solution(mesh):
    split = P("batch", "seq", None)
    shard = P(("seq", "batch"), None)
    flat = P(None, ("seq", "batch"))
    return jax.shard_map(
        functools.partial(body, Grid(mesh)),
        mesh=mesh,
        in_specs=(split, split, split, P("batch"), P("batch", None)) + (shard,) * 7 + (flat, flat),
        out_specs=(split, split, split) + (shard,) * 7 + (flat, flat),
        check_vma=False,
    )
```

```python
import functools

import jax
import jax.numpy as jnp
from jax import lax
from jax.experimental import pallas as pl
from jax.experimental.pallas import tpu as pltpu
from jax.sharding import PartitionSpec as P

HEADS = 12
HEAD_DIM = 64
BANK_BLOCK = 128
GROUPS = 4
GROUP_HEADS = HEADS // GROUPS
GROUP_WIDTH = GROUP_HEADS * HEAD_DIM
QUERY, SIDE = 256, 384
PACK = QUERY + SIDE
EPSILON = 1e-05
NEGATIVE = -1e30
SCALE = HEAD_DIM ** (-0.5)
LANES_IN = (((1,), (1,)), ((), ()))
ROWS_IN = (((0,), (0,)), ((), ()))
VMEM_LIMIT = 60 * 1024 * 1024


def layer_norm(values, gain, shift):
    centered = values - jnp.mean(values, axis=-1, keepdims=True)
    variance = jnp.mean(centered * centered, axis=-1, keepdims=True)
    return centered * lax.rsqrt(variance + EPSILON) * gain + shift


def gelu_exact(values):
    return jax.nn.gelu(values, approximate=False)


def rounded(values):
    return values.astype(jnp.bfloat16)


def wide(values):
    return values.astype(jnp.float32)


def matmul(left, right):
    return jnp.dot(left, right, preferred_element_type=jnp.float32)


def weight_grad(left, right):
    return lax.dot_general(left, right, ROWS_IN, preferred_element_type=jnp.float32)


def back_matmul(left, right):
    return lax.dot_general(left, right, LANES_IN, preferred_element_type=jnp.float32)


def column_sums(values):
    return jnp.sum(wide(values), axis=0)


class Grid:
    def __init__(self, mesh):
        self.seq = mesh.shape["seq"]
        self.y = mesh.shape["batch"]
        self.z = GROUPS
        self.c = self.h = self.l = 2
        self.x = self.seq // (self.z * self.c)

    def coords(self, index):
        spot, y = divmod(index, self.y)
        spot, c = divmod(spot, self.c)
        z, x = divmod(spot, self.x)
        return z, x, c, y

    def index(self, z, x, c, y):
        return ((z * self.x + x) * self.c + c) * self.y + y

    def send(self, array, axis, shift, mirror=False):
        if axis in "hl":
            axis, shift = "z", shift * (2 if axis == "h" else 1)
        place = "zxcy".index(axis)
        pairs = []
        for index in range(self.seq * self.y):
            spot = list(self.coords(index))
            spot[place] ^= shift
            if mirror:
                spot[1], spot[2] = self.x - 1 - spot[1], self.c - 1 - spot[2]
            pairs.append((index, self.index(*spot)))
        return lax.ppermute(array, ("seq", "batch"), pairs)


def in_order(pieces, me):
    pieces = list(pieces)
    bit = 1
    while bit < len(pieces):
        swap = (me & bit) != 0
        pieces = [jnp.where(swap, pieces[j ^ bit], piece) for j, piece in enumerate(pieces)]
        bit *= 2
    return jnp.stack(pieces)


def take(array, index, axis):
    return lax.dynamic_index_in_dim(array, index, axis, keepdims=False)


def head_parts(block, scale, third_low):
    lane = lax.broadcasted_iota(jnp.int32, (block.shape[0], 128), 1)
    first = wide(block[:, 0:128]) * scale
    third = wide(block[:, 128:256]) * scale
    third = jnp.where(lane < 64, third, 0.0)
    if not third_low:
        third = pltpu.roll(third, 64, 1)
    return (
        rounded(jnp.where(lane < 64, first, 0.0)),
        rounded(jnp.where(lane >= 64, first, 0.0)),
        rounded(third),
    )


def key_tiles(ref, start, size):
    rows = pl.ds(start, size)
    keys = ref[rows, 0:128]
    values = ref[rows, 128:256]
    third = ref[rows, 256:384]
    return (keys, keys, third), (values, values, third)


def allowed_keys(key_first, query_first, prefix_len, shape):
    key_pos = key_first + lax.broadcasted_iota(jnp.int32, shape, 0)
    query_pos = query_first + lax.broadcasted_iota(jnp.int32, shape, 1)
    return (key_pos <= query_pos) | (key_pos < prefix_len)


def each_block(table, refs, rows, query_first, prefix_len, work):
    count = refs[0].shape[0] // rows
    for part, ref in enumerate(refs):

        def step(local, carry, part=part, ref=ref):
            block = part * count + local
            key_first = table[block]
            last = key_first + rows - 1
            seen = (key_first <= query_first + rows - 1) | (key_first < prefix_len)
            whole = (last <= query_first) | (last < prefix_len)

            @pl.when(seen & whole)
            def _():
                work(ref, local * rows, block, key_first, False)

            @pl.when(seen & jnp.logical_not(whole))
            def _():
                work(ref, local * rows, block, key_first, True)

            return carry

        lax.fori_loop(0, count, step, 0)


def forward_kernel(rows, parts, first, last, table, query_in, *refs):
    refs = list(refs)
    sides = [refs.pop(0) for _ in range(parts)]
    if not first:
        accum_in, stats_in = refs.pop(0), refs.pop(0)
    out, state, query, accum, stats = refs
    m = pl.program_id(0)
    blocks = parts * (sides[0].shape[0] // rows)
    query_first = table[blocks + m]
    prefix_len = table[blocks + GROUPS]
    for head, part in enumerate(head_parts(query_in[0], SCALE, True)):
        query[head] = part
    if first:
        accum[...] = jnp.zeros_like(accum)
        stats[0:8, :] = jnp.full((8, rows), NEGATIVE, jnp.float32)
        stats[8:16, :] = jnp.zeros((8, rows), jnp.float32)
    else:
        accum[...] = accum_in[0]
        stats[...] = stats_in[0]

    def work(ref, start, block, key_first, masked):
        keys, values = key_tiles(ref, start, rows)
        if masked:
            mask = allowed_keys(key_first, query_first, prefix_len, (rows, rows))
        for head in range(GROUP_HEADS):
            scores = lax.dot_general(
                keys[head], query[head], LANES_IN, preferred_element_type=jnp.float32
            )
            if masked:
                scores = jnp.where(mask, scores, NEGATIVE)
            old = stats[head : head + 1, :]
            top = jnp.maximum(old, jnp.max(scores, axis=0, keepdims=True))
            weights = jnp.exp(scores - top)
            shrink = jnp.exp(old - top)
            stats[head : head + 1, :] = top
            stats[8 + head : 9 + head, :] = stats[8 + head : 9 + head, :] * shrink + jnp.sum(
                weights, axis=0, keepdims=True
            )
            accum[head] = accum[head] * shrink + lax.dot_general(
                values[head], rounded(weights), ROWS_IN, preferred_element_type=jnp.float32
            )

    each_block(table, sides, rows, query_first, prefix_len, work)
    if not last:
        out[0] = accum[...]
        state[0] = stats[...]
        return
    totals = stats[8 : 8 + GROUP_HEADS, :]
    final = [accum[head] / totals[head : head + 1, :] for head in range(GROUP_HEADS)]
    line = lax.broadcasted_iota(jnp.int32, (128, rows), 0)
    out[0, :, 0:128] = jnp.where(line < 64, final[0], final[1]).T
    third = jnp.concatenate([final[2][64:128], jnp.zeros((64, rows), jnp.float32)], axis=0)
    out[0, :, 128:256] = third.T
    state[0] = jnp.zeros((8, rows), jnp.float32)
    state[0, 0:GROUP_HEADS, :] = stats[0:GROUP_HEADS, :] + jnp.log(totals)


def backward_kernel(rows, parts, first, last, table, query_in, dout, state, *refs):
    refs = list(refs)
    sides = [refs.pop(0) for _ in range(parts)]
    carried = refs.pop(0)
    grads_out = [refs.pop(0) for _ in range(parts)]
    qgrad_out = refs.pop(0)
    if first:
        state_out = refs.pop(0)
    query, accum, qgrad, lines = refs
    m = pl.program_id(0)
    count = sides[0].shape[0] // rows
    blocks = parts * count
    query_first = table[blocks + m]
    prefix_len = table[blocks + GROUPS]

    @pl.when(m == 0)
    def _():
        def clear(index, carry):
            accum[pl.ds(index * rows, rows), :] = jnp.zeros((rows, SIDE), jnp.float32)
            return carry

        lax.fori_loop(0, blocks, clear, 0)

    for head, part in enumerate(head_parts(query_in[0], SCALE, True)):
        query[head] = part
    for head, part in enumerate(head_parts(dout[0], 1.0, False)):
        query[GROUP_HEADS + head] = part
    lines[...] = state[0]
    if first:
        pair_prod = (wide(dout[0, :, 0:128]) * carried[0, :, 0:128]).T
        third_prod = (wide(dout[0, :, 128:256]) * carried[0, :, 128:256]).T
        lines[3:4, :] = jnp.sum(pair_prod[0:64], axis=0, keepdims=True)
        lines[4:5, :] = jnp.sum(pair_prod[64:128], axis=0, keepdims=True)
        lines[5:6, :] = jnp.sum(third_prod[0:64], axis=0, keepdims=True)
        state_out[0] = lines[...]
        qgrad[...] = jnp.zeros_like(qgrad)
    else:
        qgrad[...] = carried[0]

    def work(ref, start, block, key_first, masked):
        keys, values = key_tiles(ref, start, rows)
        if masked:
            mask = allowed_keys(key_first, query_first, prefix_len, (rows, rows))
        key_parts, value_parts = [], []
        for head in range(GROUP_HEADS):
            scores = lax.dot_general(
                keys[head], query[head], LANES_IN, preferred_element_type=jnp.float32
            )
            if masked:
                scores = jnp.where(mask, scores, NEGATIVE)
            probs = jnp.exp(scores - lines[head : head + 1, :])
            slopes = lax.dot_general(
                values[head],
                query[GROUP_HEADS + head],
                LANES_IN,
                preferred_element_type=jnp.float32,
            )
            low = rounded(probs * (slopes - lines[3 + head : 4 + head, :]))
            value_parts.append(matmul(rounded(probs), query[GROUP_HEADS + head]))
            key_parts.append(matmul(low, query[head]))
            qgrad[head] += lax.dot_general(
                keys[head], low, ROWS_IN, preferred_element_type=jnp.float32
            )
        span = pl.ds(pl.multiple_of(block * rows, rows), rows)
        accum[span, 0:128] += key_parts[0] + key_parts[1]
        accum[span, 128:256] += value_parts[0] + value_parts[1]
        accum[span, 256:384] += key_parts[2] + value_parts[2]

    each_block(table, sides, rows, query_first, prefix_len, work)
    if last:
        line = lax.broadcasted_iota(jnp.int32, (128, rows), 0)
        qgrad_out[0, :, 0:128] = rounded(jnp.where(line < 64, qgrad[0], qgrad[1]).T * SCALE)
        qgrad_out[0, :, 128:256] = rounded(jnp.where(line < 64, qgrad[2], 0.0).T * SCALE)
    else:
        qgrad_out[0] = qgrad[...]

    @pl.when(m == GROUPS - 1)
    def _():
        for part, ref in enumerate(grads_out):

            def write(index, carry, part=part, ref=ref):
                source = pl.ds((part * count + index) * rows, rows)
                ref[pl.ds(index * rows, rows), :] = rounded(accum[source, :])
                return carry

            lax.fori_loop(0, count, write, 0)


def whole(shape):
    return pl.BlockSpec(shape, lambda *_: (0,) * len(shape), pipeline_mode=pl.Buffered(1))


def slab(shape):
    return pl.BlockSpec((1,) + shape, lambda m, *_: (m,) + (0,) * len(shape))


def self_forward(table, queries, sides, carried, last):
    rows = queries.shape[1]
    parts, length = len(sides), sides[0].shape[0]
    pairs = GROUPS * parts * length // rows * GROUP_HEADS // 2
    accum, stats = (GROUP_HEADS, 128, rows), (16, rows)
    outs = [(rows, 256), (8, rows)] if last else [accum, stats]
    first = carried is None
    return pl.pallas_call(
        functools.partial(forward_kernel, rows, parts, first, last),
        grid_spec=pltpu.PrefetchScalarGridSpec(
            num_scalar_prefetch=1,
            grid=(GROUPS,),
            in_specs=[slab((rows, QUERY))]
            + [whole((length, SIDE))] * parts
            + ([] if first else [slab(accum), slab(stats)]),
            out_specs=[slab(shape) for shape in outs],
            scratch_shapes=[
                pltpu.VMEM((GROUP_HEADS, rows, 128), jnp.bfloat16),
                pltpu.VMEM(accum, jnp.float32),
                pltpu.VMEM(stats, jnp.float32),
            ],
        ),
        out_shape=[jax.ShapeDtypeStruct((GROUPS,) + shape, jnp.float32) for shape in outs],
        compiler_params=pltpu.CompilerParams(vmem_limit_bytes=VMEM_LIMIT),
        cost_estimate=pl.CostEstimate(
            flops=pairs * rows * rows * 128 * 16,
            bytes_accessed=4 * length * parts * SIDE,
            transcendentals=pairs * rows * rows,
        ),
        name="self_forward",
    )(table, queries, *sides, *(() if first else carried))


def self_backward(table, queries, dout, state, sides, carried, first, last):
    rows = queries.shape[1]
    parts, length = len(sides), sides[0].shape[0]
    pairs = GROUPS * parts * length // rows * GROUP_HEADS // 2
    slope = (GROUP_HEADS, 128, rows)
    outs = [jax.ShapeDtypeStruct((length, SIDE), jnp.bfloat16)] * parts
    out_specs = [whole((length, SIDE))] * parts
    if last:
        outs = outs + [jax.ShapeDtypeStruct((GROUPS, rows, QUERY), jnp.bfloat16)]
        out_specs = out_specs + [slab((rows, QUERY))]
    else:
        outs = outs + [jax.ShapeDtypeStruct((GROUPS,) + slope, jnp.float32)]
        out_specs = out_specs + [slab(slope)]
    if first:
        outs = outs + [jax.ShapeDtypeStruct((GROUPS, 8, rows), jnp.float32)]
        out_specs = out_specs + [slab((8, rows))]
    return pl.pallas_call(
        functools.partial(backward_kernel, rows, parts, first, last),
        grid_spec=pltpu.PrefetchScalarGridSpec(
            num_scalar_prefetch=1,
            grid=(GROUPS,),
            in_specs=[slab((rows, QUERY)), slab((rows, 256)), slab((8, rows))]
            + [whole((length, SIDE))] * parts
            + [slab((rows, 256)) if first else slab(slope)],
            out_specs=out_specs,
            scratch_shapes=[
                pltpu.VMEM((2 * GROUP_HEADS, rows, 128), jnp.bfloat16),
                pltpu.VMEM((parts * length, SIDE), jnp.float32),
                pltpu.VMEM(slope, jnp.float32),
                pltpu.VMEM((8, rows), jnp.float32),
            ],
        ),
        out_shape=outs,
        compiler_params=pltpu.CompilerParams(vmem_limit_bytes=VMEM_LIMIT),
        cost_estimate=pl.CostEstimate(
            flops=pairs * rows * rows * 128 * 20,
            bytes_accessed=8 * length * parts * SIDE,
            transcendentals=pairs * rows * rows,
        ),
        name="self_backward",
    )(table, queries, dout, state, *sides, carried)


def pair_heads(block, scale=1.0):
    lane = lax.broadcasted_iota(jnp.int32, block.shape, 1)
    values = wide(block) * scale
    return rounded(jnp.where(lane < 64, values, 0.0)), rounded(jnp.where(lane >= 64, values, 0.0))


def cross_forward_kernel(query, keys, values, out, lse):
    rows = query.shape[0]
    parts = pair_heads(query[...], SCALE)
    sides = []
    lse[0] = jnp.zeros((8, rows), jnp.float32)
    for head in range(2):
        scores = lax.dot_general(
            keys[...], parts[head], LANES_IN, preferred_element_type=jnp.float32
        )
        top = jnp.max(scores, axis=0, keepdims=True)
        weights = jnp.exp(scores - top)
        total = jnp.sum(weights, axis=0, keepdims=True)
        mixed = lax.dot_general(
            values[...], rounded(weights), ROWS_IN, preferred_element_type=jnp.float32
        )
        sides.append(mixed / total)
        lse[0, head : head + 1, :] = top + jnp.log(total)
    line = lax.broadcasted_iota(jnp.int32, (128, rows), 0)
    out[...] = rounded(jnp.where(line < 64, sides[0], sides[1]).T)


def cross_backward_kernel(query, keys, values, dout, lse, qgrad, kgrad, vgrad):
    rows = query.shape[0]
    parts = pair_heads(query[...], SCALE)
    grads = pair_heads(dout[...])
    sides, key_parts, value_parts = [], [], []
    for head in range(2):
        scores = lax.dot_general(
            keys[...], parts[head], LANES_IN, preferred_element_type=jnp.float32
        )
        probs = jnp.exp(scores - lse[0, head : head + 1, :])
        slopes = lax.dot_general(
            values[...], grads[head], LANES_IN, preferred_element_type=jnp.float32
        )
        delta = jnp.sum(probs * slopes, axis=0, keepdims=True)
        low = rounded(probs * (slopes - delta))
        value_parts.append(matmul(rounded(probs), grads[head]))
        key_parts.append(matmul(low, parts[head]))
        sides.append(lax.dot_general(keys[...], low, ROWS_IN, preferred_element_type=jnp.float32))
    line = lax.broadcasted_iota(jnp.int32, (128, rows), 0)
    qgrad[...] = rounded(jnp.where(line < 64, sides[0], sides[1]).T * SCALE)
    kgrad[...] = rounded(key_parts[0] + key_parts[1])
    vgrad[...] = rounded(value_parts[0] + value_parts[1])


def cross_forward(query, pair):
    rows, width = query.shape
    count = width // 128
    kept = pair.shape[0]
    return pl.pallas_call(
        cross_forward_kernel,
        grid=(count,),
        in_specs=[
            pl.BlockSpec((rows, 128), lambda i: (0, i)),
            pl.BlockSpec((kept, 128), lambda i: (0, i)),
            pl.BlockSpec((kept, 128), lambda i: (0, count + i)),
        ],
        out_specs=[
            pl.BlockSpec((rows, 128), lambda i: (0, i)),
            pl.BlockSpec((1, 8, rows), lambda i: (i, 0, 0)),
        ],
        out_shape=[
            jax.ShapeDtypeStruct((rows, width), jnp.bfloat16),
            jax.ShapeDtypeStruct((count, 8, rows), jnp.float32),
        ],
        compiler_params=pltpu.CompilerParams(vmem_limit_bytes=VMEM_LIMIT),
        cost_estimate=pl.CostEstimate(
            flops=8 * rows * kept * width, bytes_accessed=4 * kept * width, transcendentals=12 * rows * kept
        ),
        name="cross_forward",
    )(query, pair, pair)


def cross_backward(query, pair, dout, lse):
    rows, width = query.shape
    count = width // 128
    kept = pair.shape[0]
    return pl.pallas_call(
        cross_backward_kernel,
        grid=(count,),
        in_specs=[
            pl.BlockSpec((rows, 128), lambda i: (0, i)),
            pl.BlockSpec((kept, 128), lambda i: (0, i)),
            pl.BlockSpec((kept, 128), lambda i: (0, count + i)),
            pl.BlockSpec((rows, 128), lambda i: (0, i)),
            pl.BlockSpec((1, 8, rows), lambda i: (i, 0, 0)),
        ],
        out_specs=[
            pl.BlockSpec((rows, 128), lambda i: (0, i)),
            pl.BlockSpec((kept, 128), lambda i: (0, i)),
            pl.BlockSpec((kept, 128), lambda i: (0, i)),
        ],
        out_shape=[
            jax.ShapeDtypeStruct((rows, width), jnp.bfloat16),
            jax.ShapeDtypeStruct((kept, width), jnp.bfloat16),
            jax.ShapeDtypeStruct((kept, width), jnp.bfloat16),
        ],
        compiler_params=pltpu.CompilerParams(vmem_limit_bytes=VMEM_LIMIT),
        cost_estimate=pl.CostEstimate(
            flops=20 * rows * kept * width, bytes_accessed=8 * kept * width, transcendentals=12 * rows * kept
        ),
        name="cross_backward",
    )(query, pair, pair, dout, lse)


def pick_kernel(table, bank, out):
    i = pl.program_id(0)
    keep = table[pl.num_programs(0) + i]
    out[0] = jnp.where(keep > 0, bank[0], jnp.zeros_like(bank[0]))


def pick_rows(chunks, spots, found):
    count = spots.shape[0]
    size = chunks.shape[1:]
    table = jnp.concatenate([spots, found.astype(jnp.int32)])
    return pl.pallas_call(
        pick_kernel,
        grid_spec=pltpu.PrefetchScalarGridSpec(
            num_scalar_prefetch=1,
            grid=(count,),
            in_specs=[pl.BlockSpec((1,) + size, lambda i, t: (t[i], 0, 0))],
            out_specs=pl.BlockSpec((1,) + size, lambda i, t: (i, 0, 0)),
        ),
        out_shape=jax.ShapeDtypeStruct((count,) + size, chunks.dtype),
        name="pick_rows",
    )(table, chunks)


def place_kernel(count, table, grads, out):
    spot = pl.program_id(0)
    out[...] = jnp.zeros_like(out)
    for i in range(count):

        @pl.when(table[i] == spot)
        def _(i=i):
            out[0] += wide(grads[i])


def place_rows(grads, spots, chunks):
    count = spots.shape[0]
    size = grads.shape[1:]
    return pl.pallas_call(
        functools.partial(place_kernel, count),
        grid_spec=pltpu.PrefetchScalarGridSpec(
            num_scalar_prefetch=1,
            grid=(chunks,),
            in_specs=[whole((count,) + size)],
            out_specs=pl.BlockSpec((1,) + size, lambda n, t: (n, 0, 0)),
        ),
        out_shape=jax.ShapeDtypeStruct((chunks,) + size, jnp.float32),
        name="place_rows",
    )(spots, grads)


class Chain:
    def __init__(self, stages):
        self.stages = stages
        self.result = None
        self.pending = next(stages)

    def step(self, pending):
        try:
            self.pending = self.stages.send(pending)
        except StopIteration as stop:
            self.pending, self.result = (), stop.value


def meet(values, *chains):
    values, pending = lax.optimization_barrier((values, [chain.pending for chain in chains]))
    for chain, arrays in zip(chains, pending):
        chain.step(arrays)
    return values


def settle(values, *chains):
    values, kept = lax.optimization_barrier((values, [chain.pending[0] for chain in chains]))
    for chain, array in zip(chains, kept):
        chain.pending = [array] + list(chain.pending[1:])
    return values


def total_of(arrays):
    total = wide(arrays[0])
    for array in arrays[1:]:
        total = total + wide(array)
    return total


def body(
    grid,
    tokens,
    cotangent,
    bank,
    prefix,
    blocks,
    self_qkv,
    self_out,
    cross_q,
    cross_kv,
    cross_out,
    ffn_in,
    ffn_out,
    gains,
    biases,
):
    Z, X, C, Y = grid.z, grid.x, grid.c, grid.y
    devices = grid.seq * Y
    seq_index = lax.axis_index("seq")
    me = {
        "y": lax.axis_index("batch"),
        "c": seq_index % C,
        "x": (seq_index // C) % X,
        "z": seq_index // (C * X),
        "h": seq_index // (2 * C * X),
        "l": seq_index // (C * X) % 2,
    }
    my_z, my_x, my_c = me["z"], me["x"], me["c"]
    rows, width = tokens.shape[1:]
    hidden = ffn_in.shape[1]
    part = width // devices
    fan = hidden // width
    inputs = tokens[0]

    def parted(array, axis, place):
        size = getattr(grid, axis)
        kept = [take(array, me[axis], place)]
        for shift in range(1, size):
            kept.append(grid.send(take(array, me[axis] ^ shift, place), axis, shift))
        return kept

    def reduction(array, axes, lead=0, final=True):
        names = ["h", "l", "x", "c", "y"]
        for axis in axes:
            place = lead + names.index(axis)
            names.remove(axis)
            arrays = yield parted(array, axis, place)
            total = total_of(arrays)
            array = rounded(total)
        return total if final else array

    def sharded(array):
        return array.reshape(2, 2, X, C, Y, array.shape[0] // devices, array.shape[1])

    grouped = self_qkv.reshape(part, 3, GROUPS, GROUP_WIDTH)
    extra = jnp.stack([biases[3], biases[4]], axis=1)
    extra = jnp.broadcast_to(
        jnp.pad(extra, ((0, 0), (0, QUERY - GROUP_WIDTH - 2)))[:, None],
        (part, GROUPS, QUERY - GROUP_WIDTH),
    )
    packed = jnp.concatenate(
        [
            grouped[:, 0],
            extra,
            grouped[:, 1, :, :128],
            grouped[:, 2, :, :128],
            grouped[:, 1, :, 128:],
            grouped[:, 2, :, 128:],
        ],
        axis=2,
    ).transpose(1, 0, 2)
    packed, later = lax.optimization_barrier(
        (packed, (self_out, cross_q, cross_out, cross_kv, ffn_in, ffn_out, gains, biases))
    )
    self_out, cross_q, cross_out, cross_kv, ffn_in, ffn_out, gains, biases = later
    pieces = parted(packed, "z", 0)

    small = jnp.concatenate([gains, biases], axis=0).T
    small = jnp.pad(small, ((0, 0), (0, 128 - small.shape[1])))
    first_pack = jnp.concatenate([self_out, cross_q, cross_out, cross_kv, small], axis=1)
    inner_columns = (
        ffn_in.reshape(part, devices, fan, part).transpose(0, 2, 1, 3).reshape(part, hidden)
    )
    outer_blocks = ffn_out.reshape(fan, part, width).transpose(1, 0, 2).reshape(part, hidden)
    second_pack = jnp.stack([inner_columns, outer_blocks])
    first_all = lax.all_gather(first_pack, ("seq", "batch"), axis=0, tiled=True)
    second_all = lax.all_gather(second_pack, ("seq", "batch"), axis=1, tiled=True)

    pieces, inputs, bank_rows = lax.optimization_barrier((pieces, inputs, bank[0]))
    across = grid.send(inputs, "h", 1)
    beside = grid.send(inputs, "l", 1)

    chunk = BANK_BLOCK * blocks.shape[1] // grid.seq
    per_block = BANK_BLOCK // chunk
    local_chunks = bank.shape[1] // chunk
    local_blocks = bank.shape[1] // BANK_BLOCK
    bank_chunks = bank_rows.reshape(local_chunks, chunk, width)
    home = seq_index * local_blocks
    every = jnp.arange(grid.seq, dtype=jnp.int32)
    wanted = jnp.take(blocks[0], every // per_block) - home
    found = (wanted >= 0) & (wanted < local_blocks)
    spots = jnp.where(found, wanted * per_block + every % per_block, 0)
    picked = pick_rows(bank_chunks, spots, found).reshape(2, 2, X, C, 1, chunk, width)

    def spreading(own):
        array = own
        for axis in "hlxc":
            size = getattr(grid, axis)
            array = jnp.stack((yield [array] + [grid.send(array, axis, m) for m in range(1, size)]))
        return array

    def retrieval():
        own = (yield from reduction(picked, "cxlh", final=False))[0]
        every_row = yield from spreading(own)
        return own, every_row.reshape(grid.seq * chunk, width)

    retrieve = Chain(retrieval())
    gathered = in_order(pieces, my_z)
    for axis in "yxc":
        pieces = [gathered] + [grid.send(gathered, axis, m) for m in range(1, getattr(grid, axis))]
        if axis == "x":
            pieces, across, beside = meet((pieces, across, beside), retrieve)
        gathered = in_order(pieces, me[axis])
    token_parts = [inputs, beside, across, grid.send(across, "l", 1)]
    qkv_group = gathered.transpose(3, 1, 0, 2, 4, 5).reshape(width, PACK)
    column = jnp.arange(PACK, dtype=jnp.int32)
    real = (column < GROUP_WIDTH) | (column >= QUERY)
    is_query = column < GROUP_WIDTH
    is_pair_value = (column >= QUERY + 128) & (column < QUERY + 256)
    is_value = is_pair_value | (column >= QUERY + 320)
    local = jnp.where(is_query, column, column - jnp.where(is_pair_value, QUERY + 128, QUERY + 192))
    line = jnp.where(is_query | is_value, local + my_z * GROUP_WIDTH, -1)
    chosen = (jnp.arange(width, dtype=jnp.int32)[:, None] == line[None]).astype(jnp.bfloat16)
    picked_bias = weight_grad(qkv_group[:, GROUP_WIDTH:QUERY], chosen)
    qkv_bias = jnp.where(is_query, picked_bias[0], picked_bias[1])
    qkv_weight = jnp.where(real[None], qkv_group, jnp.zeros_like(qkv_group))

    qkv_weight, qkv_bias, token_parts = meet((qkv_weight, qkv_bias, token_parts), retrieve)

    token_column = jnp.concatenate(token_parts, axis=0)
    own_queries = rounded(matmul(token_column, qkv_weight[:, :QUERY]) + qkv_bias[:QUERY])
    own_side = rounded(matmul(token_column, qkv_weight[:, QUERY:]) + qkv_bias[QUERY:])
    own_queries = own_queries.reshape(GROUPS, rows, QUERY)

    far_queries = grid.send(own_queries[1::2], "z", 0, mirror=True)
    near_other = grid.send(own_side, "c", 1)
    far_queries, side = lax.optimization_barrier((far_queries, own_side))
    far_own = [grid.send(side, "x", m) for m in range(1, X)]
    queries = jnp.stack(
        [own_queries[m] if m % 2 == 0 else far_queries[m // 2] for m in range(GROUPS)]
    )

    turn = jnp.arange(GROUPS, dtype=jnp.int32)
    turn_z = my_z ^ turn

    def key_firsts(x, c):
        return ((turn_z * X + x) * C + c) * rows

    query_firsts = jnp.where(
        turn % 2 == 0, key_firsts(my_x, my_c), key_firsts(X - 1 - my_x, C - 1 - my_c)
    )

    def table_of(shifts, c):
        keys = [key_firsts(my_x ^ m, c) for m in shifts]
        return jnp.concatenate(keys + [query_firsts, prefix]).astype(jnp.int32)

    far = list(range(1, X))
    tables = {
        "near own": table_of([0], my_c),
        "near other": table_of([0], C - 1 - my_c),
        "far own": table_of(far, my_c),
        "far other": table_of(far, C - 1 - my_c),
    }

    carry = self_forward(tables["near own"], queries, [own_side], None, False)
    carry, near_other = meet((carry, near_other), retrieve)
    carry = self_forward(tables["near other"], queries, [near_other], carry, False)
    carry, far_own = meet((carry, far_own), retrieve)
    far_other = [grid.send(side, "c", 1) for side in far_own]
    carry = self_forward(tables["far own"], queries, far_own, carry, False)
    carry, far_other = meet((carry, far_other), retrieve)
    attention, lse = self_forward(tables["far other"], queries, far_other, carry, True)
    attention, lse = meet((attention, lse), retrieve)
    attention_mine = rounded(attention)

    def swapped(array, m):
        return grid.send(array, "z", m, mirror=m % 2 == 1)

    pieces = [attention_mine[0]] + [swapped(attention_mine[m], m) for m in range(1, Z)]
    pieces = meet(pieces, retrieve)
    retrieve.step(retrieve.pending)
    own_rows, all_rows = retrieve.result
    attention_low = (
        in_order(pieces, my_z)[:, :, :GROUP_WIDTH].transpose(1, 0, 2).reshape(rows, width)
    )

    selfout_full = first_all[:, :width]
    crossq_full = first_all[:, width : 2 * width]
    crossout_full = first_all[:, 2 * width : 3 * width]
    crosskv_full = first_all[:, 3 * width : 5 * width]
    small_full = wide(first_all[:, 5 * width :].T)
    gain = small_full[:3]
    bias = small_full[3:17]
    ffnin_full = second_all[0]
    outer = [second_all[1, :, f * width : (f + 1) * width] for f in range(fan)]
    inner_bias = bias[10:14].reshape(devices, fan, part).transpose(1, 0, 2).reshape(-1)

    resid_one = wide(inputs) + matmul(attention_low, selfout_full) + bias[5]
    hidden_one = layer_norm(resid_one, gain[0], bias[0])
    hidden_one_low = rounded(hidden_one)
    cross_query = rounded(matmul(hidden_one_low, crossq_full) + bias[6])
    cross_pair = rounded(
        matmul(all_rows, crosskv_full) + jnp.concatenate([jnp.zeros((width,), jnp.float32), bias[7]])
    )
    cross_att, cross_lse = cross_forward(cross_query, cross_pair)
    resid_two = hidden_one + matmul(cross_att, crossout_full) + bias[8]
    hidden_two = layer_norm(resid_two, gain[1], bias[1])
    hidden_two_low = rounded(hidden_two)
    inner = matmul(hidden_two_low, ffnin_full) + inner_bias
    activated = rounded(gelu_exact(inner))

    def fan_part(array, f):
        return array[:, f * width : (f + 1) * width]

    resid_three = hidden_two + bias[9]
    for f in range(fan):
        resid_three = resid_three + matmul(fan_part(activated, f), outer[f])
    output = layer_norm(resid_three, gain[2], bias[2])

    _unused, norm_three = jax.vjp(layer_norm, resid_three, gain[2], bias[2])
    dresid_three, dgain_three, dshift_three = norm_three(wide(cotangent[0]))
    douter_low = rounded(dresid_three)
    grad_ffnout = rounded(weight_grad(activated, douter_low))
    reduce_ffnout = Chain(
        reduction(grad_ffnout.reshape(fan, 2, 2, X, C, Y, part, width), "cyxlh", lead=1)
    )
    _unused, gelu_back = jax.vjp(gelu_exact, inner)
    dactivated = jnp.concatenate([back_matmul(douter_low, block) for block in outer], axis=1)
    dinner_low = rounded(gelu_back(dactivated)[0])
    grad_ffnin = rounded(weight_grad(hidden_two_low, dinner_low))
    reduce_ffnin = Chain(reduction(sharded(grad_ffnin), "cyxlh"))

    _unused, norm_two = jax.vjp(layer_norm, resid_two, gain[1], bias[1])
    dresid_two, dgain_two, dshift_two = norm_two(dresid_three + back_matmul(dinner_low, ffnin_full))
    dcross_low = rounded(dresid_two)
    dcross_att = rounded(back_matmul(dcross_low, crossout_full))
    dcross_query, dcross_key, dcross_value = cross_backward(
        cross_query, cross_pair, dcross_att, cross_lse
    )
    dcross_query, dcross_key, dcross_value = meet(
        (dcross_query, dcross_key, dcross_value), reduce_ffnout, reduce_ffnin
    )

    dcross_all = jnp.concatenate([dcross_key, dcross_value], axis=1)
    dcross_all = dcross_all.reshape(C, X, 2, 2, chunk, 2 * width)

    def unspreading(array):
        for axis in "cxlh":
            size = getattr(grid, axis)
            arrays = yield [array[0]] + [grid.send(array[m], axis, m) for m in range(1, size)]
            array = rounded(total_of(arrays))
        return array

    unspread = Chain(unspreading(dcross_all))

    _unused, norm_one = jax.vjp(layer_norm, resid_one, gain[0], bias[0])
    dresid_one, dgain_one, dshift_one = norm_one(dresid_two + back_matmul(dcross_query, crossq_full))
    dbranch_low = rounded(dresid_one)
    datt_low = rounded(back_matmul(dbranch_low, selfout_full))
    datt_groups = jnp.pad(
        datt_low.reshape(rows, GROUPS, GROUP_WIDTH).transpose(1, 0, 2),
        ((0, 0), (0, 0), (0, 256 - GROUP_WIDTH)),
    )
    pieces = [take(datt_groups, my_z, 0)]
    for m in range(1, Z):
        pieces.append(swapped(take(datt_groups, my_z ^ m, 0), m))
    grad_mid = jnp.stack(
        [
            rounded(weight_grad(attention_low, dbranch_low)),
            rounded(weight_grad(hidden_one_low, dcross_query)),
            rounded(weight_grad(cross_att, dcross_low)),
        ]
    )
    grad_mid, pieces = meet((grad_mid, pieces), unspread)
    reduce_mid = Chain(reduction(grad_mid.reshape(3, 2, 2, X, C, Y, part, width), "cyxlh", lead=1))
    dout = jnp.stack(pieces)

    *far_other_grad, slopes, state = self_backward(
        tables["far other"], queries, dout, lse, far_other, attention, True, False
    )
    far_other_grad, slopes = meet(
        (far_other_grad, slopes), reduce_ffnout, reduce_mid, unspread
    )
    far_moved = [grid.send(grad, "c", 1) for grad in far_other_grad]
    *far_own_grad, slopes = self_backward(
        tables["far own"], queries, dout, state, far_own, slopes, False, False
    )
    far_own_grad, far_moved, slopes = meet(
        (far_own_grad, far_moved, slopes), unspread, reduce_ffnout, reduce_ffnin
    )
    far_grad = [rounded(total_of(pair)) for pair in zip(far_own_grad, far_moved)]
    far_moved = [grid.send(grad, "x", m) for m, grad in zip(far, far_grad)]
    near_other_grad, slopes = self_backward(
        tables["near other"], queries, dout, state, [near_other], slopes, False, False
    )
    near_other_grad, far_moved, slopes = meet(
        (near_other_grad, far_moved, slopes), unspread, reduce_ffnout, reduce_ffnin, reduce_mid
    )
    near_moved = grid.send(near_other_grad, "c", 1)

    dcross_pair = unspread.result
    bias_rows = jnp.stack(
        [
            dgain_one,
            dgain_two,
            dgain_three,
            dshift_one,
            dshift_two,
            dshift_three,
            column_sums(dbranch_low),
            column_sums(dcross_query),
            column_sums(dcross_pair[:, width:]),
            column_sums(dcross_low),
            column_sums(douter_low),
        ]
    )
    inner_sums = column_sums(dinner_low).reshape(fan, devices, part).transpose(1, 0, 2)
    bias_rows = jnp.concatenate([bias_rows, inner_sums.reshape(fan, width)], axis=0)
    bias_columns = jnp.pad(rounded(bias_rows.T), ((0, 0), (0, 128 - bias_rows.shape[0])))
    grad_late = jnp.concatenate([rounded(weight_grad(own_rows, dcross_pair)), bias_columns], axis=1)
    reduce_late = Chain(reduction(sharded(grad_late), "cyxlh"))
    spread_back = Chain(spreading(rounded(back_matmul(dcross_pair, crosskv_full))))

    slopes = settle(slopes, reduce_late, spread_back, reduce_ffnin, reduce_mid)
    near_own_grad, query_grad = self_backward(
        tables["near own"], queries, dout, state, [own_side], slopes, False, True
    )
    near_own_grad, near_moved, query_grad = meet(
        (near_own_grad, near_moved, query_grad), reduce_late, spread_back, reduce_mid
    )

    far_query_grad = grid.send(query_grad[1::2], "z", 0, mirror=True)
    side_grad = rounded(total_of([near_own_grad, near_moved] + far_moved))
    query_grad = jnp.stack(
        [query_grad[m] if m % 2 == 0 else far_query_grad[m // 2] for m in range(GROUPS)]
    )
    dqkv = jnp.concatenate([query_grad.reshape(GROUPS * rows, QUERY), side_grad], axis=1)
    far_tokens_grad = rounded(back_matmul(dqkv[rows:], qkv_weight)).reshape(Z - 1, rows, width)
    dqkv, far_tokens_grad = lax.optimization_barrier((dqkv, far_tokens_grad))
    third = grid.send(far_tokens_grad[2], "l", 1)
    grad_group = weight_grad(token_column, dqkv)
    sums = jnp.sum(wide(dqkv), axis=0)
    sums = jnp.stack([jnp.where(is_query, sums, 0.0), jnp.where(is_value, sums, 0.0)])
    sums = jnp.pad(rounded(sums), ((0, QUERY - GROUP_WIDTH - 2), (0, 0)))
    grad_group = jnp.concatenate(
        [grad_group[:, :GROUP_WIDTH], back_matmul(chosen, sums), grad_group[:, QUERY:]], axis=1
    )
    reduce_group = Chain(reduction(sharded(rounded(grad_group)), "cyx", final=False))
    tokens_base = dresid_one + back_matmul(dqkv[:rows], qkv_weight)
    tokens_base, third, near_tokens_grad = meet(
        (tokens_base, third, far_tokens_grad[:2]),
        reduce_group,
        reduce_late,
        spread_back,
        reduce_mid,
        reduce_ffnin,
    )
    second = grid.send(rounded(total_of([near_tokens_grad[1], third])), "h", 1)
    tokens_base, second, last_tokens_grad = meet(
        (tokens_base, second, near_tokens_grad[0]),
        reduce_group,
        reduce_late,
        spread_back,
        reduce_mid,
    )
    first = grid.send(last_tokens_grad, "l", 1)
    tokens_base, second, first = meet(
        (tokens_base, second, first), reduce_group, reduce_late, spread_back
    )
    drows = spread_back.result
    meet((), reduce_late, reduce_ffnout, reduce_ffnin)
    pieces = parted(reduce_group.result.reshape(Z, part, PACK), "z", 0)
    drows, pieces[0] = lax.optimization_barrier((drows, pieces[0]))
    tokens_grad = total_of([tokens_base, first, second])

    spot = jnp.arange(grid.seq, dtype=jnp.int32)
    spot_z = my_z ^ (spot % 2 * 2 + spot // 2 % 2)
    source = (spot_z * X + (my_x ^ (spot // Z % X))) * C + (my_c ^ (spot // (Z * X)))
    target = jnp.take(blocks[0], source // per_block) - home
    inside = (target >= 0) & (target < local_blocks)
    places = jnp.where(inside, target * per_block + source % per_block, -1)
    drows = drows.reshape(grid.seq, chunk, width)
    bank_grad = place_rows(drows, places, local_chunks).reshape(bank.shape[1], width)

    grad_groups = wide(in_order(pieces, my_z))
    sides = grad_groups[:, :, QUERY:]
    out_qkv = jnp.stack(
        [
            grad_groups[:, :, :GROUP_WIDTH],
            jnp.concatenate([sides[:, :, :128], sides[:, :, 256:320]], axis=2),
            jnp.concatenate([sides[:, :, 128:256], sides[:, :, 320:384]], axis=2),
        ]
    )
    out_qkv = out_qkv.transpose(2, 0, 1, 3).reshape(part, 3 * width)
    late_bias = jnp.sum(grad_groups[:, :, GROUP_WIDTH : GROUP_WIDTH + 2], axis=0)

    out_late, out_mid = reduce_late.result, reduce_mid.result
    out_ffnin = (
        reduce_ffnin.result.reshape(part, fan, devices, part)
        .transpose(0, 2, 1, 3)
        .reshape(part, hidden)
    )
    out_small = out_late[:, 2 * width :].T
    bias_grad = jnp.concatenate([out_small[3:6], late_bias.T, out_small[6:15]], axis=0)
    return (
        rounded(output)[None],
        tokens_grad[None],
        bank_grad[None],
        out_qkv,
        out_mid[0],
        out_mid[1],
        out_late[:, : 2 * width],
        out_mid[2],
        out_ffnin,
        reduce_ffnout.result.reshape(fan * part, width),
        out_small[:3],
        bias_grad,
    )


def solution(mesh):
    split = P("batch", "seq", None)
    shard = P(("seq", "batch"), None)
    flat = P(None, ("seq", "batch"))
    return jax.shard_map(
        functools.partial(body, Grid(mesh)),
        mesh=mesh,
        in_specs=(split, split, split, P("batch"), P("batch", None)) + (shard,) * 7 + (flat, flat),
        out_specs=(split, split, split) + (shard,) * 7 + (flat, flat),
        check_vma=False,
    )
```

```python
import functools

import jax
import jax.numpy as jnp
from jax import lax
from jax.experimental import pallas as pl
from jax.experimental.pallas import tpu as pltpu
from jax.sharding import PartitionSpec as P

HEADS = 12
HEAD_DIM = 64
BANK_BLOCK = 128
GROUPS = 4
GROUP_HEADS = HEADS // GROUPS
GROUP_WIDTH = GROUP_HEADS * HEAD_DIM
QUERY, SIDE = 256, 384
PACK = QUERY + SIDE
EPSILON = 1e-05
NEGATIVE = -1e30
SCALE = HEAD_DIM ** (-0.5)
LANES_IN = (((1,), (1,)), ((), ()))
ROWS_IN = (((0,), (0,)), ((), ()))
VMEM_LIMIT = 60 * 1024 * 1024


def layer_norm(values, gain, shift):
    centered = values - jnp.mean(values, axis=-1, keepdims=True)
    variance = jnp.mean(centered * centered, axis=-1, keepdims=True)
    return centered * lax.rsqrt(variance + EPSILON) * gain + shift


def gelu_exact(values):
    return jax.nn.gelu(values, approximate=False)


def rounded(values):
    return values.astype(jnp.bfloat16)


def wide(values):
    return values.astype(jnp.float32)


def matmul(left, right):
    return jnp.dot(left, right, preferred_element_type=jnp.float32)


def weight_grad(left, right):
    return lax.dot_general(left, right, ROWS_IN, preferred_element_type=jnp.float32)


def back_matmul(left, right):
    return lax.dot_general(left, right, LANES_IN, preferred_element_type=jnp.float32)


def column_sums(values):
    return jnp.sum(wide(values), axis=0)


class Grid:
    def __init__(self, mesh):
        self.seq = mesh.shape["seq"]
        self.y = mesh.shape["batch"]
        self.z = GROUPS
        self.c = self.h = self.l = 2
        self.x = self.seq // (self.z * self.c)

    def coords(self, index):
        spot, y = divmod(index, self.y)
        spot, c = divmod(spot, self.c)
        z, x = divmod(spot, self.x)
        return z, x, c, y

    def index(self, z, x, c, y):
        return ((z * self.x + x) * self.c + c) * self.y + y

    def send(self, array, axis, shift, mirror=False):
        if axis in "hl":
            axis, shift = "z", shift * (2 if axis == "h" else 1)
        place = "zxcy".index(axis)
        pairs = []
        for index in range(self.seq * self.y):
            spot = list(self.coords(index))
            spot[place] ^= shift
            if mirror:
                spot[1], spot[2] = self.x - 1 - spot[1], self.c - 1 - spot[2]
            pairs.append((index, self.index(*spot)))
        return lax.ppermute(array, ("seq", "batch"), pairs)


def in_order(pieces, me):
    pieces = list(pieces)
    bit = 1
    while bit < len(pieces):
        swap = (me & bit) != 0
        pieces = [jnp.where(swap, pieces[j ^ bit], piece) for j, piece in enumerate(pieces)]
        bit *= 2
    return jnp.stack(pieces)


def take(array, index, axis):
    return lax.dynamic_index_in_dim(array, index, axis, keepdims=False)


def head_parts(block, scale, third_low):
    lane = lax.broadcasted_iota(jnp.int32, (block.shape[0], 128), 1)
    first = wide(block[:, 0:128]) * scale
    third = wide(block[:, 128:256]) * scale
    third = jnp.where(lane < 64, third, 0.0)
    if not third_low:
        third = pltpu.roll(third, 64, 1)
    return (
        rounded(jnp.where(lane < 64, first, 0.0)),
        rounded(jnp.where(lane >= 64, first, 0.0)),
        rounded(third),
    )


def key_tiles(ref, start, size):
    rows = pl.ds(start, size)
    keys = ref[rows, 0:128]
    values = ref[rows, 128:256]
    third = ref[rows, 256:384]
    return (keys, keys, third), (values, values, third)


def allowed_keys(key_first, query_first, prefix_len, shape):
    key_pos = key_first + lax.broadcasted_iota(jnp.int32, shape, 0)
    query_pos = query_first + lax.broadcasted_iota(jnp.int32, shape, 1)
    return (key_pos <= query_pos) | (key_pos < prefix_len)


def each_block(table, refs, rows, query_first, prefix_len, work):
    count = refs[0].shape[0] // rows
    for part, ref in enumerate(refs):

        def step(local, carry, part=part, ref=ref):
            block = part * count + local
            key_first = table[block]
            last = key_first + rows - 1
            seen = (key_first <= query_first + rows - 1) | (key_first < prefix_len)
            whole = (last <= query_first) | (last < prefix_len)

            @pl.when(seen & whole)
            def _():
                work(ref, local * rows, block, key_first, False)

            @pl.when(seen & jnp.logical_not(whole))
            def _():
                work(ref, local * rows, block, key_first, True)

            return carry

        lax.fori_loop(0, count, step, 0)


def forward_kernel(rows, parts, first, last, table, query_in, *refs):
    refs = list(refs)
    sides = [refs.pop(0) for _ in range(parts)]
    if not first:
        accum_in, stats_in = refs.pop(0), refs.pop(0)
    out, state, query, accum, stats = refs
    m = pl.program_id(0)
    blocks = parts * (sides[0].shape[0] // rows)
    query_first = table[blocks + m]
    prefix_len = table[blocks + GROUPS]
    for head, part in enumerate(head_parts(query_in[0], SCALE, True)):
        query[head] = part
    if first:
        accum[...] = jnp.zeros_like(accum)
        stats[0:8, :] = jnp.full((8, rows), NEGATIVE, jnp.float32)
        stats[8:16, :] = jnp.zeros((8, rows), jnp.float32)
    else:
        accum[...] = accum_in[0]
        stats[...] = stats_in[0]

    def work(ref, start, block, key_first, masked):
        keys, values = key_tiles(ref, start, rows)
        if masked:
            mask = allowed_keys(key_first, query_first, prefix_len, (rows, rows))
        for head in range(GROUP_HEADS):
            scores = lax.dot_general(
                keys[head], query[head], LANES_IN, preferred_element_type=jnp.float32
            )
            if masked:
                scores = jnp.where(mask, scores, NEGATIVE)
            old = stats[head : head + 1, :]
            top = jnp.maximum(old, jnp.max(scores, axis=0, keepdims=True))
            weights = jnp.exp(scores - top)
            shrink = jnp.exp(old - top)
            stats[head : head + 1, :] = top
            stats[8 + head : 9 + head, :] = stats[8 + head : 9 + head, :] * shrink + jnp.sum(
                weights, axis=0, keepdims=True
            )
            accum[head] = accum[head] * shrink + lax.dot_general(
                values[head], rounded(weights), ROWS_IN, preferred_element_type=jnp.float32
            )

    each_block(table, sides, rows, query_first, prefix_len, work)
    if not last:
        out[0] = accum[...]
        state[0] = stats[...]
        return
    totals = stats[8 : 8 + GROUP_HEADS, :]
    final = [accum[head] / totals[head : head + 1, :] for head in range(GROUP_HEADS)]
    line = lax.broadcasted_iota(jnp.int32, (128, rows), 0)
    out[0, :, 0:128] = jnp.where(line < 64, final[0], final[1]).T
    third = jnp.concatenate([final[2][64:128], jnp.zeros((64, rows), jnp.float32)], axis=0)
    out[0, :, 128:256] = third.T
    state[0] = jnp.zeros((8, rows), jnp.float32)
    state[0, 0:GROUP_HEADS, :] = stats[0:GROUP_HEADS, :] + jnp.log(totals)


def backward_kernel(rows, parts, first, last, table, query_in, dout, state, *refs):
    refs = list(refs)
    sides = [refs.pop(0) for _ in range(parts)]
    carried = refs.pop(0)
    grads_out = [refs.pop(0) for _ in range(parts)]
    qgrad_out = refs.pop(0)
    if first:
        state_out = refs.pop(0)
    query, accum, qgrad, lines = refs
    m = pl.program_id(0)
    count = sides[0].shape[0] // rows
    blocks = parts * count
    query_first = table[blocks + m]
    prefix_len = table[blocks + GROUPS]

    @pl.when(m == 0)
    def _():
        def clear(index, carry):
            accum[pl.ds(index * rows, rows), :] = jnp.zeros((rows, SIDE), jnp.float32)
            return carry

        lax.fori_loop(0, blocks, clear, 0)

    for head, part in enumerate(head_parts(query_in[0], SCALE, True)):
        query[head] = part
    for head, part in enumerate(head_parts(dout[0], 1.0, False)):
        query[GROUP_HEADS + head] = part
    lines[...] = state[0]
    if first:
        pair_prod = (wide(dout[0, :, 0:128]) * carried[0, :, 0:128]).T
        third_prod = (wide(dout[0, :, 128:256]) * carried[0, :, 128:256]).T
        lines[3:4, :] = jnp.sum(pair_prod[0:64], axis=0, keepdims=True)
        lines[4:5, :] = jnp.sum(pair_prod[64:128], axis=0, keepdims=True)
        lines[5:6, :] = jnp.sum(third_prod[0:64], axis=0, keepdims=True)
        state_out[0] = lines[...]
        qgrad[...] = jnp.zeros_like(qgrad)
    else:
        qgrad[...] = carried[0]

    def work(ref, start, block, key_first, masked):
        keys, values = key_tiles(ref, start, rows)
        if masked:
            mask = allowed_keys(key_first, query_first, prefix_len, (rows, rows))
        key_parts, value_parts = [], []
        for head in range(GROUP_HEADS):
            scores = lax.dot_general(
                keys[head], query[head], LANES_IN, preferred_element_type=jnp.float32
            )
            if masked:
                scores = jnp.where(mask, scores, NEGATIVE)
            probs = jnp.exp(scores - lines[head : head + 1, :])
            slopes = lax.dot_general(
                values[head],
                query[GROUP_HEADS + head],
                LANES_IN,
                preferred_element_type=jnp.float32,
            )
            low = rounded(probs * (slopes - lines[3 + head : 4 + head, :]))
            value_parts.append(matmul(rounded(probs), query[GROUP_HEADS + head]))
            key_parts.append(matmul(low, query[head]))
            qgrad[head] += lax.dot_general(
                keys[head], low, ROWS_IN, preferred_element_type=jnp.float32
            )
        span = pl.ds(pl.multiple_of(block * rows, rows), rows)
        accum[span, 0:128] += key_parts[0] + key_parts[1]
        accum[span, 128:256] += value_parts[0] + value_parts[1]
        accum[span, 256:384] += key_parts[2] + value_parts[2]

    each_block(table, sides, rows, query_first, prefix_len, work)
    if last:
        line = lax.broadcasted_iota(jnp.int32, (128, rows), 0)
        qgrad_out[0, :, 0:128] = rounded(jnp.where(line < 64, qgrad[0], qgrad[1]).T * SCALE)
        qgrad_out[0, :, 128:256] = rounded(jnp.where(line < 64, qgrad[2], 0.0).T * SCALE)
    else:
        qgrad_out[0] = qgrad[...]

    @pl.when(m == GROUPS - 1)
    def _():
        for part, ref in enumerate(grads_out):

            def write(index, carry, part=part, ref=ref):
                source = pl.ds((part * count + index) * rows, rows)
                ref[pl.ds(index * rows, rows), :] = rounded(accum[source, :])
                return carry

            lax.fori_loop(0, count, write, 0)


def whole(shape):
    return pl.BlockSpec(shape, lambda *_: (0,) * len(shape), pipeline_mode=pl.Buffered(1))


def slab(shape):
    return pl.BlockSpec((1,) + shape, lambda m, *_: (m,) + (0,) * len(shape))


def self_forward(table, queries, sides, carried, last):
    rows = queries.shape[1]
    parts, length = len(sides), sides[0].shape[0]
    pairs = GROUPS * parts * length // rows * GROUP_HEADS // 2
    accum, stats = (GROUP_HEADS, 128, rows), (16, rows)
    outs = [(rows, 256), (8, rows)] if last else [accum, stats]
    first = carried is None
    return pl.pallas_call(
        functools.partial(forward_kernel, rows, parts, first, last),
        grid_spec=pltpu.PrefetchScalarGridSpec(
            num_scalar_prefetch=1,
            grid=(GROUPS,),
            in_specs=[slab((rows, QUERY))]
            + [whole((length, SIDE))] * parts
            + ([] if first else [slab(accum), slab(stats)]),
            out_specs=[slab(shape) for shape in outs],
            scratch_shapes=[
                pltpu.VMEM((GROUP_HEADS, rows, 128), jnp.bfloat16),
                pltpu.VMEM(accum, jnp.float32),
                pltpu.VMEM(stats, jnp.float32),
            ],
        ),
        out_shape=[jax.ShapeDtypeStruct((GROUPS,) + shape, jnp.float32) for shape in outs],
        compiler_params=pltpu.CompilerParams(vmem_limit_bytes=VMEM_LIMIT),
        cost_estimate=pl.CostEstimate(
            flops=pairs * rows * rows * 128 * 16,
            bytes_accessed=4 * length * parts * SIDE,
            transcendentals=pairs * rows * rows,
        ),
        name="self_forward",
    )(table, queries, *sides, *(() if first else carried))


def self_backward(table, queries, dout, state, sides, carried, first, last):
    rows = queries.shape[1]
    parts, length = len(sides), sides[0].shape[0]
    pairs = GROUPS * parts * length // rows * GROUP_HEADS // 2
    slope = (GROUP_HEADS, 128, rows)
    outs = [jax.ShapeDtypeStruct((length, SIDE), jnp.bfloat16)] * parts
    out_specs = [whole((length, SIDE))] * parts
    if last:
        outs = outs + [jax.ShapeDtypeStruct((GROUPS, rows, QUERY), jnp.bfloat16)]
        out_specs = out_specs + [slab((rows, QUERY))]
    else:
        outs = outs + [jax.ShapeDtypeStruct((GROUPS,) + slope, jnp.float32)]
        out_specs = out_specs + [slab(slope)]
    if first:
        outs = outs + [jax.ShapeDtypeStruct((GROUPS, 8, rows), jnp.float32)]
        out_specs = out_specs + [slab((8, rows))]
    return pl.pallas_call(
        functools.partial(backward_kernel, rows, parts, first, last),
        grid_spec=pltpu.PrefetchScalarGridSpec(
            num_scalar_prefetch=1,
            grid=(GROUPS,),
            in_specs=[slab((rows, QUERY)), slab((rows, 256)), slab((8, rows))]
            + [whole((length, SIDE))] * parts
            + [slab((rows, 256)) if first else slab(slope)],
            out_specs=out_specs,
            scratch_shapes=[
                pltpu.VMEM((2 * GROUP_HEADS, rows, 128), jnp.bfloat16),
                pltpu.VMEM((parts * length, SIDE), jnp.float32),
                pltpu.VMEM(slope, jnp.float32),
                pltpu.VMEM((8, rows), jnp.float32),
            ],
        ),
        out_shape=outs,
        compiler_params=pltpu.CompilerParams(vmem_limit_bytes=VMEM_LIMIT),
        cost_estimate=pl.CostEstimate(
            flops=pairs * rows * rows * 128 * 20,
            bytes_accessed=8 * length * parts * SIDE,
            transcendentals=pairs * rows * rows,
        ),
        name="self_backward",
    )(table, queries, dout, state, *sides, carried)


def pair_heads(block, scale=1.0):
    lane = lax.broadcasted_iota(jnp.int32, block.shape, 1)
    values = wide(block) * scale
    return rounded(jnp.where(lane < 64, values, 0.0)), rounded(jnp.where(lane >= 64, values, 0.0))


def cross_forward_kernel(query, keys, values, out, lse):
    rows = query.shape[0]
    parts = pair_heads(query[...], SCALE)
    sides = []
    lse[0] = jnp.zeros((8, rows), jnp.float32)
    for head in range(2):
        scores = lax.dot_general(
            keys[...], parts[head], LANES_IN, preferred_element_type=jnp.float32
        )
        top = jnp.max(scores, axis=0, keepdims=True)
        weights = jnp.exp(scores - top)
        total = jnp.sum(weights, axis=0, keepdims=True)
        mixed = lax.dot_general(
            values[...], rounded(weights), ROWS_IN, preferred_element_type=jnp.float32
        )
        sides.append(mixed / total)
        lse[0, head : head + 1, :] = top + jnp.log(total)
    line = lax.broadcasted_iota(jnp.int32, (128, rows), 0)
    out[...] = rounded(jnp.where(line < 64, sides[0], sides[1]).T)


def cross_backward_kernel(query, keys, values, dout, lse, qgrad, kgrad, vgrad):
    rows = query.shape[0]
    parts = pair_heads(query[...], SCALE)
    grads = pair_heads(dout[...])
    sides, key_parts, value_parts = [], [], []
    for head in range(2):
        scores = lax.dot_general(
            keys[...], parts[head], LANES_IN, preferred_element_type=jnp.float32
        )
        probs = jnp.exp(scores - lse[0, head : head + 1, :])
        slopes = lax.dot_general(
            values[...], grads[head], LANES_IN, preferred_element_type=jnp.float32
        )
        delta = jnp.sum(probs * slopes, axis=0, keepdims=True)
        low = rounded(probs * (slopes - delta))
        value_parts.append(matmul(rounded(probs), grads[head]))
        key_parts.append(matmul(low, parts[head]))
        sides.append(lax.dot_general(keys[...], low, ROWS_IN, preferred_element_type=jnp.float32))
    line = lax.broadcasted_iota(jnp.int32, (128, rows), 0)
    qgrad[...] = rounded(jnp.where(line < 64, sides[0], sides[1]).T * SCALE)
    kgrad[...] = rounded(key_parts[0] + key_parts[1])
    vgrad[...] = rounded(value_parts[0] + value_parts[1])


def cross_forward(query, pair):
    rows, width = query.shape
    count = width // 128
    kept = pair.shape[0]
    return pl.pallas_call(
        cross_forward_kernel,
        grid=(count,),
        in_specs=[
            pl.BlockSpec((rows, 128), lambda i: (0, i)),
            pl.BlockSpec((kept, 128), lambda i: (0, i)),
            pl.BlockSpec((kept, 128), lambda i: (0, count + i)),
        ],
        out_specs=[
            pl.BlockSpec((rows, 128), lambda i: (0, i)),
            pl.BlockSpec((1, 8, rows), lambda i: (i, 0, 0)),
        ],
        out_shape=[
            jax.ShapeDtypeStruct((rows, width), jnp.bfloat16),
            jax.ShapeDtypeStruct((count, 8, rows), jnp.float32),
        ],
        compiler_params=pltpu.CompilerParams(vmem_limit_bytes=VMEM_LIMIT),
        cost_estimate=pl.CostEstimate(
            flops=8 * rows * kept * width, bytes_accessed=4 * kept * width, transcendentals=12 * rows * kept
        ),
        name="cross_forward",
    )(query, pair, pair)


def cross_backward(query, pair, dout, lse):
    rows, width = query.shape
    count = width // 128
    kept = pair.shape[0]
    return pl.pallas_call(
        cross_backward_kernel,
        grid=(count,),
        in_specs=[
            pl.BlockSpec((rows, 128), lambda i: (0, i)),
            pl.BlockSpec((kept, 128), lambda i: (0, i)),
            pl.BlockSpec((kept, 128), lambda i: (0, count + i)),
            pl.BlockSpec((rows, 128), lambda i: (0, i)),
            pl.BlockSpec((1, 8, rows), lambda i: (i, 0, 0)),
        ],
        out_specs=[
            pl.BlockSpec((rows, 128), lambda i: (0, i)),
            pl.BlockSpec((kept, 128), lambda i: (0, i)),
            pl.BlockSpec((kept, 128), lambda i: (0, i)),
        ],
        out_shape=[
            jax.ShapeDtypeStruct((rows, width), jnp.bfloat16),
            jax.ShapeDtypeStruct((kept, width), jnp.bfloat16),
            jax.ShapeDtypeStruct((kept, width), jnp.bfloat16),
        ],
        compiler_params=pltpu.CompilerParams(vmem_limit_bytes=VMEM_LIMIT),
        cost_estimate=pl.CostEstimate(
            flops=20 * rows * kept * width, bytes_accessed=8 * kept * width, transcendentals=12 * rows * kept
        ),
        name="cross_backward",
    )(query, pair, pair, dout, lse)


def pick_kernel(table, bank, out):
    i = pl.program_id(0)
    keep = table[pl.num_programs(0) + i]
    out[0] = jnp.where(keep > 0, bank[0], jnp.zeros_like(bank[0]))


def pick_rows(chunks, spots, found):
    count = spots.shape[0]
    size = chunks.shape[1:]
    table = jnp.concatenate([spots, found.astype(jnp.int32)])
    return pl.pallas_call(
        pick_kernel,
        grid_spec=pltpu.PrefetchScalarGridSpec(
            num_scalar_prefetch=1,
            grid=(count,),
            in_specs=[pl.BlockSpec((1,) + size, lambda i, t: (t[i], 0, 0))],
            out_specs=pl.BlockSpec((1,) + size, lambda i, t: (i, 0, 0)),
        ),
        out_shape=jax.ShapeDtypeStruct((count,) + size, chunks.dtype),
        name="pick_rows",
    )(table, chunks)


def place_kernel(count, table, grads, out):
    spot = pl.program_id(0)
    out[...] = jnp.zeros_like(out)
    for i in range(count):

        @pl.when(table[i] == spot)
        def _(i=i):
            out[0] += wide(grads[i])


def place_rows(grads, spots, chunks):
    count = spots.shape[0]
    size = grads.shape[1:]
    return pl.pallas_call(
        functools.partial(place_kernel, count),
        grid_spec=pltpu.PrefetchScalarGridSpec(
            num_scalar_prefetch=1,
            grid=(chunks,),
            in_specs=[whole((count,) + size)],
            out_specs=pl.BlockSpec((1,) + size, lambda n, t: (n, 0, 0)),
        ),
        out_shape=jax.ShapeDtypeStruct((chunks,) + size, jnp.float32),
        name="place_rows",
    )(spots, grads)


class Chain:
    def __init__(self, stages):
        self.stages = stages
        self.result = None
        self.pending = next(stages)

    def step(self, pending):
        try:
            self.pending = self.stages.send(pending)
        except StopIteration as stop:
            self.pending, self.result = (), stop.value


def meet(values, *chains):
    values, pending = lax.optimization_barrier((values, [chain.pending for chain in chains]))
    for chain, arrays in zip(chains, pending):
        chain.step(arrays)
    return values


def settle(values, *chains):
    values, kept = lax.optimization_barrier((values, [chain.pending[0] for chain in chains]))
    for chain, array in zip(chains, kept):
        chain.pending = [array] + list(chain.pending[1:])
    return values


def total_of(arrays):
    total = wide(arrays[0])
    for array in arrays[1:]:
        total = total + wide(array)
    return total


def body(
    grid,
    tokens,
    cotangent,
    bank,
    prefix,
    blocks,
    self_qkv,
    self_out,
    cross_q,
    cross_kv,
    cross_out,
    ffn_in,
    ffn_out,
    gains,
    biases,
):
    Z, X, C, Y = grid.z, grid.x, grid.c, grid.y
    devices = grid.seq * Y
    seq_index = lax.axis_index("seq")
    me = {
        "y": lax.axis_index("batch"),
        "c": seq_index % C,
        "x": (seq_index // C) % X,
        "z": seq_index // (C * X),
        "h": seq_index // (2 * C * X),
        "l": seq_index // (C * X) % 2,
    }
    my_z, my_x, my_c = me["z"], me["x"], me["c"]
    rows, width = tokens.shape[1:]
    hidden = ffn_in.shape[1]
    part = width // devices
    fan = hidden // width
    inputs = tokens[0]

    def parted(array, axis, place):
        size = getattr(grid, axis)
        kept = [take(array, me[axis], place)]
        for shift in range(1, size):
            kept.append(grid.send(take(array, me[axis] ^ shift, place), axis, shift))
        return kept

    def reduction(array, axes, lead=0, final=True):
        names = ["h", "l", "x", "c", "y"]
        for axis in axes:
            place = lead + names.index(axis)
            names.remove(axis)
            arrays = yield parted(array, axis, place)
            total = total_of(arrays)
            array = rounded(total)
        return total if final else array

    def sharded(array):
        return array.reshape(2, 2, X, C, Y, array.shape[0] // devices, array.shape[1])

    grouped = self_qkv.reshape(part, 3, GROUPS, GROUP_WIDTH)
    extra = jnp.stack([biases[3], biases[4]], axis=1)
    extra = jnp.broadcast_to(
        jnp.pad(extra, ((0, 0), (0, QUERY - GROUP_WIDTH - 2)))[:, None],
        (part, GROUPS, QUERY - GROUP_WIDTH),
    )
    packed = jnp.concatenate(
        [
            grouped[:, 0],
            extra,
            grouped[:, 1, :, :128],
            grouped[:, 2, :, :128],
            grouped[:, 1, :, 128:],
            grouped[:, 2, :, 128:],
        ],
        axis=2,
    ).transpose(1, 0, 2)
    packed, later = lax.optimization_barrier(
        (packed, (self_out, cross_q, cross_out, cross_kv, ffn_in, ffn_out, gains, biases))
    )
    self_out, cross_q, cross_out, cross_kv, ffn_in, ffn_out, gains, biases = later
    pieces = parted(packed, "z", 0)

    small = jnp.concatenate([gains, biases], axis=0).T
    small = jnp.pad(small, ((0, 0), (0, 128 - small.shape[1])))
    first_pack = jnp.concatenate([self_out, cross_q, cross_out, cross_kv, small], axis=1)
    inner_columns = (
        ffn_in.reshape(part, devices, fan, part).transpose(0, 2, 1, 3).reshape(part, hidden)
    )
    outer_blocks = ffn_out.reshape(fan, part, width).transpose(1, 0, 2).reshape(part, hidden)
    second_pack = jnp.stack([inner_columns, outer_blocks])
    first_all = lax.all_gather(first_pack, ("seq", "batch"), axis=0, tiled=True)
    second_all = lax.all_gather(second_pack, ("seq", "batch"), axis=1, tiled=True)

    pieces, inputs, bank_rows = lax.optimization_barrier((pieces, inputs, bank[0]))
    across = grid.send(inputs, "h", 1)
    beside = grid.send(inputs, "l", 1)

    chunk = BANK_BLOCK * blocks.shape[1] // grid.seq
    per_block = BANK_BLOCK // chunk
    local_chunks = bank.shape[1] // chunk
    local_blocks = bank.shape[1] // BANK_BLOCK
    bank_chunks = bank_rows.reshape(local_chunks, chunk, width)
    home = seq_index * local_blocks
    every = jnp.arange(grid.seq, dtype=jnp.int32)
    wanted = jnp.take(blocks[0], every // per_block) - home
    found = (wanted >= 0) & (wanted < local_blocks)
    spots = jnp.where(found, wanted * per_block + every % per_block, 0)
    picked = pick_rows(bank_chunks, spots, found).reshape(2, 2, X, C, 1, chunk, width)

    def spreading(own):
        array = own
        for axis in "hlxc":
            size = getattr(grid, axis)
            array = jnp.stack((yield [array] + [grid.send(array, axis, m) for m in range(1, size)]))
        return array

    def retrieval():
        own = (yield from reduction(picked, "cxlh", final=False))[0]
        every_row = yield from spreading(own)
        return own, every_row.reshape(grid.seq * chunk, width)

    retrieve = Chain(retrieval())
    gathered = in_order(pieces, my_z)
    for axis in "yxc":
        pieces = [gathered] + [grid.send(gathered, axis, m) for m in range(1, getattr(grid, axis))]
        if axis == "x":
            pieces, across, beside = meet((pieces, across, beside), retrieve)
        gathered = in_order(pieces, me[axis])
    token_parts = [inputs, beside, across, grid.send(across, "l", 1)]
    qkv_group = gathered.transpose(3, 1, 0, 2, 4, 5).reshape(width, PACK)
    column = jnp.arange(PACK, dtype=jnp.int32)
    real = (column < GROUP_WIDTH) | (column >= QUERY)
    is_query = column < GROUP_WIDTH
    is_pair_value = (column >= QUERY + 128) & (column < QUERY + 256)
    is_value = is_pair_value | (column >= QUERY + 320)
    local = jnp.where(is_query, column, column - jnp.where(is_pair_value, QUERY + 128, QUERY + 192))
    line = jnp.where(is_query | is_value, local + my_z * GROUP_WIDTH, -1)
    chosen = (jnp.arange(width, dtype=jnp.int32)[:, None] == line[None]).astype(jnp.bfloat16)
    picked_bias = weight_grad(qkv_group[:, GROUP_WIDTH:QUERY], chosen)
    qkv_bias = jnp.where(is_query, picked_bias[0], picked_bias[1])
    qkv_weight = jnp.where(real[None], qkv_group, jnp.zeros_like(qkv_group))

    qkv_weight, qkv_bias, token_parts = meet((qkv_weight, qkv_bias, token_parts), retrieve)

    token_column = jnp.concatenate(token_parts, axis=0)
    own_queries = rounded(matmul(token_column, qkv_weight[:, :QUERY]) + qkv_bias[:QUERY])
    own_side = rounded(matmul(token_column, qkv_weight[:, QUERY:]) + qkv_bias[QUERY:])
    own_queries = own_queries.reshape(GROUPS, rows, QUERY)

    far_queries = grid.send(own_queries[1::2], "z", 0, mirror=True)
    near_other = grid.send(own_side, "c", 1)
    far_queries, side = lax.optimization_barrier((far_queries, own_side))
    far_own = [grid.send(side, "x", m) for m in range(1, X)]
    queries = jnp.stack(
        [own_queries[m] if m % 2 == 0 else far_queries[m // 2] for m in range(GROUPS)]
    )

    turn = jnp.arange(GROUPS, dtype=jnp.int32)
    turn_z = my_z ^ turn

    def key_firsts(x, c):
        return ((turn_z * X + x) * C + c) * rows

    query_firsts = jnp.where(
        turn % 2 == 0, key_firsts(my_x, my_c), key_firsts(X - 1 - my_x, C - 1 - my_c)
    )

    def table_of(shifts, c):
        keys = [key_firsts(my_x ^ m, c) for m in shifts]
        return jnp.concatenate(keys + [query_firsts, prefix]).astype(jnp.int32)

    far = list(range(1, X))
    tables = {
        "near own": table_of([0], my_c),
        "near other": table_of([0], C - 1 - my_c),
        "far own": table_of(far, my_c),
        "far other": table_of(far, C - 1 - my_c),
    }

    carry = self_forward(tables["near own"], queries, [own_side], None, False)
    carry, near_other = meet((carry, near_other), retrieve)
    carry = self_forward(tables["near other"], queries, [near_other], carry, False)
    carry, far_own = meet((carry, far_own), retrieve)
    far_other = [grid.send(side, "c", 1) for side in far_own]
    carry = self_forward(tables["far own"], queries, far_own, carry, False)
    carry, far_other = meet((carry, far_other), retrieve)
    attention, lse = self_forward(tables["far other"], queries, far_other, carry, True)
    attention, lse = meet((attention, lse), retrieve)
    attention_mine = rounded(attention)

    def swapped(array, m):
        return grid.send(array, "z", m, mirror=m % 2 == 1)

    pieces = [attention_mine[0]] + [swapped(attention_mine[m], m) for m in range(1, Z)]
    pieces = meet(pieces, retrieve)
    retrieve.step(retrieve.pending)
    own_rows, all_rows = retrieve.result
    attention_low = (
        in_order(pieces, my_z)[:, :, :GROUP_WIDTH].transpose(1, 0, 2).reshape(rows, width)
    )

    selfout_full = first_all[:, :width]
    crossq_full = first_all[:, width : 2 * width]
    crossout_full = first_all[:, 2 * width : 3 * width]
    crosskv_full = first_all[:, 3 * width : 5 * width]
    small_full = wide(first_all[:, 5 * width :].T)
    gain = small_full[:3]
    bias = small_full[3:17]
    ffnin_full = second_all[0]
    outer = [second_all[1, :, f * width : (f + 1) * width] for f in range(fan)]
    inner_bias = bias[10:14].reshape(devices, fan, part).transpose(1, 0, 2).reshape(-1)

    resid_one = wide(inputs) + matmul(attention_low, selfout_full) + bias[5]
    hidden_one = layer_norm(resid_one, gain[0], bias[0])
    hidden_one_low = rounded(hidden_one)
    cross_query = rounded(matmul(hidden_one_low, crossq_full) + bias[6])
    cross_pair = rounded(
        matmul(all_rows, crosskv_full) + jnp.concatenate([jnp.zeros((width,), jnp.float32), bias[7]])
    )
    cross_att, cross_lse = cross_forward(cross_query, cross_pair)
    resid_two = hidden_one + matmul(cross_att, crossout_full) + bias[8]
    hidden_two = layer_norm(resid_two, gain[1], bias[1])
    hidden_two_low = rounded(hidden_two)
    inner = matmul(hidden_two_low, ffnin_full) + inner_bias
    activated = rounded(gelu_exact(inner))

    def fan_part(array, f):
        return array[:, f * width : (f + 1) * width]

    resid_three = hidden_two + bias[9]
    for f in range(fan):
        resid_three = resid_three + matmul(fan_part(activated, f), outer[f])
    output = layer_norm(resid_three, gain[2], bias[2])

    _unused, norm_three = jax.vjp(layer_norm, resid_three, gain[2], bias[2])
    dresid_three, dgain_three, dshift_three = norm_three(wide(cotangent[0]))
    douter_low = rounded(dresid_three)
    grad_ffnout = rounded(weight_grad(activated, douter_low))
    reduce_ffnout = Chain(
        reduction(grad_ffnout.reshape(fan, 2, 2, X, C, Y, part, width), "cyxlh", lead=1)
    )
    _unused, gelu_back = jax.vjp(gelu_exact, inner)
    dactivated = jnp.concatenate([back_matmul(douter_low, block) for block in outer], axis=1)
    dinner_low = rounded(gelu_back(dactivated)[0])
    grad_ffnin = rounded(weight_grad(hidden_two_low, dinner_low))
    reduce_ffnin = Chain(reduction(sharded(grad_ffnin), "cyxlh"))

    _unused, norm_two = jax.vjp(layer_norm, resid_two, gain[1], bias[1])
    dresid_two, dgain_two, dshift_two = norm_two(dresid_three + back_matmul(dinner_low, ffnin_full))
    dcross_low = rounded(dresid_two)
    dcross_att = rounded(back_matmul(dcross_low, crossout_full))
    dcross_query, dcross_key, dcross_value = cross_backward(
        cross_query, cross_pair, dcross_att, cross_lse
    )
    dcross_query, dcross_key, dcross_value = meet(
        (dcross_query, dcross_key, dcross_value), reduce_ffnout, reduce_ffnin
    )

    dcross_all = jnp.concatenate([dcross_key, dcross_value], axis=1)
    dcross_all = dcross_all.reshape(C, X, 2, 2, chunk, 2 * width)

    def unspreading(array):
        for axis in "cxlh":
            size = getattr(grid, axis)
            arrays = yield [array[0]] + [grid.send(array[m], axis, m) for m in range(1, size)]
            array = rounded(total_of(arrays))
        return array

    unspread = Chain(unspreading(dcross_all))

    _unused, norm_one = jax.vjp(layer_norm, resid_one, gain[0], bias[0])
    dresid_one, dgain_one, dshift_one = norm_one(dresid_two + back_matmul(dcross_query, crossq_full))
    dbranch_low = rounded(dresid_one)
    datt_low = rounded(back_matmul(dbranch_low, selfout_full))
    datt_groups = jnp.pad(
        datt_low.reshape(rows, GROUPS, GROUP_WIDTH).transpose(1, 0, 2),
        ((0, 0), (0, 0), (0, 256 - GROUP_WIDTH)),
    )
    pieces = [take(datt_groups, my_z, 0)]
    for m in range(1, Z):
        pieces.append(swapped(take(datt_groups, my_z ^ m, 0), m))
    grad_mid = jnp.stack(
        [
            rounded(weight_grad(attention_low, dbranch_low)),
            rounded(weight_grad(hidden_one_low, dcross_query)),
            rounded(weight_grad(cross_att, dcross_low)),
        ]
    )
    grad_mid, pieces = meet((grad_mid, pieces), unspread)
    reduce_mid = Chain(reduction(grad_mid.reshape(3, 2, 2, X, C, Y, part, width), "cyxlh", lead=1))
    dout = jnp.stack(pieces)

    *far_other_grad, slopes, state = self_backward(
        tables["far other"], queries, dout, lse, far_other, attention, True, False
    )
    far_other_grad, slopes = meet(
        (far_other_grad, slopes), reduce_ffnout, reduce_mid, unspread
    )
    far_moved = [grid.send(grad, "c", 1) for grad in far_other_grad]
    *far_own_grad, slopes = self_backward(
        tables["far own"], queries, dout, state, far_own, slopes, False, False
    )
    far_own_grad, far_moved, slopes = meet(
        (far_own_grad, far_moved, slopes), unspread, reduce_ffnout, reduce_ffnin
    )
    far_grad = [rounded(total_of(pair)) for pair in zip(far_own_grad, far_moved)]
    far_moved = [grid.send(grad, "x", m) for m, grad in zip(far, far_grad)]
    near_other_grad, slopes = self_backward(
        tables["near other"], queries, dout, state, [near_other], slopes, False, False
    )
    near_other_grad, far_moved, slopes = meet(
        (near_other_grad, far_moved, slopes), unspread, reduce_ffnout, reduce_ffnin, reduce_mid
    )
    near_moved = grid.send(near_other_grad, "c", 1)

    dcross_pair = unspread.result
    bias_rows = jnp.stack(
        [
            dgain_one,
            dgain_two,
            dgain_three,
            dshift_one,
            dshift_two,
            dshift_three,
            column_sums(dbranch_low),
            column_sums(dcross_query),
            column_sums(dcross_pair[:, width:]),
            column_sums(dcross_low),
            column_sums(douter_low),
        ]
    )
    inner_sums = column_sums(dinner_low).reshape(fan, devices, part).transpose(1, 0, 2)
    bias_rows = jnp.concatenate([bias_rows, inner_sums.reshape(fan, width)], axis=0)
    bias_columns = jnp.pad(rounded(bias_rows.T), ((0, 0), (0, 128 - bias_rows.shape[0])))
    grad_late = jnp.concatenate([rounded(weight_grad(own_rows, dcross_pair)), bias_columns], axis=1)
    reduce_late = Chain(reduction(sharded(grad_late), "cxylh"))
    spread_back = Chain(spreading(rounded(back_matmul(dcross_pair, crosskv_full))))

    slopes = settle(slopes, reduce_late, spread_back, reduce_ffnin, reduce_mid)
    near_own_grad, query_grad = self_backward(
        tables["near own"], queries, dout, state, [own_side], slopes, False, True
    )
    near_own_grad, near_moved, query_grad = meet(
        (near_own_grad, near_moved, query_grad), reduce_late, spread_back, reduce_mid
    )

    far_query_grad = grid.send(query_grad[1::2], "z", 0, mirror=True)
    side_grad = rounded(total_of([near_own_grad, near_moved] + far_moved))
    query_grad = jnp.stack(
        [query_grad[m] if m % 2 == 0 else far_query_grad[m // 2] for m in range(GROUPS)]
    )
    dqkv = jnp.concatenate([query_grad.reshape(GROUPS * rows, QUERY), side_grad], axis=1)
    far_tokens_grad = rounded(back_matmul(dqkv[rows:], qkv_weight)).reshape(Z - 1, rows, width)
    dqkv, far_tokens_grad = meet(
        (dqkv, far_tokens_grad), reduce_ffnin, reduce_late, spread_back, reduce_mid
    )
    third = grid.send(far_tokens_grad[2], "l", 1)
    grad_group = weight_grad(token_column, dqkv)
    sums = jnp.sum(wide(dqkv), axis=0)
    sums = jnp.stack([jnp.where(is_query, sums, 0.0), jnp.where(is_value, sums, 0.0)])
    sums = jnp.pad(rounded(sums), ((0, QUERY - GROUP_WIDTH - 2), (0, 0)))
    grad_group = jnp.concatenate(
        [grad_group[:, :GROUP_WIDTH], back_matmul(chosen, sums), grad_group[:, QUERY:]], axis=1
    )
    reduce_group = Chain(reduction(sharded(rounded(grad_group)), "cyx", final=False))
    tokens_base = dresid_one + back_matmul(dqkv[:rows], qkv_weight)
    tokens_base, third, near_tokens_grad = meet(
        (tokens_base, third, far_tokens_grad[:2]),
        reduce_group,
        reduce_late,
        spread_back,
        reduce_mid,
    )
    second = grid.send(rounded(total_of([near_tokens_grad[1], third])), "h", 1)
    first = grid.send(near_tokens_grad[0], "l", 1)
    tokens_base, second = meet((tokens_base, second), reduce_group, reduce_late, spread_back)
    drows = spread_back.result
    meet((), reduce_group, reduce_late, reduce_ffnout, reduce_ffnin)
    pieces = parted(reduce_group.result.reshape(Z, part, PACK), "z", 0)
    drows, pieces[0] = lax.optimization_barrier((drows, pieces[0]))
    tokens_grad = total_of([tokens_base, first, second])

    spot = jnp.arange(grid.seq, dtype=jnp.int32)
    spot_z = my_z ^ (spot % 2 * 2 + spot // 2 % 2)
    source = (spot_z * X + (my_x ^ (spot // Z % X))) * C + (my_c ^ (spot // (Z * X)))
    target = jnp.take(blocks[0], source // per_block) - home
    inside = (target >= 0) & (target < local_blocks)
    places = jnp.where(inside, target * per_block + source % per_block, -1)
    drows = drows.reshape(grid.seq, chunk, width)
    bank_grad = place_rows(drows, places, local_chunks).reshape(bank.shape[1], width)

    grad_groups = wide(in_order(pieces, my_z))
    sides = grad_groups[:, :, QUERY:]
    out_qkv = jnp.stack(
        [
            grad_groups[:, :, :GROUP_WIDTH],
            jnp.concatenate([sides[:, :, :128], sides[:, :, 256:320]], axis=2),
            jnp.concatenate([sides[:, :, 128:256], sides[:, :, 320:384]], axis=2),
        ]
    )
    out_qkv = out_qkv.transpose(2, 0, 1, 3).reshape(part, 3 * width)
    late_bias = jnp.sum(grad_groups[:, :, GROUP_WIDTH : GROUP_WIDTH + 2], axis=0)

    out_late, out_mid = reduce_late.result, reduce_mid.result
    out_ffnin = (
        reduce_ffnin.result.reshape(part, fan, devices, part)
        .transpose(0, 2, 1, 3)
        .reshape(part, hidden)
    )
    out_small = out_late[:, 2 * width :].T
    bias_grad = jnp.concatenate([out_small[3:6], late_bias.T, out_small[6:15]], axis=0)
    return (
        rounded(output)[None],
        tokens_grad[None],
        bank_grad[None],
        out_qkv,
        out_mid[0],
        out_mid[1],
        out_late[:, : 2 * width],
        out_mid[2],
        out_ffnin,
        reduce_ffnout.result.reshape(fan * part, width),
        out_small[:3],
        bias_grad,
    )


def solution(mesh):
    split = P("batch", "seq", None)
    shard = P(("seq", "batch"), None)
    flat = P(None, ("seq", "batch"))
    return jax.shard_map(
        functools.partial(body, Grid(mesh)),
        mesh=mesh,
        in_specs=(split, split, split, P("batch"), P("batch", None)) + (shard,) * 7 + (flat, flat),
        out_specs=(split, split, split) + (shard,) * 7 + (flat, flat),
        check_vma=False,
    )
```

```python
import functools

import jax
import jax.numpy as jnp
from jax import lax
from jax.experimental import pallas as pl
from jax.experimental.pallas import tpu as pltpu
from jax.sharding import PartitionSpec as P

HEADS = 12
HEAD_DIM = 64
BANK_BLOCK = 128
GROUPS = 4
GROUP_HEADS = HEADS // GROUPS
GROUP_WIDTH = GROUP_HEADS * HEAD_DIM
QUERY, SIDE = 256, 384
PACK = QUERY + SIDE
EPSILON = 1e-05
NEGATIVE = -1e30
SCALE = HEAD_DIM ** (-0.5)
LANES_IN = (((1,), (1,)), ((), ()))
ROWS_IN = (((0,), (0,)), ((), ()))
VMEM_LIMIT = 60 * 1024 * 1024


def layer_norm(values, gain, shift):
    centered = values - jnp.mean(values, axis=-1, keepdims=True)
    variance = jnp.mean(centered * centered, axis=-1, keepdims=True)
    return centered * lax.rsqrt(variance + EPSILON) * gain + shift


def gelu_exact(values):
    return jax.nn.gelu(values, approximate=False)


def rounded(values):
    return values.astype(jnp.bfloat16)


def wide(values):
    return values.astype(jnp.float32)


def matmul(left, right):
    return jnp.dot(left, right, preferred_element_type=jnp.float32)


def weight_grad(left, right):
    return lax.dot_general(left, right, ROWS_IN, preferred_element_type=jnp.float32)


def back_matmul(left, right):
    return lax.dot_general(left, right, LANES_IN, preferred_element_type=jnp.float32)


def column_sums(values):
    return jnp.sum(wide(values), axis=0)


class Grid:
    def __init__(self, mesh):
        self.seq = mesh.shape["seq"]
        self.y = mesh.shape["batch"]
        self.z = GROUPS
        self.c = self.h = self.l = 2
        self.x = self.seq // (self.z * self.c)

    def coords(self, index):
        spot, y = divmod(index, self.y)
        spot, c = divmod(spot, self.c)
        z, x = divmod(spot, self.x)
        return z, x, c, y

    def index(self, z, x, c, y):
        return ((z * self.x + x) * self.c + c) * self.y + y

    def send(self, array, axis, shift, mirror=False):
        if axis in "hl":
            axis, shift = "z", shift * (2 if axis == "h" else 1)
        place = "zxcy".index(axis)
        pairs = []
        for index in range(self.seq * self.y):
            spot = list(self.coords(index))
            spot[place] ^= shift
            if mirror:
                spot[1], spot[2] = self.x - 1 - spot[1], self.c - 1 - spot[2]
            pairs.append((index, self.index(*spot)))
        return lax.ppermute(array, ("seq", "batch"), pairs)


def in_order(pieces, me):
    pieces = list(pieces)
    bit = 1
    while bit < len(pieces):
        swap = (me & bit) != 0
        pieces = [jnp.where(swap, pieces[j ^ bit], piece) for j, piece in enumerate(pieces)]
        bit *= 2
    return jnp.stack(pieces)


def take(array, index, axis):
    return lax.dynamic_index_in_dim(array, index, axis, keepdims=False)


def head_parts(block, scale, third_low):
    lane = lax.broadcasted_iota(jnp.int32, (block.shape[0], 128), 1)
    first = wide(block[:, 0:128]) * scale
    third = wide(block[:, 128:256]) * scale
    third = jnp.where(lane < 64, third, 0.0)
    if not third_low:
        third = pltpu.roll(third, 64, 1)
    return (
        rounded(jnp.where(lane < 64, first, 0.0)),
        rounded(jnp.where(lane >= 64, first, 0.0)),
        rounded(third),
    )


def key_tiles(ref, start, size):
    rows = pl.ds(start, size)
    keys = ref[rows, 0:128]
    values = ref[rows, 128:256]
    third = ref[rows, 256:384]
    return (keys, keys, third), (values, values, third)


def allowed_keys(key_first, query_first, prefix_len, shape):
    key_pos = key_first + lax.broadcasted_iota(jnp.int32, shape, 0)
    query_pos = query_first + lax.broadcasted_iota(jnp.int32, shape, 1)
    return (key_pos <= query_pos) | (key_pos < prefix_len)


def each_block(table, refs, rows, query_first, prefix_len, work):
    count = refs[0].shape[0] // rows
    for part, ref in enumerate(refs):

        def step(local, carry, part=part, ref=ref):
            block = part * count + local
            key_first = table[block]
            last = key_first + rows - 1
            seen = (key_first <= query_first + rows - 1) | (key_first < prefix_len)
            whole = (last <= query_first) | (last < prefix_len)

            @pl.when(seen & whole)
            def _():
                work(ref, local * rows, block, key_first, False)

            @pl.when(seen & jnp.logical_not(whole))
            def _():
                work(ref, local * rows, block, key_first, True)

            return carry

        lax.fori_loop(0, count, step, 0)


def forward_kernel(rows, parts, first, last, table, query_in, *refs):
    refs = list(refs)
    sides = [refs.pop(0) for _ in range(parts)]
    if not first:
        accum_in, stats_in = refs.pop(0), refs.pop(0)
    out, state, query, accum, stats = refs
    m = pl.program_id(0)
    blocks = parts * (sides[0].shape[0] // rows)
    query_first = table[blocks + m]
    prefix_len = table[blocks + GROUPS]
    for head, part in enumerate(head_parts(query_in[0], SCALE, True)):
        query[head] = part
    if first:
        accum[...] = jnp.zeros_like(accum)
        stats[0:8, :] = jnp.full((8, rows), NEGATIVE, jnp.float32)
        stats[8:16, :] = jnp.zeros((8, rows), jnp.float32)
    else:
        accum[...] = accum_in[0]
        stats[...] = stats_in[0]

    def work(ref, start, block, key_first, masked):
        keys, values = key_tiles(ref, start, rows)
        if masked:
            mask = allowed_keys(key_first, query_first, prefix_len, (rows, rows))
        for head in range(GROUP_HEADS):
            scores = lax.dot_general(
                keys[head], query[head], LANES_IN, preferred_element_type=jnp.float32
            )
            if masked:
                scores = jnp.where(mask, scores, NEGATIVE)
            old = stats[head : head + 1, :]
            top = jnp.maximum(old, jnp.max(scores, axis=0, keepdims=True))
            weights = jnp.exp(scores - top)
            shrink = jnp.exp(old - top)
            stats[head : head + 1, :] = top
            stats[8 + head : 9 + head, :] = stats[8 + head : 9 + head, :] * shrink + jnp.sum(
                weights, axis=0, keepdims=True
            )
            accum[head] = accum[head] * shrink + lax.dot_general(
                values[head], rounded(weights), ROWS_IN, preferred_element_type=jnp.float32
            )

    each_block(table, sides, rows, query_first, prefix_len, work)
    if not last:
        out[0] = accum[...]
        state[0] = stats[...]
        return
    totals = stats[8 : 8 + GROUP_HEADS, :]
    final = [accum[head] / totals[head : head + 1, :] for head in range(GROUP_HEADS)]
    line = lax.broadcasted_iota(jnp.int32, (128, rows), 0)
    out[0, :, 0:128] = jnp.where(line < 64, final[0], final[1]).T
    third = jnp.concatenate([final[2][64:128], jnp.zeros((64, rows), jnp.float32)], axis=0)
    out[0, :, 128:256] = third.T
    state[0] = jnp.zeros((8, rows), jnp.float32)
    state[0, 0:GROUP_HEADS, :] = stats[0:GROUP_HEADS, :] + jnp.log(totals)


def backward_kernel(rows, parts, first, last, table, query_in, dout, state, *refs):
    refs = list(refs)
    sides = [refs.pop(0) for _ in range(parts)]
    carried = refs.pop(0)
    grads_out = [refs.pop(0) for _ in range(parts)]
    qgrad_out = refs.pop(0)
    if first:
        state_out = refs.pop(0)
    query, accum, qgrad, lines = refs
    m = pl.program_id(0)
    count = sides[0].shape[0] // rows
    blocks = parts * count
    query_first = table[blocks + m]
    prefix_len = table[blocks + GROUPS]

    @pl.when(m == 0)
    def _():
        def clear(index, carry):
            accum[pl.ds(index * rows, rows), :] = jnp.zeros((rows, SIDE), jnp.float32)
            return carry

        lax.fori_loop(0, blocks, clear, 0)

    for head, part in enumerate(head_parts(query_in[0], SCALE, True)):
        query[head] = part
    for head, part in enumerate(head_parts(dout[0], 1.0, False)):
        query[GROUP_HEADS + head] = part
    lines[...] = state[0]
    if first:
        pair_prod = (wide(dout[0, :, 0:128]) * carried[0, :, 0:128]).T
        third_prod = (wide(dout[0, :, 128:256]) * carried[0, :, 128:256]).T
        lines[3:4, :] = jnp.sum(pair_prod[0:64], axis=0, keepdims=True)
        lines[4:5, :] = jnp.sum(pair_prod[64:128], axis=0, keepdims=True)
        lines[5:6, :] = jnp.sum(third_prod[0:64], axis=0, keepdims=True)
        state_out[0] = lines[...]
        qgrad[...] = jnp.zeros_like(qgrad)
    else:
        qgrad[...] = carried[0]

    def work(ref, start, block, key_first, masked):
        keys, values = key_tiles(ref, start, rows)
        if masked:
            mask = allowed_keys(key_first, query_first, prefix_len, (rows, rows))
        key_parts, value_parts = [], []
        for head in range(GROUP_HEADS):
            scores = lax.dot_general(
                keys[head], query[head], LANES_IN, preferred_element_type=jnp.float32
            )
            if masked:
                scores = jnp.where(mask, scores, NEGATIVE)
            probs = jnp.exp(scores - lines[head : head + 1, :])
            slopes = lax.dot_general(
                values[head],
                query[GROUP_HEADS + head],
                LANES_IN,
                preferred_element_type=jnp.float32,
            )
            low = rounded(probs * (slopes - lines[3 + head : 4 + head, :]))
            value_parts.append(matmul(rounded(probs), query[GROUP_HEADS + head]))
            key_parts.append(matmul(low, query[head]))
            qgrad[head] += lax.dot_general(
                keys[head], low, ROWS_IN, preferred_element_type=jnp.float32
            )
        span = pl.ds(pl.multiple_of(block * rows, rows), rows)
        accum[span, 0:128] += key_parts[0] + key_parts[1]
        accum[span, 128:256] += value_parts[0] + value_parts[1]
        accum[span, 256:384] += key_parts[2] + value_parts[2]

    each_block(table, sides, rows, query_first, prefix_len, work)
    if last:
        line = lax.broadcasted_iota(jnp.int32, (128, rows), 0)
        qgrad_out[0, :, 0:128] = rounded(jnp.where(line < 64, qgrad[0], qgrad[1]).T * SCALE)
        qgrad_out[0, :, 128:256] = rounded(jnp.where(line < 64, qgrad[2], 0.0).T * SCALE)
    else:
        qgrad_out[0] = qgrad[...]

    @pl.when(m == GROUPS - 1)
    def _():
        for part, ref in enumerate(grads_out):

            def write(index, carry, part=part, ref=ref):
                source = pl.ds((part * count + index) * rows, rows)
                ref[pl.ds(index * rows, rows), :] = rounded(accum[source, :])
                return carry

            lax.fori_loop(0, count, write, 0)


def whole(shape):
    return pl.BlockSpec(shape, lambda *_: (0,) * len(shape), pipeline_mode=pl.Buffered(1))


def slab(shape):
    return pl.BlockSpec((1,) + shape, lambda m, *_: (m,) + (0,) * len(shape))


def self_forward(table, queries, sides, carried, last):
    rows = queries.shape[1]
    parts, length = len(sides), sides[0].shape[0]
    pairs = GROUPS * parts * length // rows * GROUP_HEADS // 2
    accum, stats = (GROUP_HEADS, 128, rows), (16, rows)
    outs = [(rows, 256), (8, rows)] if last else [accum, stats]
    first = carried is None
    return pl.pallas_call(
        functools.partial(forward_kernel, rows, parts, first, last),
        grid_spec=pltpu.PrefetchScalarGridSpec(
            num_scalar_prefetch=1,
            grid=(GROUPS,),
            in_specs=[slab((rows, QUERY))]
            + [whole((length, SIDE))] * parts
            + ([] if first else [slab(accum), slab(stats)]),
            out_specs=[slab(shape) for shape in outs],
            scratch_shapes=[
                pltpu.VMEM((GROUP_HEADS, rows, 128), jnp.bfloat16),
                pltpu.VMEM(accum, jnp.float32),
                pltpu.VMEM(stats, jnp.float32),
            ],
        ),
        out_shape=[jax.ShapeDtypeStruct((GROUPS,) + shape, jnp.float32) for shape in outs],
        compiler_params=pltpu.CompilerParams(vmem_limit_bytes=VMEM_LIMIT),
        cost_estimate=pl.CostEstimate(
            flops=pairs * rows * rows * 128 * 16,
            bytes_accessed=4 * length * parts * SIDE,
            transcendentals=pairs * rows * rows,
        ),
        name="self_forward",
    )(table, queries, *sides, *(() if first else carried))


def self_backward(table, queries, dout, state, sides, carried, first, last):
    rows = queries.shape[1]
    parts, length = len(sides), sides[0].shape[0]
    pairs = GROUPS * parts * length // rows * GROUP_HEADS // 2
    slope = (GROUP_HEADS, 128, rows)
    outs = [jax.ShapeDtypeStruct((length, SIDE), jnp.bfloat16)] * parts
    out_specs = [whole((length, SIDE))] * parts
    if last:
        outs = outs + [jax.ShapeDtypeStruct((GROUPS, rows, QUERY), jnp.bfloat16)]
        out_specs = out_specs + [slab((rows, QUERY))]
    else:
        outs = outs + [jax.ShapeDtypeStruct((GROUPS,) + slope, jnp.float32)]
        out_specs = out_specs + [slab(slope)]
    if first:
        outs = outs + [jax.ShapeDtypeStruct((GROUPS, 8, rows), jnp.float32)]
        out_specs = out_specs + [slab((8, rows))]
    return pl.pallas_call(
        functools.partial(backward_kernel, rows, parts, first, last),
        grid_spec=pltpu.PrefetchScalarGridSpec(
            num_scalar_prefetch=1,
            grid=(GROUPS,),
            in_specs=[slab((rows, QUERY)), slab((rows, 256)), slab((8, rows))]
            + [whole((length, SIDE))] * parts
            + [slab((rows, 256)) if first else slab(slope)],
            out_specs=out_specs,
            scratch_shapes=[
                pltpu.VMEM((2 * GROUP_HEADS, rows, 128), jnp.bfloat16),
                pltpu.VMEM((parts * length, SIDE), jnp.float32),
                pltpu.VMEM(slope, jnp.float32),
                pltpu.VMEM((8, rows), jnp.float32),
            ],
        ),
        out_shape=outs,
        compiler_params=pltpu.CompilerParams(vmem_limit_bytes=VMEM_LIMIT),
        cost_estimate=pl.CostEstimate(
            flops=pairs * rows * rows * 128 * 20,
            bytes_accessed=8 * length * parts * SIDE,
            transcendentals=pairs * rows * rows,
        ),
        name="self_backward",
    )(table, queries, dout, state, *sides, carried)


def pair_heads(block, scale=1.0):
    lane = lax.broadcasted_iota(jnp.int32, block.shape, 1)
    values = wide(block) * scale
    return rounded(jnp.where(lane < 64, values, 0.0)), rounded(jnp.where(lane >= 64, values, 0.0))


def cross_forward_kernel(query, keys, values, out, lse):
    rows = query.shape[0]
    parts = pair_heads(query[...], SCALE)
    sides = []
    lse[0] = jnp.zeros((8, rows), jnp.float32)
    for head in range(2):
        scores = lax.dot_general(
            keys[...], parts[head], LANES_IN, preferred_element_type=jnp.float32
        )
        top = jnp.max(scores, axis=0, keepdims=True)
        weights = jnp.exp(scores - top)
        total = jnp.sum(weights, axis=0, keepdims=True)
        mixed = lax.dot_general(
            values[...], rounded(weights), ROWS_IN, preferred_element_type=jnp.float32
        )
        sides.append(mixed / total)
        lse[0, head : head + 1, :] = top + jnp.log(total)
    line = lax.broadcasted_iota(jnp.int32, (128, rows), 0)
    out[...] = rounded(jnp.where(line < 64, sides[0], sides[1]).T)


def cross_backward_kernel(query, keys, values, dout, lse, qgrad, kgrad, vgrad):
    rows = query.shape[0]
    parts = pair_heads(query[...], SCALE)
    grads = pair_heads(dout[...])
    sides, key_parts, value_parts = [], [], []
    for head in range(2):
        scores = lax.dot_general(
            keys[...], parts[head], LANES_IN, preferred_element_type=jnp.float32
        )
        probs = jnp.exp(scores - lse[0, head : head + 1, :])
        slopes = lax.dot_general(
            values[...], grads[head], LANES_IN, preferred_element_type=jnp.float32
        )
        delta = jnp.sum(probs * slopes, axis=0, keepdims=True)
        low = rounded(probs * (slopes - delta))
        value_parts.append(matmul(rounded(probs), grads[head]))
        key_parts.append(matmul(low, parts[head]))
        sides.append(lax.dot_general(keys[...], low, ROWS_IN, preferred_element_type=jnp.float32))
    line = lax.broadcasted_iota(jnp.int32, (128, rows), 0)
    qgrad[...] = rounded(jnp.where(line < 64, sides[0], sides[1]).T * SCALE)
    kgrad[...] = rounded(key_parts[0] + key_parts[1])
    vgrad[...] = rounded(value_parts[0] + value_parts[1])


def cross_forward(query, pair):
    rows, width = query.shape
    count = width // 128
    kept = pair.shape[0]
    return pl.pallas_call(
        cross_forward_kernel,
        grid=(count,),
        in_specs=[
            pl.BlockSpec((rows, 128), lambda i: (0, i)),
            pl.BlockSpec((kept, 128), lambda i: (0, i)),
            pl.BlockSpec((kept, 128), lambda i: (0, count + i)),
        ],
        out_specs=[
            pl.BlockSpec((rows, 128), lambda i: (0, i)),
            pl.BlockSpec((1, 8, rows), lambda i: (i, 0, 0)),
        ],
        out_shape=[
            jax.ShapeDtypeStruct((rows, width), jnp.bfloat16),
            jax.ShapeDtypeStruct((count, 8, rows), jnp.float32),
        ],
        compiler_params=pltpu.CompilerParams(vmem_limit_bytes=VMEM_LIMIT),
        cost_estimate=pl.CostEstimate(
            flops=8 * rows * kept * width, bytes_accessed=4 * kept * width, transcendentals=12 * rows * kept
        ),
        name="cross_forward",
    )(query, pair, pair)


def cross_backward(query, pair, dout, lse):
    rows, width = query.shape
    count = width // 128
    kept = pair.shape[0]
    return pl.pallas_call(
        cross_backward_kernel,
        grid=(count,),
        in_specs=[
            pl.BlockSpec((rows, 128), lambda i: (0, i)),
            pl.BlockSpec((kept, 128), lambda i: (0, i)),
            pl.BlockSpec((kept, 128), lambda i: (0, count + i)),
            pl.BlockSpec((rows, 128), lambda i: (0, i)),
            pl.BlockSpec((1, 8, rows), lambda i: (i, 0, 0)),
        ],
        out_specs=[
            pl.BlockSpec((rows, 128), lambda i: (0, i)),
            pl.BlockSpec((kept, 128), lambda i: (0, i)),
            pl.BlockSpec((kept, 128), lambda i: (0, i)),
        ],
        out_shape=[
            jax.ShapeDtypeStruct((rows, width), jnp.bfloat16),
            jax.ShapeDtypeStruct((kept, width), jnp.bfloat16),
            jax.ShapeDtypeStruct((kept, width), jnp.bfloat16),
        ],
        compiler_params=pltpu.CompilerParams(vmem_limit_bytes=VMEM_LIMIT),
        cost_estimate=pl.CostEstimate(
            flops=20 * rows * kept * width, bytes_accessed=8 * kept * width, transcendentals=12 * rows * kept
        ),
        name="cross_backward",
    )(query, pair, pair, dout, lse)


def pick_kernel(table, bank, out):
    i = pl.program_id(0)
    keep = table[pl.num_programs(0) + i]
    out[0] = jnp.where(keep > 0, bank[0], jnp.zeros_like(bank[0]))


def pick_rows(chunks, spots, found):
    count = spots.shape[0]
    size = chunks.shape[1:]
    table = jnp.concatenate([spots, found.astype(jnp.int32)])
    return pl.pallas_call(
        pick_kernel,
        grid_spec=pltpu.PrefetchScalarGridSpec(
            num_scalar_prefetch=1,
            grid=(count,),
            in_specs=[pl.BlockSpec((1,) + size, lambda i, t: (t[i], 0, 0))],
            out_specs=pl.BlockSpec((1,) + size, lambda i, t: (i, 0, 0)),
        ),
        out_shape=jax.ShapeDtypeStruct((count,) + size, chunks.dtype),
        name="pick_rows",
    )(table, chunks)


def place_kernel(count, table, grads, out):
    spot = pl.program_id(0)
    out[...] = jnp.zeros_like(out)
    for i in range(count):

        @pl.when(table[i] == spot)
        def _(i=i):
            out[0] += wide(grads[i])


def place_rows(grads, spots, chunks):
    count = spots.shape[0]
    size = grads.shape[1:]
    return pl.pallas_call(
        functools.partial(place_kernel, count),
        grid_spec=pltpu.PrefetchScalarGridSpec(
            num_scalar_prefetch=1,
            grid=(chunks,),
            in_specs=[whole((count,) + size)],
            out_specs=pl.BlockSpec((1,) + size, lambda n, t: (n, 0, 0)),
        ),
        out_shape=jax.ShapeDtypeStruct((chunks,) + size, jnp.float32),
        name="place_rows",
    )(spots, grads)


class Chain:
    def __init__(self, stages):
        self.stages = stages
        self.result = None
        self.pending = next(stages)

    def step(self, pending):
        try:
            self.pending = self.stages.send(pending)
        except StopIteration as stop:
            self.pending, self.result = (), stop.value


def meet(values, *chains):
    values, pending = lax.optimization_barrier((values, [chain.pending for chain in chains]))
    for chain, arrays in zip(chains, pending):
        chain.step(arrays)
    return values


def hold(values, *chains):
    values, pending = lax.optimization_barrier((values, [chain.pending for chain in chains]))
    for chain, arrays in zip(chains, pending):
        chain.pending = arrays
    return values


def settle(values, *chains):
    values, kept = lax.optimization_barrier((values, [chain.pending[0] for chain in chains]))
    for chain, array in zip(chains, kept):
        chain.pending = [array] + list(chain.pending[1:])
    return values


def total_of(arrays):
    total = wide(arrays[0])
    for array in arrays[1:]:
        total = total + wide(array)
    return total


def body(
    grid,
    tokens,
    cotangent,
    bank,
    prefix,
    blocks,
    self_qkv,
    self_out,
    cross_q,
    cross_kv,
    cross_out,
    ffn_in,
    ffn_out,
    gains,
    biases,
):
    Z, X, C, Y = grid.z, grid.x, grid.c, grid.y
    devices = grid.seq * Y
    seq_index = lax.axis_index("seq")
    me = {
        "y": lax.axis_index("batch"),
        "c": seq_index % C,
        "x": (seq_index // C) % X,
        "z": seq_index // (C * X),
        "h": seq_index // (2 * C * X),
        "l": seq_index // (C * X) % 2,
    }
    my_z, my_x, my_c = me["z"], me["x"], me["c"]
    rows, width = tokens.shape[1:]
    hidden = ffn_in.shape[1]
    part = width // devices
    fan = hidden // width
    inputs = tokens[0]

    def parted(array, axis, place):
        size = getattr(grid, axis)
        kept = [take(array, me[axis], place)]
        for shift in range(1, size):
            kept.append(grid.send(take(array, me[axis] ^ shift, place), axis, shift))
        return kept

    def reduction(array, axes, lead=0, final=True):
        names = ["h", "l", "x", "c", "y"]
        for axis in axes:
            place = lead + names.index(axis)
            names.remove(axis)
            arrays = yield parted(array, axis, place)
            total = total_of(arrays)
            array = rounded(total)
        return total if final else array

    def sharded(array):
        return array.reshape(2, 2, X, C, Y, array.shape[0] // devices, array.shape[1])

    grouped = self_qkv.reshape(part, 3, GROUPS, GROUP_WIDTH)
    extra = jnp.stack([biases[3], biases[4]], axis=1)
    extra = jnp.broadcast_to(
        jnp.pad(extra, ((0, 0), (0, QUERY - GROUP_WIDTH - 2)))[:, None],
        (part, GROUPS, QUERY - GROUP_WIDTH),
    )
    packed = jnp.concatenate(
        [
            grouped[:, 0],
            extra,
            grouped[:, 1, :, :128],
            grouped[:, 2, :, :128],
            grouped[:, 1, :, 128:],
            grouped[:, 2, :, 128:],
        ],
        axis=2,
    ).transpose(1, 0, 2)
    pieces = parted(packed, "z", 0)

    small = jnp.concatenate([gains, biases], axis=0).T
    small = jnp.pad(small, ((0, 0), (0, 128 - small.shape[1])))
    first_pack = jnp.concatenate([self_out, cross_q, cross_out, cross_kv, small], axis=1)
    inner_columns = (
        ffn_in.reshape(part, devices, fan, part).transpose(0, 2, 1, 3).reshape(part, hidden)
    )
    outer_blocks = ffn_out.reshape(fan, part, width).transpose(1, 0, 2).reshape(part, hidden)
    second_pack = jnp.stack([inner_columns, outer_blocks])
    first_all = lax.all_gather(first_pack, ("seq", "batch"), axis=0, tiled=True)
    second_all = lax.all_gather(second_pack, ("seq", "batch"), axis=1, tiled=True)

    pieces, inputs = lax.optimization_barrier((pieces, inputs))
    across = grid.send(inputs, "h", 1)
    token_parts = [inputs, grid.send(inputs, "l", 1), across, grid.send(across, "l", 1)]

    chunk = BANK_BLOCK * blocks.shape[1] // grid.seq
    per_block = BANK_BLOCK // chunk
    local_chunks = bank.shape[1] // chunk
    local_blocks = bank.shape[1] // BANK_BLOCK
    bank_chunks = bank[0].reshape(local_chunks, chunk, width)
    home = seq_index * local_blocks
    every = jnp.arange(grid.seq, dtype=jnp.int32)
    wanted = jnp.take(blocks[0], every // per_block) - home
    found = (wanted >= 0) & (wanted < local_blocks)
    spots = jnp.where(found, wanted * per_block + every % per_block, 0)
    picked = pick_rows(bank_chunks, spots, found).reshape(2, 2, X, C, 1, chunk, width)

    def spreading(own):
        array = own
        for axis in "hlxc":
            size = getattr(grid, axis)
            array = jnp.stack((yield [array] + [grid.send(array, axis, m) for m in range(1, size)]))
        return array

    def retrieval():
        own = (yield from reduction(picked, "cxlh", final=False))[0]
        every_row = yield from spreading(own)
        return own, every_row.reshape(grid.seq * chunk, width)

    retrieve = Chain(retrieval())
    gathered = in_order(pieces, my_z)
    for axis in "yxc":
        pieces = [gathered] + [grid.send(gathered, axis, m) for m in range(1, getattr(grid, axis))]
        if axis == "y":
            pieces = meet(pieces, retrieve)
        gathered = in_order(pieces, me[axis])
    qkv_group = gathered.transpose(3, 1, 0, 2, 4, 5).reshape(width, PACK)
    column = jnp.arange(PACK, dtype=jnp.int32)
    real = (column < GROUP_WIDTH) | (column >= QUERY)
    is_query = column < GROUP_WIDTH
    is_pair_value = (column >= QUERY + 128) & (column < QUERY + 256)
    is_value = is_pair_value | (column >= QUERY + 320)
    local = jnp.where(is_query, column, column - jnp.where(is_pair_value, QUERY + 128, QUERY + 192))
    line = jnp.where(is_query | is_value, local + my_z * GROUP_WIDTH, -1)
    chosen = (jnp.arange(width, dtype=jnp.int32)[:, None] == line[None]).astype(jnp.bfloat16)
    picked_bias = weight_grad(qkv_group[:, GROUP_WIDTH:QUERY], chosen)
    qkv_bias = jnp.where(is_query, picked_bias[0], picked_bias[1])
    qkv_weight = jnp.where(real[None], qkv_group, jnp.zeros_like(qkv_group))

    qkv_weight, qkv_bias, token_parts = meet((qkv_weight, qkv_bias, token_parts), retrieve)

    token_column = jnp.concatenate(token_parts, axis=0)
    own_queries = rounded(matmul(token_column, qkv_weight[:, :QUERY]) + qkv_bias[:QUERY])
    own_side = rounded(matmul(token_column, qkv_weight[:, QUERY:]) + qkv_bias[QUERY:])
    own_queries = own_queries.reshape(GROUPS, rows, QUERY)

    far_queries = grid.send(own_queries[1::2], "z", 0, mirror=True)
    near_other = grid.send(own_side, "c", 1)
    far_queries, side = lax.optimization_barrier((far_queries, own_side))
    far_own = [grid.send(side, "x", m) for m in range(1, X)]
    queries = jnp.stack(
        [own_queries[m] if m % 2 == 0 else far_queries[m // 2] for m in range(GROUPS)]
    )

    turn = jnp.arange(GROUPS, dtype=jnp.int32)
    turn_z = my_z ^ turn

    def key_firsts(x, c):
        return ((turn_z * X + x) * C + c) * rows

    query_firsts = jnp.where(
        turn % 2 == 0, key_firsts(my_x, my_c), key_firsts(X - 1 - my_x, C - 1 - my_c)
    )

    def table_of(shifts, c):
        keys = [key_firsts(my_x ^ m, c) for m in shifts]
        return jnp.concatenate(keys + [query_firsts, prefix]).astype(jnp.int32)

    far = list(range(1, X))
    tables = {
        "near own": table_of([0], my_c),
        "near other": table_of([0], C - 1 - my_c),
        "far own": table_of(far, my_c),
        "far other": table_of(far, C - 1 - my_c),
    }

    carry = self_forward(tables["near own"], queries, [own_side], None, False)
    carry, near_other = meet((carry, near_other), retrieve)
    carry = self_forward(tables["near other"], queries, [near_other], carry, False)
    carry, far_own = meet((carry, far_own), retrieve)
    far_other = [grid.send(side, "c", 1) for side in far_own]
    carry = self_forward(tables["far own"], queries, far_own, carry, False)
    carry, far_other = meet((carry, far_other), retrieve)
    attention, lse = self_forward(tables["far other"], queries, far_other, carry, True)
    attention, lse = meet((attention, lse), retrieve)
    attention_mine = rounded(attention)

    def swapped(array, m):
        return grid.send(array, "z", m, mirror=m % 2 == 1)

    pieces = [attention_mine[0]] + [swapped(attention_mine[m], m) for m in range(1, Z)]
    pieces = meet(pieces, retrieve)
    retrieve.step(retrieve.pending)
    own_rows, all_rows = retrieve.result
    attention_low = (
        in_order(pieces, my_z)[:, :, :GROUP_WIDTH].transpose(1, 0, 2).reshape(rows, width)
    )

    selfout_full = first_all[:, :width]
    crossq_full = first_all[:, width : 2 * width]
    crossout_full = first_all[:, 2 * width : 3 * width]
    crosskv_full = first_all[:, 3 * width : 5 * width]
    small_full = wide(first_all[:, 5 * width :].T)
    gain = small_full[:3]
    bias = small_full[3:17]
    ffnin_full = second_all[0]
    outer = [second_all[1, :, f * width : (f + 1) * width] for f in range(fan)]
    inner_bias = bias[10:14].reshape(devices, fan, part).transpose(1, 0, 2).reshape(-1)

    resid_one = wide(inputs) + matmul(attention_low, selfout_full) + bias[5]
    hidden_one = layer_norm(resid_one, gain[0], bias[0])
    hidden_one_low = rounded(hidden_one)
    cross_query = rounded(matmul(hidden_one_low, crossq_full) + bias[6])
    cross_pair = rounded(
        matmul(all_rows, crosskv_full) + jnp.concatenate([jnp.zeros((width,), jnp.float32), bias[7]])
    )
    cross_att, cross_lse = cross_forward(cross_query, cross_pair)
    resid_two = hidden_one + matmul(cross_att, crossout_full) + bias[8]
    hidden_two = layer_norm(resid_two, gain[1], bias[1])
    hidden_two_low = rounded(hidden_two)
    inner = matmul(hidden_two_low, ffnin_full) + inner_bias
    activated = rounded(gelu_exact(inner))

    def fan_part(array, f):
        return array[:, f * width : (f + 1) * width]

    resid_three = hidden_two + bias[9]
    for f in range(fan):
        resid_three = resid_three + matmul(fan_part(activated, f), outer[f])
    output = layer_norm(resid_three, gain[2], bias[2])

    _unused, norm_three = jax.vjp(layer_norm, resid_three, gain[2], bias[2])
    dresid_three, dgain_three, dshift_three = norm_three(wide(cotangent[0]))
    douter_low = rounded(dresid_three)
    grad_ffnout = rounded(weight_grad(activated, douter_low))
    reduce_ffnout = Chain(
        reduction(grad_ffnout.reshape(fan, 2, 2, X, C, Y, part, width), "cyxlh", lead=1)
    )
    _unused, gelu_back = jax.vjp(gelu_exact, inner)
    dactivated = jnp.concatenate([back_matmul(douter_low, block) for block in outer], axis=1)
    dinner_low = rounded(gelu_back(dactivated)[0])
    grad_ffnin = rounded(weight_grad(hidden_two_low, dinner_low))
    reduce_ffnin = Chain(reduction(sharded(grad_ffnin), "cyxlh"))

    _unused, norm_two = jax.vjp(layer_norm, resid_two, gain[1], bias[1])
    dresid_two, dgain_two, dshift_two = norm_two(dresid_three + back_matmul(dinner_low, ffnin_full))
    dcross_low = rounded(dresid_two)
    dcross_att = rounded(back_matmul(dcross_low, crossout_full))
    dcross_query, dcross_key, dcross_value = cross_backward(
        cross_query, cross_pair, dcross_att, cross_lse
    )
    dcross_query, dcross_key, dcross_value = meet(
        (dcross_query, dcross_key, dcross_value), reduce_ffnout, reduce_ffnin
    )

    dcross_all = jnp.concatenate([dcross_key, dcross_value], axis=1)
    dcross_all = dcross_all.reshape(C, X, 2, 2, chunk, 2 * width)

    def unspreading(array):
        for axis in "cxlh":
            size = getattr(grid, axis)
            arrays = yield [array[0]] + [grid.send(array[m], axis, m) for m in range(1, size)]
            array = rounded(total_of(arrays))
        return array

    unspread = Chain(unspreading(dcross_all))

    _unused, norm_one = jax.vjp(layer_norm, resid_one, gain[0], bias[0])
    dresid_one, dgain_one, dshift_one = norm_one(dresid_two + back_matmul(dcross_query, crossq_full))
    dbranch_low = rounded(dresid_one)
    datt_low = rounded(back_matmul(dbranch_low, selfout_full))
    datt_groups = jnp.pad(
        datt_low.reshape(rows, GROUPS, GROUP_WIDTH).transpose(1, 0, 2),
        ((0, 0), (0, 0), (0, 256 - GROUP_WIDTH)),
    )
    pieces = [take(datt_groups, my_z, 0)]
    for m in range(1, Z):
        pieces.append(swapped(take(datt_groups, my_z ^ m, 0), m))
    grad_mid = jnp.stack(
        [
            rounded(weight_grad(attention_low, dbranch_low)),
            rounded(weight_grad(hidden_one_low, dcross_query)),
            rounded(weight_grad(cross_att, dcross_low)),
        ]
    )
    grad_mid, pieces = meet((grad_mid, pieces), unspread)
    reduce_mid = Chain(reduction(grad_mid.reshape(3, 2, 2, X, C, Y, part, width), "cyxlh", lead=1))
    dout = jnp.stack(pieces)

    *far_other_grad, slopes, state = self_backward(
        tables["far other"], queries, dout, lse, far_other, attention, True, False
    )
    far_other_grad, slopes = meet(
        (far_other_grad, slopes), reduce_ffnout, reduce_mid, unspread
    )
    far_moved = [grid.send(grad, "c", 1) for grad in far_other_grad]
    *far_own_grad, slopes = self_backward(
        tables["far own"], queries, dout, state, far_own, slopes, False, False
    )
    far_own_grad, far_moved, slopes = meet(
        (far_own_grad, far_moved, slopes), unspread, reduce_ffnout, reduce_ffnin
    )
    far_grad = [rounded(total_of(pair)) for pair in zip(far_own_grad, far_moved)]
    far_moved = [grid.send(grad, "x", m) for m, grad in zip(far, far_grad)]
    near_other_grad, slopes = self_backward(
        tables["near other"], queries, dout, state, [near_other], slopes, False, False
    )
    near_other_grad, far_moved, slopes = meet(
        (near_other_grad, far_moved, slopes), unspread, reduce_ffnout, reduce_ffnin, reduce_mid
    )
    near_moved = grid.send(near_other_grad, "c", 1)

    dcross_pair = unspread.result
    bias_rows = jnp.stack(
        [
            dgain_one,
            dgain_two,
            dgain_three,
            dshift_one,
            dshift_two,
            dshift_three,
            column_sums(dbranch_low),
            column_sums(dcross_query),
            column_sums(dcross_pair[:, width:]),
            column_sums(dcross_low),
            column_sums(douter_low),
        ]
    )
    inner_sums = column_sums(dinner_low).reshape(fan, devices, part).transpose(1, 0, 2)
    bias_rows = jnp.concatenate([bias_rows, inner_sums.reshape(fan, width)], axis=0)
    bias_columns = jnp.pad(rounded(bias_rows.T), ((0, 0), (0, 128 - bias_rows.shape[0])))
    grad_late = jnp.concatenate([rounded(weight_grad(own_rows, dcross_pair)), bias_columns], axis=1)
    reduce_late = Chain(reduction(sharded(grad_late), "cyxlh"))
    spread_back = Chain(spreading(rounded(back_matmul(dcross_pair, crosskv_full))))

    slopes = settle(slopes, reduce_late, spread_back)
    near_own_grad, query_grad = self_backward(
        tables["near own"], queries, dout, state, [own_side], slopes, False, True
    )
    near_own_grad, near_moved, query_grad = hold(
        (near_own_grad, near_moved, query_grad), reduce_late, spread_back
    )

    far_query_grad = grid.send(query_grad[1::2], "z", 0, mirror=True)
    side_grad = rounded(total_of([near_own_grad, near_moved] + far_moved))
    query_grad = jnp.stack(
        [query_grad[m] if m % 2 == 0 else far_query_grad[m // 2] for m in range(GROUPS)]
    )
    dqkv = jnp.concatenate([query_grad.reshape(GROUPS * rows, QUERY), side_grad], axis=1)
    far_tokens_grad = rounded(back_matmul(dqkv[rows:], qkv_weight)).reshape(Z - 1, rows, width)
    dqkv, far_tokens_grad = meet(
        (dqkv, far_tokens_grad), reduce_ffnout, reduce_ffnin, reduce_mid, reduce_late, spread_back
    )
    third = grid.send(far_tokens_grad[2], "l", 1)
    first = grid.send(far_tokens_grad[0], "l", 1)
    grad_group = weight_grad(token_column, dqkv)
    sums = jnp.sum(wide(dqkv), axis=0)
    sums = jnp.stack([jnp.where(is_query, sums, 0.0), jnp.where(is_value, sums, 0.0)])
    sums = jnp.pad(rounded(sums), ((0, QUERY - GROUP_WIDTH - 2), (0, 0)))
    grad_group = jnp.concatenate(
        [grad_group[:, :GROUP_WIDTH], back_matmul(chosen, sums), grad_group[:, QUERY:]], axis=1
    )
    reduce_group = Chain(reduction(sharded(rounded(grad_group)), "cyx", final=False))
    tokens_base = dresid_one + back_matmul(dqkv[:rows], qkv_weight)
    second = grid.send(rounded(total_of([far_tokens_grad[1], third])), "h", 1)
    tokens_base = meet(tokens_base, reduce_group, spread_back, reduce_late)
    tokens_base = meet(tokens_base, reduce_group, spread_back, reduce_mid)
    tokens_base = meet(tokens_base, reduce_group, spread_back, reduce_late)
    pieces = parted(reduce_group.result.reshape(Z, part, PACK), "z", 0)
    tokens_grad = total_of([tokens_base, first, second])
    for chain in (reduce_ffnin, reduce_mid, reduce_late, reduce_late):
        chain.step(chain.pending)

    spot = jnp.arange(grid.seq, dtype=jnp.int32)
    spot_z = my_z ^ (spot % 2 * 2 + spot // 2 % 2)
    source = (spot_z * X + (my_x ^ (spot // Z % X))) * C + (my_c ^ (spot // (Z * X)))
    target = jnp.take(blocks[0], source // per_block) - home
    inside = (target >= 0) & (target < local_blocks)
    places = jnp.where(inside, target * per_block + source % per_block, -1)
    drows = spread_back.result.reshape(grid.seq, chunk, width)
    bank_grad = place_rows(drows, places, local_chunks).reshape(bank.shape[1], width)

    grad_groups = wide(in_order(pieces, my_z))
    sides = grad_groups[:, :, QUERY:]
    out_qkv = jnp.stack(
        [
            grad_groups[:, :, :GROUP_WIDTH],
            jnp.concatenate([sides[:, :, :128], sides[:, :, 256:320]], axis=2),
            jnp.concatenate([sides[:, :, 128:256], sides[:, :, 320:384]], axis=2),
        ]
    )
    out_qkv = out_qkv.transpose(2, 0, 1, 3).reshape(part, 3 * width)
    late_bias = jnp.sum(grad_groups[:, :, GROUP_WIDTH : GROUP_WIDTH + 2], axis=0)

    out_late, out_mid = reduce_late.result, reduce_mid.result
    out_ffnin = (
        reduce_ffnin.result.reshape(part, fan, devices, part)
        .transpose(0, 2, 1, 3)
        .reshape(part, hidden)
    )
    out_small = out_late[:, 2 * width :].T
    bias_grad = jnp.concatenate([out_small[3:6], late_bias.T, out_small[6:15]], axis=0)
    return (
        rounded(output)[None],
        tokens_grad[None],
        bank_grad[None],
        out_qkv,
        out_mid[0],
        out_mid[1],
        out_late[:, : 2 * width],
        out_mid[2],
        out_ffnin,
        reduce_ffnout.result.reshape(fan * part, width),
        out_small[:3],
        bias_grad,
    )


def solution(mesh):
    split = P("batch", "seq", None)
    shard = P(("seq", "batch"), None)
    flat = P(None, ("seq", "batch"))
    return jax.shard_map(
        functools.partial(body, Grid(mesh)),
        mesh=mesh,
        in_specs=(split, split, split, P("batch"), P("batch", None)) + (shard,) * 7 + (flat, flat),
        out_specs=(split, split, split) + (shard,) * 7 + (flat, flat),
        check_vma=False,
    )
```
